32 devices in a mesh: gx: 8 (over z, y), gy: 4 (over x, core).
Axes of the slice: x: 2, y: 2, z: 4, core: 2. Of those that a mesh axis runs over, the one named last changes fastest.
Arguments:
- right_side: float32 [7, 7, 7, 16, 16, 128], P(None, None, None, 'gx', 'gy'), may hold values from -6 to 6
- coefficient: float32 [16, 16, 128], P('gx', 'gy'), may hold values from 0.2 to 5
- degrees: int32 [3, 16, 16, 128], P(None, 'gx', 'gy'), may hold values from 2 to 6
Outputs:
- smoothed: float32 [7, 7, 7, 16, 16, 128], P(None, None, None, 'gx', 'gy')
- coarse_residual: float32 [64, 16, 2048], P(None, 'gx', 'gy')
The draws below stay inside these ranges and needn't reach their ends.
All inputs are finite; a program needn't handle non-finite values.
Results may differ from the reference program's by a relative error of at most 0.0003.
Values sent between devices are 32-bit elements; how exact they have to be, the bound alone decides.
A program may use at most 64 MiB of HBM per device.

```python
import math
import jax
import jax.numpy as jnp
from jax import lax

MODES = 7
CMODES = 4
SMOOTH = 3
NX = 16
NY = 16
NZ = 128


def place_ends(values, stream_key, least, top_value):
    longest = values.shape.index(max(values.shape))
    spots = []
    for shift in (0, 1):
        where = [jax.random.randint(jax.random.fold_in(stream_key, axis), (), 0, length) for axis, length in enumerate(values.shape)]
        where[longest] = (where[longest] + shift) % values.shape[longest]
        spots.append(tuple(where))
    return values.at[spots[0]].set(least).at[spots[1]].set(top_value)


def block_levels(rng, extent, split, least, top_value):
    loudness = 1.0
    for dim, parts in split:
        draws = jax.random.uniform(jax.random.fold_in(jax.random.fold_in(rng, 6), dim), (parts,), jnp.float32, least / len(split), top_value / len(split))
        loudness = loudness * jnp.repeat(jnp.exp(draws), extent[dim] // parts).reshape((-1,) + (1,) * (len(extent) - 1 - dim))
    return loudness


def noise(stream_key, dims, deviation, reach, split=(), kind=jnp.bfloat16):
    loudness = block_levels(stream_key, dims, split, -0.22, 0.18) if split else 1.0
    entries = jax.random.normal(stream_key, dims, jnp.float32) * deviation * loudness
    return jnp.minimum(jnp.maximum(entries, -reach), reach).astype(kind)


def setup_inputs(seed: int = 0) -> dict:
    seeds = jax.random.split(jax.random.key(seed), 4)
    return {
        "right_side": noise(seeds[0], (MODES, MODES, MODES, NX, NY, NZ), 1.0, 6.0, ((3, 8), (4, 4)), jnp.float32),
        "coefficient": jnp.clip(jnp.exp(math.log(5.0) - 3.218876 * jax.random.uniform(seeds[1], (NX, NY, NZ), jnp.float32) ** block_levels(seeds[1], (NX, NY, NZ), ((0, 8), (1, 4)), -0.2, 0.2)), 0.2, 5.0),
        "degrees": place_ends(jax.random.randint(seeds[2], (3, NX, NY, NZ), 2, 7), jax.random.fold_in(seeds[2], 1), 2, 6).astype(jnp.int32),
    }


lam_high = 6.0
lam_low = 0.5
exact_precision = lax.Precision.HIGHEST
TRACE_FORMS = ("ka,abgxyz->kbgxyz", "kb,abgxyz->kagxyz", "kg,abgxyz->kabxyz")
SPREAD_FORMS = ("ka,kbgxyz->abgxyz", "kb,kagxyz->abgxyz", "kg,kabxyz->abgxyz")
VOLUME_FORMS = ("ai,ibgxyz->abgxyz", "bi,aigxyz->abgxyz", "gi,abixyz->abgxyz")


def tables(mode_count):
    mode_index = jnp.arange(mode_count).astype(jnp.float32)
    parity = 1.0 - 2.0 * jnp.mod(mode_index, 2.0)
    slopes = mode_index * (mode_index + 1.0) / 2.0
    vectors = jnp.stack([jnp.ones_like(mode_index), slopes, parity, -parity * slopes])
    signs = jnp.array([1.0, -1.0, -1.0, -1.0], dtype=jnp.float32)
    signed = vectors * signs[:, None]
    masses = 2.0 / (2.0 * mode_index + 1.0)
    lesser = jnp.minimum(mode_index[:, None], mode_index[None, :])
    parity_even = jnp.mod(mode_index[:, None] + mode_index[None, :], 2.0) == 0.0
    stiffness = jnp.where(parity_even, lesser * (lesser + 1.0), 0.0).astype(jnp.float32)
    return vectors, signed, masses, stiffness, mode_index


def along(vector, direction):
    layout = [1, 1, 1, 1, 1, 1]
    layout[direction] = vector.shape[0]
    return vector.reshape(layout)


def edge_pad(rank, direction):
    widths = [(0, 0)] * rank
    widths[direction] = (1, 1)
    return widths


def degree_mask(degrees, mode_count):
    levels = jnp.arange(mode_count, dtype=jnp.int32)
    inside = (along(levels, 0) <= degrees[0]) & (along(levels, 1) <= degrees[1]) & (along(levels, 2) <= degrees[2])
    return jnp.where(inside, 1.0, 0.0).astype(jnp.float32)


def face_weight(offset, cell_count, length_total, direction):
    position = offset + jnp.arange(cell_count + 1, dtype=jnp.int32)
    inside = (position >= 1) & (position <= length_total - 1)
    weight = jnp.where(inside, 0.5, 1.0).astype(jnp.float32)
    layout = [1, 1, 1]
    layout[direction] = cell_count + 1
    return weight.reshape(layout)


def face_geometry(coef_pad, degree_pad, direction):
    length = coef_pad.shape[direction]
    left_coef = lax.slice_in_dim(coef_pad, 0, length - 1, axis=direction)
    right_coef = lax.slice_in_dim(coef_pad, 1, length, axis=direction)
    larger = jnp.maximum(lax.slice_in_dim(degree_pad, 0, length - 1, axis=direction),
                         lax.slice_in_dim(degree_pad, 1, length, axis=direction))
    penalty = jnp.maximum(left_coef, right_coef) * (larger + 1.0) * (larger + 2.0)
    return left_coef, right_coef, penalty


def scale_traces(traces, coef_pad):
    return jnp.stack([traces[0], traces[1] * coef_pad, traces[2], traces[3] * coef_pad])


def face_terms(traces, geometry, weight, direction, signed, tangent_mass):
    left_coef, right_coef, penalty = geometry
    spatial = 3 + direction
    length = traces.shape[3 + direction]

    def left_part(values):
        return lax.slice_in_dim(values, 0, length - 1, axis=spatial - 1)

    def right_part(values):
        return lax.slice_in_dim(values, 1, length, axis=spatial - 1)

    def upper_face(values):
        return lax.slice_in_dim(values, 1, length - 1, axis=spatial - 1)

    def lower_face(values):
        return lax.slice_in_dim(values, 0, length - 2, axis=spatial - 1)

    jump_term = left_part(traces[0]) - right_part(traces[2])
    flux_term = weight * (left_part(traces[1]) + right_part(traces[3]))
    across = penalty * jump_term - flux_term
    left_sym = weight * left_coef * jump_term
    right_sym = weight * right_coef * jump_term
    stacked = jnp.stack([upper_face(across), upper_face(left_sym), lower_face(across), lower_face(right_sym)]) * tangent_mass
    return jnp.einsum(SPREAD_FORMS[direction], signed, stacked, precision=exact_precision)


def volume(values, coefficient, masses, stiffness):
    mass_a, mass_b, mass_g = along(masses, 0), along(masses, 1), along(masses, 2)
    result = jnp.einsum(VOLUME_FORMS[0], stiffness, values, precision=exact_precision) * mass_b * mass_g
    result = result + jnp.einsum(VOLUME_FORMS[1], stiffness, values, precision=exact_precision) * mass_a * mass_g
    result = result + jnp.einsum(VOLUME_FORMS[2], stiffness, values, precision=exact_precision) * mass_a * mass_b
    return coefficient * result


def jacobi_inverse(coefficient, geometry, weights, masses, stiffness, mode_index, mask):
    mass_axes = (along(masses, 0), along(masses, 1), along(masses, 2))
    stiff_diag = jnp.diagonal(stiffness)
    result = coefficient * (along(stiff_diag, 0) * mass_axes[1] * mass_axes[2]
                            + mass_axes[0] * along(stiff_diag, 1) * mass_axes[2]
                            + mass_axes[0] * mass_axes[1] * along(stiff_diag, 2))
    for direction in range(3):
        others = [mass_axes[other] for other in range(3) if other != direction]
        penalty = geometry[direction][2]
        weight = weights[direction]
        length = penalty.shape[direction]
        penalty_sum = lax.slice_in_dim(penalty, 1, length, axis=direction) + lax.slice_in_dim(penalty, 0, length - 1, axis=direction)
        weight_sum = lax.slice_in_dim(weight, 1, length, axis=direction) + lax.slice_in_dim(weight, 0, length - 1, axis=direction)
        curvature = along(mode_index * (mode_index + 1.0), direction)
        result = result + others[0] * others[1] * (penalty_sum - weight_sum * coefficient * curvature)
    return mask / result


def restrict(residual, degrees, coarse_modes):
    levels = jnp.arange(coarse_modes, dtype=jnp.int32)
    halves = degrees // 2
    keep = (along(levels, 0) <= halves[0]) & (along(levels, 1) <= halves[1]) & (along(levels, 2) <= halves[2])
    kept = jnp.where(keep, residual[:coarse_modes, :coarse_modes, :coarse_modes], 0.0)
    return kept.reshape((coarse_modes * coarse_modes * coarse_modes,) + residual.shape[3:])


def reference(right_side, coefficient, degrees):
    vectors, signed, masses, stiffness, mode_index = tables(MODES)
    tangent_mass = masses[None, :, None, None, None, None] * masses[None, None, :, None, None, None]
    mask = degree_mask(degrees, MODES)
    source = right_side * mask
    degree_float = degrees.astype(jnp.float32)
    totals = (NX, NY, NZ)
    weights = [face_weight(0, totals[direction], totals[direction], direction) for direction in range(3)]
    coef_pads = [jnp.pad(coefficient, edge_pad(3, direction)) for direction in range(3)]
    geometry = [face_geometry(coef_pads[direction], jnp.pad(degree_float[direction], edge_pad(3, direction)), direction) for direction in range(3)]
    inverse = jacobi_inverse(coefficient, geometry, weights, masses, stiffness, mode_index, mask)

    def operator(values):
        result = volume(values, coefficient, masses, stiffness)
        for direction in range(3):
            padded = jnp.pad(values, edge_pad(6, 3 + direction))
            traces = jnp.einsum(TRACE_FORMS[direction], vectors, padded, precision=exact_precision)
            traces = scale_traces(traces, coef_pads[direction])
            result = result + face_terms(traces, geometry[direction], weights[direction], direction, signed, tangent_mass)
        return mask * result

    centre = (lam_high + lam_low) / 2.0
    radius = (lam_high - lam_low) / 2.0
    interval_ratio = centre / radius
    rho_now = 1.0 / interval_ratio
    step_term = inverse * source / centre
    solution = step_term
    for sweep_index in range(SMOOTH - 1):
        rho_next = 1.0 / (2.0 * interval_ratio - rho_now)
        residual = source - operator(solution)
        step_term = rho_next * rho_now * step_term + (2.0 * rho_next / radius) * inverse * residual
        solution = solution + step_term
        rho_now = rho_next
    residual = source - operator(solution)
    coarse = restrict(residual, degrees, CMODES)
    coarse = jnp.transpose(coarse, (0, 1, 3, 2)).reshape(CMODES * CMODES * CMODES, NX, NZ * NY)
    return solution, coarse
```

```python
import functools

import jax
import jax.numpy as jnp
from jax import lax
from jax.experimental import pallas as pl
from jax.experimental.pallas import tpu as pltpu
from jax.sharding import PartitionSpec as P

CMODES = 4
LAM_HIGH = 6.0
LAM_LOW = 0.5
MODES = 7
MESH = pl.DeviceIdType.MESH
F32 = jnp.float32
HALF = [(2.0 * n + 1.0) / 2.0 for n in range(MODES)]
SLOPE = [n * (n + 1.0) / 2.0 for n in range(MODES)]


def chebyshev():
    centre = (LAM_HIGH + LAM_LOW) / 2.0
    radius = (LAM_HIGH - LAM_LOW) / 2.0
    ratio = centre / radius
    rho = 1.0 / ratio
    pairs = []
    for _ in range(2):
        following = 1.0 / (2.0 * ratio - rho)
        pairs.append((following * rho, 2.0 * following / radius))
        rho = following
    return 1.0 / centre, pairs


def rows(shape):
    return lax.broadcasted_iota(jnp.int32, shape, len(shape) - 2)


def lanes(shape):
    return lax.broadcasted_iota(jnp.int32, shape, len(shape) - 1)


def turn(v, shift):
    return pltpu.roll(v, shift, v.ndim - 2)


def pack_x_up(p, q):
    return jnp.where(rows(p.shape) < 4, turn(p, 4), q)


def pack_x_down(p, q):
    return jnp.where(rows(p.shape) < 4, p, turn(q, 4))


def prev_x(p, q, g):
    low = rows(p.shape) < 4
    return jnp.where(low, g, turn(p, 4)), turn(jnp.where(low, q, g), 4)


def next_x(p, q, g):
    low = rows(p.shape) < 4
    return turn(jnp.where(low, g, p), 4), jnp.where(low, turn(q, 4), g)


def halves(p):
    half = (p.shape[0] + 1) // 2
    if p.shape[0] == 1:
        return p, p
    high = p[half:]
    if p.shape[0] % 2:
        high = jnp.concatenate([high, p[half - 1:half]], axis=0)
    return p[:half], high


def pack_y_up(p, q):
    (p, p_high), (q, q_high) = halves(p), halves(q)
    r = rows(p.shape) & 3
    return jnp.where(r < 2, jnp.where(r == 0, turn(p, 5), turn(q, 6)), jnp.where(r == 2, turn(p_high, 7), q_high))


def pack_y_down(p, q):
    (p, p_high), (q, q_high) = halves(p), halves(q)
    r = rows(p.shape) & 3
    return jnp.where(r < 2, jnp.where(r == 1, turn(p_high, 1), q_high), jnp.where(r == 3, turn(p, 3), turn(q, 2)))


def open_y(g, count, shifts):
    def both(low, high):
        first = turn(g, low) if low else g
        if count == 1:
            return first
        return jnp.concatenate([first, turn(g, high)[:count - g.shape[0]]], axis=0)
    return both(shifts[0], shifts[1]), both(shifts[2], shifts[3])


def prev_y(p, q, g):
    edge = (rows(p.shape) & 3) == 0
    g = open_y(g, p.shape[0], (0, 6, 7, 5))
    return jnp.where(edge, g[0], turn(p, 1)), jnp.where(edge, g[1], turn(q, 1))


def next_y(p, q, g):
    edge = (rows(p.shape) & 3) == 3
    g = open_y(g, p.shape[0], (0, 2, 1, 3))
    return jnp.where(edge, g[0], turn(p, 7)), jnp.where(edge, g[1], turn(q, 7))


def prev_z(p):
    return jnp.where(lanes(p.shape) == 0, 0.0, pltpu.roll(p, 1, p.ndim - 1))


def next_z(p):
    end = p.shape[-1] - 1
    return jnp.where(lanes(p.shape) == end, 0.0, pltpu.roll(p, end, p.ndim - 1))


def line(u, half_coef):
    t4 = u[4] + u[6]
    t2 = u[2] + t4
    even = u[0] + t2
    t3 = u[3] + u[5]
    odd = u[1] + t3
    s2 = 6.0 * t2
    s4 = s2 + 14.0 * t4
    s6 = s4 + 22.0 * u[6]
    s1 = 2.0 * odd
    s3 = s1 + 10.0 * t3
    s5 = s3 + 18.0 * u[5]
    tp = even + odd
    tm = even - odd
    fp = half_coef * (s6 + s5)
    fm = half_coef * (s5 - s6)
    return (tp, tm, fp, fm), (None, s1, s2, s3, s4, s5, s6)


def spread(traces, before, after, geom, coef, sums, count):
    tp, tm, fp, fm = traces
    tau_a, tau_b, w_a, w_b, k_a, k_b = geom
    jump_a = tp - after[0]
    g_a = tau_a * jump_a - w_a * (fp + after[1])
    jump_b = before[0] - tm
    g_b = tau_b * jump_b - w_b * (before[1] + fm)
    kl = k_a * jump_a
    kr = k_b * jump_b
    p = (g_a - g_b, g_a + g_b)
    q = (kl - kr, kl + kr)
    out = [HALF[0] * p[0]]
    for n in range(1, count):
        out.append(HALF[n] * (coef * sums[n] + (p[n % 2] - SLOPE[n] * q[n % 2])))
    return out


def kernel(nx, ny, rhs_hbm, coef_hbm, deg_hbm, u, left, s, coef, deg, inv, step, acc, geo, dia, ym,
           ps, pg, xs, xg, ys, yg, xs3, xg3, ys3, yg3, kept, folds, folded,
           in_sem, p_send, p_recv, x_send, x_recv, y_send, y_recv, f_send, f_recv):
    loads = [pltpu.make_async_copy(a, b, in_sem.at[i])
             for i, (a, b) in enumerate(((coef_hbm, coef), (deg_hbm, deg), (rhs_hbm, s)))]
    for load in loads:
        load.start()
    gx, gy = lax.axis_index("gx"), lax.axis_index("gy")
    exists = (gx < nx - 1, gx > 0, gy < ny - 1, gy > 0)
    target = ({"gx": gx + 1}, {"gx": gx - 1}, {"gy": gy + 1}, {"gy": gy - 1})
    source = (exists[1], exists[0], exists[3], exists[2])

    barrier = pltpu.get_barrier_semaphore()
    for d in range(2):
        @pl.when(exists[d])
        def _(d=d):
            pl.semaphore_signal(barrier, inc=1, device_id=target[d], device_id_type=MESH)
    for d in range(ny):
        @pl.when(gy != d)
        def _(d=d):
            pl.semaphore_signal(barrier, inc=1, device_id={"gy": d}, device_id_type=MESH)

    def copy(src, dst, send, recv, d):
        return pltpu.make_async_remote_copy(src_ref=src, dst_ref=dst, send_sem=send, recv_sem=recv,
                                            device_id=target[d], device_id_type=MESH)

    def param_copy(d):
        return copy(ps.at[d], pg.at[d], p_send.at[d], p_recv.at[d], d)

    def x_copy(k, d, b):
        if k < 2:
            return copy(xs.at[k, d, b], xg.at[k, d, b], x_send.at[k, d, b], x_recv.at[k, d, b], d)
        return copy(xs3.at[d, b], xg3.at[d, b], x_send.at[k, d, b], x_recv.at[k, d, b], d)

    def y_copy(k, d, a):
        if k < 2:
            return copy(ys.at[k, d, a], yg.at[k, d, a], y_send.at[k, d, a], y_recv.at[k, d, a], 2 + d)
        return copy(ys3.at[d, a], yg3.at[d, a], y_send.at[k, d, a], y_recv.at[k, d, a], 2 + d)

    loads[0].wait()
    loads[1].wait()
    c = coef[...]
    half_coef = 0.5 * c
    depth = 128 // ny
    df = [deg[d].astype(F32) for d in range(3)]
    ps[0] = pack_x_up(c, df[0])
    ps[1] = pack_x_down(c, df[0])
    ps[2] = pack_y_up(c[None], df[1][None])[0]
    ps[3] = pack_y_down(c[None], df[1][None])[0]
    pl.semaphore_wait(barrier, sum(e.astype(jnp.int32) for e in exists[:2]) + (ny - 1))
    for d in range(4):
        @pl.when(exists[d])
        def _(d=d):
            param_copy(d).start()

    for d in range(4):
        @pl.when(jnp.logical_not(source[d]))
        def _(d=d):
            pg[d] = jnp.zeros((8, 128), F32)
            ghosts = (xg, yg)[d // 2]
            ghosts3 = (xg3, yg3)[d // 2]

            def clear(i, _):
                for k in range(2):
                    ghosts[k, d % 2, i] = jnp.zeros(ghosts.shape[3:], F32)
                return 0
            lax.fori_loop(0, MODES, clear, 0)

            def clear3(i, _):
                ghosts3[d % 2, i] = jnp.zeros(ghosts3.shape[2:], F32)
                return 0
            lax.fori_loop(0, CMODES, clear3, 0)

    shape = (MODES, 8, 128)
    levels = lax.broadcasted_iota(jnp.int32, shape, 0)
    ym[...] = jnp.where(levels <= deg[1][None], 1.0, 0.0)

    def prepare(direction, before, after, first, last):
        degree = df[direction]
        wide_a = jnp.maximum(degree, after[1])
        wide_b = jnp.maximum(degree, before[1])
        tau_a = jnp.maximum(c, after[0]) * (wide_a + 1.0) * (wide_a + 2.0)
        tau_b = jnp.maximum(c, before[0]) * (wide_b + 1.0) * (wide_b + 2.0)
        w_a = jnp.where(last, 1.0, 0.5)
        w_b = jnp.where(first, 1.0, 0.5)
        for i, value in enumerate((tau_a, tau_b, w_a, w_b, w_a * c, w_b * c)):
            geo[direction, i] = value
        rest = (1.0 - (w_a + w_b)) * c
        for n in range(MODES):
            dia[direction, n] = HALF[n] * (tau_a + tau_b + (2.0 * SLOPE[n]) * rest)

    row, lane = rows((8, 128)), lanes((8, 128))
    prepare(2, (prev_z(c), prev_z(df[2])), (next_z(c), next_z(df[2])), lane == 0, lane == 127)
    for d in range(4):
        @pl.when(source[d])
        def _(d=d):
            param_copy(d).wait_recv()
    px, py = gx * 2 + (row >> 2), gy * 4 + (row & 3)
    prepare(0, prev_x(c, df[0], pg[0]), next_x(c, df[0], pg[1]), px == 0, px == 2 * nx - 1)
    before, after = prev_y(c[None], df[1][None], pg[2:3]), next_y(c[None], df[1][None], pg[3:4])
    prepare(1, [v[0] for v in before], [v[0] for v in after], py == 0, py == 4 * ny - 1)

    first_scale, pairs = chebyshev()
    odds = 2.0 * levels.astype(F32) + 1.0

    def geom(direction):
        return tuple(geo[direction, i][None] for i in range(6))

    def start(make, k, at, base):
        for d in range(2):
            @pl.when(exists[base + d])
            def _(d=d):
                make(k, d, at).start()

    def arrive(make, k, at, base):
        for d in range(2):
            @pl.when(source[base + d])
            def _(d=d):
                make(k, d, at).wait_recv()

    def send(k, g, values):
        count = values[0].shape[0]
        (tp, tm, fp, fm), _ = line(values, half_coef[None])
        up, down = pack_x_up(tp, fp), pack_x_down(tm, fm)
        if k < 2:
            xs[k, 0, g] = up
            xs[k, 1, g] = down
        else:
            xs3[0, g] = up
            xs3[1, g] = down
        start(x_copy, k, g, 0)
        (tp, tm, fp, fm), _ = line([u[0:count, n, g] for n in range(MODES)], half_coef[None])
        up, down = pack_y_up(tp, fp), pack_y_down(tm, fm)
        if k < 2:
            ys[k, 0, g] = up
            ys[k, 1, g] = down
        else:
            ys3[0, g] = up
            ys3[1, g] = down
        start(y_copy, k, g, 2)

    loads[2].wait()

    def setup(g, _):
        inside = ym[...] * jnp.where(deg[2] >= g, 1.0, 0.0)[None]
        across = dia[1] + dia[2, g][None]
        scale = odds * ((2.0 * g.astype(F32) + 1.0) / 8.0)
        fresh = []
        for a in range(MODES):
            i = jnp.where(deg[0] >= a, 1.0, 0.0)[None] * inside / (dia[0, a][None] + across)
            r = s[a, :, g] * (scale * (2.0 * a + 1.0))
            x = i * r * first_scale
            s[a, :, g] = r
            inv[a, :, g] = i
            u[a, :, g] = x
            fresh.append(x)
        send(0, g, fresh)
        return 0
    lax.fori_loop(0, MODES, setup, 0)

    def fold_copy(d, b):
        return pltpu.make_async_remote_copy(
            src_ref=folds.at[d, b], dst_ref=folded.at[gy, b], send_sem=f_send.at[d, b],
            recv_sem=f_recv.at[gy, b], device_id={"gy": d}, device_id_type=MESH)

    def fold_arrival(d, b):
        return pltpu.make_async_remote_copy(
            src_ref=folds.at[d, b], dst_ref=folded.at[d, b], send_sem=f_send.at[d, b],
            recv_sem=f_recv.at[d, b], device_id={"gy": d}, device_id_type=MESH)

    def fold(b):
        block = lanes((CMODES**2, 128)) // depth
        for x in range(2):
            by_y = [kept[b, pl.ds(x * 4 + y, CMODES**2, stride=8), :] for y in range(4)]
            for d in range(ny):
                out = jnp.zeros((CMODES**2, 128), F32)
                for y in range(4):
                    shift = ((y - d) * depth) % 128
                    out = jnp.where(block == y, pltpu.roll(by_y[y], shift, 1) if shift else by_y[y], out)
                folds[d, b, x] = out
        for d in range(ny):
            @pl.when(gy // 2 != d // 2)
            def _(d=d):
                fold_copy(d, b).start()
        for d in range(ny):
            @pl.when((gy // 2 == d // 2) & (gy != d))
            def _(d=d):
                fold_copy(d, b).start()

            @pl.when(gy == d)
            def _(d=d):
                folded[d, b] = folds[d, b]

    for k in range(3):
        count = MODES if k < 2 else CMODES

        def pass_z(a, _):
            traces, sums = line([u[a, 0:count, n] for n in range(MODES)], half_coef[None])
            tp, tm, fp, fm = traces
            out = spread(traces, (prev_z(tp), prev_z(fp)), (next_z(tm), next_z(fm)),
                         geom(2), c[None], sums, count)
            for n in range(count):
                acc[a, 0:count, n] = out[n]
            return 0
        lax.fori_loop(0, count, pass_z, 0)

        def pass_xy(g, _, following=False):
            arrive(y_copy, k, g, 2)
            traces, sums = line([u[0:count, n, g] for n in range(MODES)], half_coef[None])
            tp, tm, fp, fm = traces
            g_prev = yg[k, 0, g] if k < 2 else yg3[0, g]
            g_next = yg[k, 1, g] if k < 2 else yg3[1, g]
            out = spread(traces, prev_y(tp, fp, g_prev), next_y(tm, fm, g_next),
                         geom(1), c[None], sums, count)
            for n in range(count):
                acc[0:count, n, g] += out[n]

            arrive(x_copy, k, g, 0)
            values = [u[n, 0:count, g] for n in range(MODES)]
            traces, sums = line(values, half_coef[None])
            tp, tm, fp, fm = traces
            g_prev = xg[k, 0, g] if k < 2 else xg3[0, g]
            g_next = xg[k, 1, g] if k < 2 else xg3[1, g]
            out = spread(traces, prev_x(tp, fp, g_prev), next_x(tm, fm, g_next),
                         geom(0), c[None], sums, count)
            if k < 2:
                fresh = []
                for n in range(MODES):
                    residual = s[n, :, g] - (acc[n, :, g] + out[n])
                    last = values[n] if k < 1 else step[n, :, g]
                    change = pairs[k][0] * last + pairs[k][1] * (inv[n, :, g] * residual)
                    moved = values[n] + change
                    if k < 1:
                        step[n, :, g] = change
                    u[n, :, g] = moved
                    fresh.append(moved)
                if following:
                    width = MODES if k < 1 else CMODES
                    send(k + 1, g, [v[0:width] for v in fresh])
            else:
                low = lax.broadcasted_iota(jnp.int32, (CMODES, 8, 128), 0)
                inside_y = jnp.where(low <= (deg[1] >> 1)[None], 1.0, 0.0)
                inside_z = jnp.where((deg[2] >> 1) >= g, 1.0, 0.0)
                mass = (1.0 / ((2.0 * low.astype(F32) + 1.0) * (2.0 * g.astype(F32) + 1.0))) * (
                    inside_y * inside_z[None])
                for n in range(CMODES):
                    inside = jnp.where((deg[0] >> 1) >= n, 8.0 / (2.0 * n + 1.0), 0.0)
                    residual = s[n, 0:CMODES, g] - (acc[n, 0:CMODES, g] + out[n])
                    kept[g, n * 32:(n + 1) * 32] = (residual * (mass * inside[None])).reshape(32, 128)
                fold(g)
            return 0
        if k == 0:
            lax.fori_loop(0, MODES, functools.partial(pass_xy, following=True), 0)
        elif k == 1:
            lax.fori_loop(0, CMODES, functools.partial(pass_xy, following=True), 0)
            lax.fori_loop(CMODES, MODES, pass_xy, 0)
        else:
            lax.fori_loop(0, CMODES, pass_xy, 0)

    for d in range(ny):
        @pl.when(gy != d)
        def _(d=d):
            for b in range(CMODES):
                fold_arrival(d, b).wait_recv()
    for d in range(ny):
        left[:, d * 128:(d + 1) * 128] = folded[d].reshape(2 * CMODES**3, 128)
    for d in range(ny):
        @pl.when(gy != d)
        def _(d=d):
            for b in range(CMODES):
                fold_copy(d, b).wait_send()

    for d in range(4):
        @pl.when(exists[d])
        def _(d=d):
            param_copy(d).wait_send()
            make = (x_copy, y_copy)[d // 2]
            for k in range(3):
                def finish(i, _):
                    make(k, d % 2, i).wait_send()
                    return 0
                lax.fori_loop(0, MODES if k < 2 else CMODES, finish, 0)


def smoother(nx, ny, rhs, coef, deg):
    field = pltpu.VMEM((MODES, MODES, MODES, 8, 128), F32)
    wide = pltpu.VMEM((2, 2, MODES, MODES, 8, 128), F32)
    narrow = pltpu.VMEM((2, CMODES, CMODES, 8, 128), F32)
    wide_half = pltpu.VMEM((2, 2, MODES, (MODES + 1) // 2, 8, 128), F32)
    narrow_half = pltpu.VMEM((2, CMODES, CMODES // 2, 8, 128), F32)
    return pl.pallas_call(
        functools.partial(kernel, nx, ny),
        out_shape=(jax.ShapeDtypeStruct((MODES, MODES, MODES, 8, 128), F32),
                   jax.ShapeDtypeStruct((2 * CMODES**3, ny * 128), F32)),
        in_specs=[pl.BlockSpec(memory_space=pltpu.HBM)] * 3,
        out_specs=[pl.BlockSpec(memory_space=pltpu.VMEM)] * 2,
        scratch_shapes=[
            field,
            pltpu.VMEM((8, 128), F32),
            pltpu.VMEM((3, 8, 128), jnp.int32),
            field, field, field,
            pltpu.VMEM((3, 6, 8, 128), F32),
            pltpu.VMEM((3, MODES, 8, 128), F32),
            pltpu.VMEM((MODES, 8, 128), F32),
            pltpu.VMEM((4, 8, 128), F32),
            pltpu.VMEM((4, 8, 128), F32),
            wide, wide, wide_half, wide_half, narrow, narrow, narrow_half, narrow_half,
            pltpu.VMEM((CMODES, 128, 128), F32),
            pltpu.VMEM((ny, CMODES, 2, CMODES**2, 128), F32),
            pltpu.VMEM((ny, CMODES, 2, CMODES**2, 128), F32),
            pltpu.SemaphoreType.DMA((3,)),
            pltpu.SemaphoreType.DMA((4,)),
            pltpu.SemaphoreType.DMA((4,)),
            pltpu.SemaphoreType.DMA((3, 2, MODES)),
            pltpu.SemaphoreType.DMA((3, 2, MODES)),
            pltpu.SemaphoreType.DMA((3, 2, MODES)),
            pltpu.SemaphoreType.DMA((3, 2, MODES)),
            pltpu.SemaphoreType.DMA((ny, CMODES)),
            pltpu.SemaphoreType.DMA((ny, CMODES)),
        ],
        compiler_params=pltpu.CompilerParams(
            collective_id=0, has_side_effects=True, vmem_limit_bytes=48 * 1024 * 1024
        ),
    )(*(pltpu.with_memory_space_constraint(v, pltpu.HBM) for v in (rhs, coef, deg)))


def finish_kernel(ny, u, blocks, stored, coarse, order, sem):
    copy = pltpu.make_async_copy(u, stored, sem)
    copy.start()
    depth = 128 // ny
    source_lane = lax.broadcasted_iota(jnp.int32, (128, 512), 0)
    fine_lane = lax.broadcasted_iota(jnp.int32, (128, 512), 1)
    spot = (source_lane % depth) * (4 * ny) + source_lane // depth
    for d in range(ny):
        order[d * 128:(d + 1) * 128] = jnp.where((source_lane < 4 * depth) & (fine_lane == spot + 4 * d), 1.0, 0.0).astype(jnp.bfloat16)
    left = blocks[...]
    total = jnp.zeros((2 * CMODES**3, 512), F32)
    for part in range(3):
        piece = left.astype(jnp.bfloat16)
        total = total + jnp.dot(piece, order[...], preferred_element_type=F32)
        if part < 2:
            left = left - piece.astype(F32)
    for b in range(CMODES):
        for x in range(2):
            for n in range(CMODES):
                for j in range(4):
                    coarse[pl.ds((n * 16 + b) * 8 + j * 2 + x, CMODES, stride=32), :] = total[
                        b * 32 + x * 16 + n * 4:b * 32 + x * 16 + n * 4 + 4, j * 128:(j + 1) * 128]
    copy.wait()


def finish(ny, u, blocks):
    return pl.pallas_call(
        functools.partial(finish_kernel, ny),
        out_shape=(jax.ShapeDtypeStruct(u.shape, F32),
                   jax.ShapeDtypeStruct((CMODES**3 * 8, 128), F32)),
        in_specs=[pl.BlockSpec(memory_space=pl.ANY), pl.BlockSpec(memory_space=pltpu.VMEM)],
        out_specs=[pl.BlockSpec(memory_space=pltpu.HBM), pl.BlockSpec(memory_space=pltpu.VMEM)],
        scratch_shapes=[pltpu.VMEM((ny * 128, 512), jnp.bfloat16), pltpu.SemaphoreType.DMA],
        compiler_params=pltpu.CompilerParams(vmem_limit_bytes=16 * 1024 * 1024),
    )(u, blocks)


def solution(mesh):
    nx, ny = mesh.shape["gx"], mesh.shape["gy"]

    def body(right_side, coefficient, degrees):
        local = right_side.shape[3:]
        flat = (local[0] * local[1], local[2])
        smoothed, blocks = smoother(
            nx, ny,
            right_side.reshape(right_side.shape[:3] + flat),
            coefficient.reshape(flat),
            degrees.reshape((3,) + flat),
        )
        smoothed, coarse = finish(ny, smoothed, blocks)
        coarse = jnp.transpose(coarse.reshape(CMODES**3, 4, 2, 128), (0, 2, 1, 3))
        return smoothed.reshape(right_side.shape), coarse.reshape(CMODES**3, 2, 512)

    in_specs = (
        P(None, None, None, "gx", "gy", None),
        P("gx", "gy", None),
        P(None, "gx", "gy", None),
    )
    out_specs = (P(None, None, None, "gx", "gy", None), P(None, "gx", "gy"))
    return jax.shard_map(body, mesh=mesh, in_specs=in_specs, out_specs=out_specs, check_vma=False)
```

```python
import functools

import jax
import jax.numpy as jnp
from jax import lax
from jax.experimental import pallas as pl
from jax.experimental.pallas import tpu as pltpu
from jax.sharding import PartitionSpec as P

CMODES = 4
LAM_HIGH = 6.0
LAM_LOW = 0.5
MODES = 7
MESH = pl.DeviceIdType.MESH
F32 = jnp.float32
HALF = [(2.0 * n + 1.0) / 2.0 for n in range(MODES)]
SLOPE = [n * (n + 1.0) / 2.0 for n in range(MODES)]


def chebyshev():
    centre = (LAM_HIGH + LAM_LOW) / 2.0
    radius = (LAM_HIGH - LAM_LOW) / 2.0
    ratio = centre / radius
    rho = 1.0 / ratio
    pairs = []
    for _ in range(2):
        following = 1.0 / (2.0 * ratio - rho)
        pairs.append((following * rho, 2.0 * following / radius))
        rho = following
    return 1.0 / centre, pairs


def rows(shape):
    return lax.broadcasted_iota(jnp.int32, shape, len(shape) - 2)


def lanes(shape):
    return lax.broadcasted_iota(jnp.int32, shape, len(shape) - 1)


def turn(v, shift):
    return pltpu.roll(v, shift, v.ndim - 2)


def pack_x_up(p, q):
    return jnp.where(rows(p.shape) < 4, turn(p, 4), q)


def pack_x_down(p, q):
    return jnp.where(rows(p.shape) < 4, p, turn(q, 4))


def prev_x(p, q, g):
    low = rows(p.shape) < 4
    return jnp.where(low, g, turn(p, 4)), turn(jnp.where(low, q, g), 4)


def next_x(p, q, g):
    low = rows(p.shape) < 4
    return turn(jnp.where(low, g, p), 4), jnp.where(low, turn(q, 4), g)


def halves(p):
    half = (p.shape[0] + 1) // 2
    if p.shape[0] == 1:
        return p, p
    high = p[half:]
    if p.shape[0] % 2:
        high = jnp.concatenate([high, p[half - 1:half]], axis=0)
    return p[:half], high


def pack_y_up(p, q):
    (p, p_high), (q, q_high) = halves(p), halves(q)
    r = rows(p.shape) & 3
    return jnp.where(r < 2, jnp.where(r == 0, turn(p, 5), turn(q, 6)), jnp.where(r == 2, turn(p_high, 7), q_high))


def pack_y_down(p, q):
    (p, p_high), (q, q_high) = halves(p), halves(q)
    r = rows(p.shape) & 3
    return jnp.where(r < 2, jnp.where(r == 1, turn(p_high, 1), q_high), jnp.where(r == 3, turn(p, 3), turn(q, 2)))


def open_y(g, count, shifts):
    def both(low, high):
        first = turn(g, low) if low else g
        if count == 1:
            return first
        return jnp.concatenate([first, turn(g, high)[:count - g.shape[0]]], axis=0)
    return both(shifts[0], shifts[1]), both(shifts[2], shifts[3])


def prev_y(p, q, g):
    edge = (rows(p.shape) & 3) == 0
    g = open_y(g, p.shape[0], (0, 6, 7, 5))
    return jnp.where(edge, g[0], turn(p, 1)), jnp.where(edge, g[1], turn(q, 1))


def next_y(p, q, g):
    edge = (rows(p.shape) & 3) == 3
    g = open_y(g, p.shape[0], (0, 2, 1, 3))
    return jnp.where(edge, g[0], turn(p, 7)), jnp.where(edge, g[1], turn(q, 7))


def prev_z(p):
    return jnp.where(lanes(p.shape) == 0, 0.0, pltpu.roll(p, 1, p.ndim - 1))


def next_z(p):
    end = p.shape[-1] - 1
    return jnp.where(lanes(p.shape) == end, 0.0, pltpu.roll(p, end, p.ndim - 1))


def line(u, half_coef):
    t4 = u[4] + u[6]
    t2 = u[2] + t4
    even = u[0] + t2
    t3 = u[3] + u[5]
    odd = u[1] + t3
    s2 = 6.0 * t2
    s4 = s2 + 14.0 * t4
    s6 = s4 + 22.0 * u[6]
    s1 = 2.0 * odd
    s3 = s1 + 10.0 * t3
    s5 = s3 + 18.0 * u[5]
    tp = even + odd
    tm = even - odd
    fp = half_coef * (s6 + s5)
    fm = half_coef * (s5 - s6)
    return (tp, tm, fp, fm), (None, s1, s2, s3, s4, s5, s6)


def spread(traces, before, after, geom, coef, sums, count):
    tp, tm, fp, fm = traces
    tau_a, tau_b, w_a, w_b, k_a, k_b = geom
    jump_a = tp - after[0]
    g_a = tau_a * jump_a - w_a * (fp + after[1])
    jump_b = before[0] - tm
    g_b = tau_b * jump_b - w_b * (before[1] + fm)
    kl = k_a * jump_a
    kr = k_b * jump_b
    p = (g_a - g_b, g_a + g_b)
    q = (kl - kr, kl + kr)
    out = [HALF[0] * p[0]]
    for n in range(1, count):
        out.append(HALF[n] * (coef * sums[n] + (p[n % 2] - SLOPE[n] * q[n % 2])))
    return out


def kernel(nx, ny, rhs_hbm, coef_hbm, deg_hbm, u, coarse, s, coef, deg, inv, step, acc, geo, dia, ym,
           ps, pg, xs, xg, ys, yg, xs3, xg3, ys3, yg3, kept, folds, folded, order,
           in_sem, p_send, p_recv, x_send, x_recv, y_send, y_recv, l_send, l_recv, f_send, f_recv):
    loads = [pltpu.make_async_copy(a, b, in_sem.at[i])
             for i, (a, b) in enumerate(((coef_hbm, coef), (deg_hbm, deg), (rhs_hbm, s)))]
    for load in loads:
        load.start()
    gx, gy = lax.axis_index("gx"), lax.axis_index("gy")
    exists = (gx < nx - 1, gx > 0, gy < ny - 1, gy > 0)
    target = ({"gx": gx + 1}, {"gx": gx - 1}, {"gy": gy + 1}, {"gy": gy - 1})
    source = (exists[1], exists[0], exists[3], exists[2])

    barrier = pltpu.get_barrier_semaphore()
    for d in range(2):
        @pl.when(exists[d])
        def _(d=d):
            pl.semaphore_signal(barrier, inc=1, device_id=target[d], device_id_type=MESH)
    for d in range(ny):
        @pl.when(gy != d)
        def _(d=d):
            pl.semaphore_signal(barrier, inc=1, device_id={"gy": d}, device_id_type=MESH)

    def copy(src, dst, send, recv, d):
        return pltpu.make_async_remote_copy(src_ref=src, dst_ref=dst, send_sem=send, recv_sem=recv,
                                            device_id=target[d], device_id_type=MESH)

    def param_copy(d):
        return copy(ps.at[d], pg.at[d], p_send.at[d], p_recv.at[d], d)

    def x_copy(k, d, b, width=MODES):
        if k < 2:
            part = pl.ds(0, width)
            return copy(xs.at[k, d, b, part], xg.at[k, d, b, part], x_send.at[k, d, b], x_recv.at[k, d, b], d)
        return copy(xs3.at[d, b], xg3.at[d, b], x_send.at[k, d, b], x_recv.at[k, d, b], d)

    def y_copy(k, d, a):
        if k < 2:
            return copy(ys.at[k, d, a], yg.at[k, d, a], y_send.at[k, d, a], y_recv.at[k, d, a], 2 + d)
        return copy(ys3.at[d, a], yg3.at[d, a], y_send.at[k, d, a], y_recv.at[k, d, a], 2 + d)

    def late_copy(d):
        part = (1, d, pl.ds(CMODES, MODES - CMODES), pl.ds(CMODES, MODES - CMODES))
        return copy(xs.at[part], xg.at[part], l_send.at[d], l_recv.at[d], d)

    loads[0].wait()
    loads[1].wait()
    c = coef[...]
    half_coef = 0.5 * c
    depth = 128 // ny
    df = [deg[d].astype(F32) for d in range(3)]
    ps[0] = pack_x_up(c, df[0])
    ps[1] = pack_x_down(c, df[0])
    ps[2] = pack_y_up(c[None], df[1][None])[0]
    ps[3] = pack_y_down(c[None], df[1][None])[0]
    pl.semaphore_wait(barrier, sum(e.astype(jnp.int32) for e in exists[:2]) + (ny - 1))
    for d in range(4):
        @pl.when(exists[d])
        def _(d=d):
            param_copy(d).start()

    for d in range(4):
        @pl.when(jnp.logical_not(source[d]))
        def _(d=d):
            pg[d] = jnp.zeros((8, 128), F32)
            ghosts = (xg, yg)[d // 2]
            ghosts3 = (xg3, yg3)[d // 2]

            def clear(i, _):
                for k in range(2):
                    ghosts[k, d % 2, i] = jnp.zeros(ghosts.shape[3:], F32)
                return 0
            lax.fori_loop(0, MODES, clear, 0)

            def clear3(i, _):
                ghosts3[d % 2, i] = jnp.zeros(ghosts3.shape[2:], F32)
                return 0
            lax.fori_loop(0, CMODES, clear3, 0)

    shape = (MODES, 8, 128)
    levels = lax.broadcasted_iota(jnp.int32, shape, 0)
    ym[...] = jnp.where(levels <= deg[1][None], 1.0, 0.0)

    def prepare(direction, before, after, first, last):
        degree = df[direction]
        wide_a = jnp.maximum(degree, after[1])
        wide_b = jnp.maximum(degree, before[1])
        tau_a = jnp.maximum(c, after[0]) * (wide_a + 1.0) * (wide_a + 2.0)
        tau_b = jnp.maximum(c, before[0]) * (wide_b + 1.0) * (wide_b + 2.0)
        w_a = jnp.where(last, 1.0, 0.5)
        w_b = jnp.where(first, 1.0, 0.5)
        for i, value in enumerate((tau_a, tau_b, w_a, w_b, w_a * c, w_b * c)):
            geo[direction, i] = value
        rest = (1.0 - (w_a + w_b)) * c
        for n in range(MODES):
            dia[direction, n] = HALF[n] * (tau_a + tau_b + (2.0 * SLOPE[n]) * rest)

    row, lane = rows((8, 128)), lanes((8, 128))
    prepare(2, (prev_z(c), prev_z(df[2])), (next_z(c), next_z(df[2])), lane == 0, lane == 127)
    for d in range(4):
        @pl.when(source[d])
        def _(d=d):
            param_copy(d).wait_recv()
    px, py = gx * 2 + (row >> 2), gy * 4 + (row & 3)
    prepare(0, prev_x(c, df[0], pg[0]), next_x(c, df[0], pg[1]), px == 0, px == 2 * nx - 1)
    before, after = prev_y(c[None], df[1][None], pg[2:3]), next_y(c[None], df[1][None], pg[3:4])
    prepare(1, [v[0] for v in before], [v[0] for v in after], py == 0, py == 4 * ny - 1)

    first_scale, pairs = chebyshev()
    odds = 2.0 * levels.astype(F32) + 1.0

    def geom(direction):
        return tuple(geo[direction, i][None] for i in range(6))

    def start(make, k, at, base):
        for d in range(2):
            @pl.when(exists[base + d])
            def _(d=d):
                make(k, d, at).start()

    def arrive(make, k, at, base):
        for d in range(2):
            @pl.when(source[base + d])
            def _(d=d):
                make(k, d, at).wait_recv()

    def send(k, g, values, width=MODES):
        count = values[0].shape[0]
        (tp, tm, fp, fm), _ = line(values, half_coef[None])
        up, down = pack_x_up(tp, fp), pack_x_down(tm, fm)
        if k < 2:
            xs[k, 0, g] = up
            xs[k, 1, g] = down
        else:
            xs3[0, g] = up
            xs3[1, g] = down
        start(functools.partial(x_copy, width=width), k, g, 0)
        (tp, tm, fp, fm), _ = line([u[0:count, n, g] for n in range(MODES)], half_coef[None])
        up, down = pack_y_up(tp, fp), pack_y_down(tm, fm)
        if k < 2:
            ys[k, 0, g] = up
            ys[k, 1, g] = down
        else:
            ys3[0, g] = up
            ys3[1, g] = down
        start(y_copy, k, g, 2)

    loads[2].wait()

    def setup(g, _):
        inside = ym[...] * jnp.where(deg[2] >= g, 1.0, 0.0)[None]
        across = dia[1] + dia[2, g][None]
        scale = odds * ((2.0 * g.astype(F32) + 1.0) / 8.0)
        fresh = []
        for a in range(MODES):
            i = jnp.where(deg[0] >= a, 1.0, 0.0)[None] * inside / (dia[0, a][None] + across)
            r = s[a, :, g] * (scale * (2.0 * a + 1.0))
            x = i * r * first_scale
            s[a, :, g] = r
            inv[a, :, g] = i
            u[a, :, g] = x
            fresh.append(x)
        send(0, g, fresh)
        return 0
    lax.fori_loop(0, MODES, setup, 0)

    def fold_copy(d, b):
        return pltpu.make_async_remote_copy(
            src_ref=folds.at[d, b], dst_ref=folded.at[gy, b], send_sem=f_send.at[d, b],
            recv_sem=f_recv.at[gy, b], device_id={"gy": d}, device_id_type=MESH)

    def fold_arrival(d, b):
        return pltpu.make_async_remote_copy(
            src_ref=folds.at[d, b], dst_ref=folded.at[d, b], send_sem=f_send.at[d, b],
            recv_sem=f_recv.at[d, b], device_id={"gy": d}, device_id_type=MESH)

    def fold(b):
        block = lanes((CMODES**2, 128)) // depth
        for x in range(2):
            by_y = [kept[b, pl.ds(x * 4 + y, CMODES**2, stride=8), :] for y in range(4)]
            for d in range(ny):
                out = jnp.zeros((CMODES**2, 128), F32)
                for y in range(4):
                    shift = ((y - d) * depth) % 128
                    out = jnp.where(block == y, pltpu.roll(by_y[y], shift, 1) if shift else by_y[y], out)
                folds[d, b, x] = out
        for d in range(ny):
            @pl.when(gy // 2 != d // 2)
            def _(d=d):
                fold_copy(d, b).start()
        for d in range(ny):
            @pl.when((gy // 2 == d // 2) & (gy != d))
            def _(d=d):
                fold_copy(d, b).start()

            @pl.when(gy == d)
            def _(d=d):
                folded[d, b] = folds[d, b]

    def x_terms(values, g_prev, g_next, count):
        traces, sums = line(values, half_coef[None])
        tp, tm, fp, fm = traces
        return spread(traces, prev_x(tp, fp, g_prev), next_x(tm, fm, g_next), geom(0), c[None], sums, count)

    def update(k, g, low, high):
        values = [u[n, low:high, g] for n in range(MODES)]
        out = x_terms(values, xg[k, 0, g, low:high], xg[k, 1, g, low:high], MODES)
        fresh = []
        for n in range(MODES):
            residual = s[n, low:high, g] - (acc[n, low:high, g] + out[n])
            last = values[n] if k < 1 else step[n, low:high, g]
            change = pairs[k][0] * last + pairs[k][1] * (inv[n, low:high, g] * residual)
            moved = values[n] + change
            if k < 1:
                step[n, low:high, g] = change
            u[n, low:high, g] = moved
            fresh.append(moved)
        return fresh

    source_lane = lax.broadcasted_iota(jnp.int32, (128, 512), 0)
    fine_lane = lax.broadcasted_iota(jnp.int32, (128, 512), 1)
    spot = (source_lane % depth) * (4 * ny) + source_lane // depth
    for d in range(ny):
        order[d * 128:(d + 1) * 128] = jnp.where(
            (source_lane < 4 * depth) & (fine_lane == spot + 4 * d), 1.0, 0.0).astype(jnp.bfloat16)

    for k in range(3):
        count = MODES if k < 2 else CMODES

        def pass_z(a, _):
            traces, sums = line([u[a, 0:count, n] for n in range(MODES)], half_coef[None])
            tp, tm, fp, fm = traces
            out = spread(traces, (prev_z(tp), prev_z(fp)), (next_z(tm), next_z(fm)),
                         geom(2), c[None], sums, count)
            for n in range(count):
                acc[a, 0:count, n] = out[n]
            return 0
        lax.fori_loop(0, count, pass_z, 0)

        def pass_xy(g, _, following=False, coarse_only=False, last=False):
            arrive(y_copy, k, g, 2)
            traces, sums = line([u[0:count, n, g] for n in range(MODES)], half_coef[None])
            tp, tm, fp, fm = traces
            g_prev = yg[k, 0, g] if k < 2 else yg3[0, g]
            g_next = yg[k, 1, g] if k < 2 else yg3[1, g]
            out = spread(traces, prev_y(tp, fp, g_prev), next_y(tm, fm, g_next),
                         geom(1), c[None], sums, count)
            for n in range(count):
                acc[0:count, n, g] += out[n]

            if k < 2:
                width = CMODES if coarse_only else MODES
                arrive(functools.partial(x_copy, width=width), k, g, 0)
                fresh = update(k, g, 0, width)
                if following:
                    keep = MODES if k < 1 else CMODES
                    send(k + 1, g, [v[0:keep] for v in fresh], CMODES if last else MODES)
            else:
                arrive(x_copy, k, g, 0)
                out = x_terms([u[n, 0:count, g] for n in range(MODES)], xg3[0, g], xg3[1, g], count)
                low = lax.broadcasted_iota(jnp.int32, (CMODES, 8, 128), 0)
                inside_y = jnp.where(low <= (deg[1] >> 1)[None], 1.0, 0.0)
                inside_z = jnp.where((deg[2] >> 1) >= g, 1.0, 0.0)
                mass = (1.0 / ((2.0 * low.astype(F32) + 1.0) * (2.0 * g.astype(F32) + 1.0))) * (
                    inside_y * inside_z[None])
                for n in range(CMODES):
                    inside = jnp.where((deg[0] >> 1) >= n, 8.0 / (2.0 * n + 1.0), 0.0)
                    residual = s[n, 0:CMODES, g] - (acc[n, 0:CMODES, g] + out[n])
                    kept[g, n * 32:(n + 1) * 32] = (residual * (mass * inside[None])).reshape(32, 128)
                fold(g)
            return 0
        if k == 0:
            lax.fori_loop(0, CMODES, functools.partial(pass_xy, following=True), 0)
            lax.fori_loop(CMODES, MODES, functools.partial(pass_xy, following=True, last=True), 0)
        elif k == 1:
            lax.fori_loop(0, CMODES, functools.partial(pass_xy, following=True), 0)
            lax.fori_loop(CMODES, MODES, functools.partial(pass_xy, coarse_only=True), 0)
            for d in range(2):
                @pl.when(exists[d])
                def _(d=d):
                    late_copy(d).start()
        else:
            lax.fori_loop(0, CMODES, pass_xy, 0)

    for d in range(2):
        @pl.when(source[d])
        def _(d=d):
            late_copy(d).wait_recv()

    def pass_late(g, _):
        update(1, g, CMODES, MODES)
        return 0
    lax.fori_loop(CMODES, MODES, pass_late, 0)

    def gather(g, _):
        for d in range(ny):
            @pl.when(gy != d)
            def _(d=d):
                fold_arrival(d, g).wait_recv()
        pieces = []
        rest = jnp.concatenate([folded[d, g].reshape(2 * CMODES**2, 128) for d in range(ny)], axis=1)
        for part in range(3):
            pieces.append(rest.astype(jnp.bfloat16))
            if part < 2:
                rest = rest - pieces[-1].astype(F32)
        total = jnp.dot(jnp.concatenate(pieces, axis=0), order[...], preferred_element_type=F32)
        total = total[0:32] + total[32:64] + total[64:96]
        for x in range(2):
            for a in range(CMODES):
                for j in range(4):
                    coarse[pl.ds((a * 16 + g) * 8 + j * 2 + x, CMODES, stride=32), :] = total[
                        x * 16 + a * 4:x * 16 + a * 4 + 4, j * 128:(j + 1) * 128]
        return 0
    lax.fori_loop(0, CMODES, gather, 0)

    for d in range(ny):
        @pl.when(gy != d)
        def _(d=d):
            for b in range(CMODES):
                fold_copy(d, b).wait_send()

    for d in range(4):
        @pl.when(exists[d])
        def _(d=d):
            param_copy(d).wait_send()
            if d < 2:
                late_copy(d).wait_send()
            make = (x_copy, y_copy)[d // 2]
            for k in range(3):
                def finish(i, _, make=make):
                    make(k, d % 2, i).wait_send()
                    return 0
                if d < 2 and k == 1:
                    lax.fori_loop(0, CMODES, finish, 0)
                    lax.fori_loop(CMODES, MODES, functools.partial(
                        finish, make=functools.partial(x_copy, width=CMODES)), 0)
                else:
                    lax.fori_loop(0, MODES if k < 2 else CMODES, finish, 0)


def smoother(nx, ny, rhs, coef, deg):
    field = pltpu.VMEM((MODES, MODES, MODES, 8, 128), F32)
    wide = pltpu.VMEM((2, 2, MODES, MODES, 8, 128), F32)
    narrow = pltpu.VMEM((2, CMODES, CMODES, 8, 128), F32)
    wide_half = pltpu.VMEM((2, 2, MODES, (MODES + 1) // 2, 8, 128), F32)
    narrow_half = pltpu.VMEM((2, CMODES, CMODES // 2, 8, 128), F32)
    return pl.pallas_call(
        functools.partial(kernel, nx, ny),
        out_shape=(jax.ShapeDtypeStruct((MODES, MODES, MODES, 8, 128), F32),
                   jax.ShapeDtypeStruct((CMODES**3 * 8, 128), F32)),
        in_specs=[pl.BlockSpec(memory_space=pltpu.HBM)] * 3,
        out_specs=[pl.BlockSpec(memory_space=pltpu.VMEM)] * 2,
        scratch_shapes=[
            field,
            pltpu.VMEM((8, 128), F32),
            pltpu.VMEM((3, 8, 128), jnp.int32),
            field, field, field,
            pltpu.VMEM((3, 6, 8, 128), F32),
            pltpu.VMEM((3, MODES, 8, 128), F32),
            pltpu.VMEM((MODES, 8, 128), F32),
            pltpu.VMEM((4, 8, 128), F32),
            pltpu.VMEM((4, 8, 128), F32),
            wide, wide, wide_half, wide_half, narrow, narrow, narrow_half, narrow_half,
            pltpu.VMEM((CMODES, 128, 128), F32),
            pltpu.VMEM((ny, CMODES, 2, CMODES**2, 128), F32),
            pltpu.VMEM((ny, CMODES, 2, CMODES**2, 128), F32),
            pltpu.VMEM((ny * 128, 512), jnp.bfloat16),
            pltpu.SemaphoreType.DMA((3,)),
            pltpu.SemaphoreType.DMA((4,)),
            pltpu.SemaphoreType.DMA((4,)),
            pltpu.SemaphoreType.DMA((3, 2, MODES)),
            pltpu.SemaphoreType.DMA((3, 2, MODES)),
            pltpu.SemaphoreType.DMA((3, 2, MODES)),
            pltpu.SemaphoreType.DMA((3, 2, MODES)),
            pltpu.SemaphoreType.DMA((2,)),
            pltpu.SemaphoreType.DMA((2,)),
            pltpu.SemaphoreType.DMA((ny, CMODES)),
            pltpu.SemaphoreType.DMA((ny, CMODES)),
        ],
        compiler_params=pltpu.CompilerParams(
            collective_id=0, has_side_effects=True, vmem_limit_bytes=48 * 1024 * 1024
        ),
    )(*(pltpu.with_memory_space_constraint(v, pltpu.HBM) for v in (rhs, coef, deg)))


def finish_kernel(u, blocks, stored, coarse, sem):
    copies = [pltpu.make_async_copy(a, b, sem.at[i]) for i, (a, b) in enumerate(((u, stored), (blocks, coarse)))]
    for copy in copies:
        copy.start()
    for copy in copies:
        copy.wait()


def finish(u, blocks):
    return pl.pallas_call(
        finish_kernel,
        out_shape=(jax.ShapeDtypeStruct(u.shape, F32), jax.ShapeDtypeStruct(blocks.shape, F32)),
        in_specs=[pl.BlockSpec(memory_space=pl.ANY)] * 2,
        out_specs=[pl.BlockSpec(memory_space=pltpu.HBM)] * 2,
        scratch_shapes=[pltpu.SemaphoreType.DMA((2,))],
        compiler_params=pltpu.CompilerParams(vmem_limit_bytes=16 * 1024 * 1024),
    )(u, blocks)


def solution(mesh):
    nx, ny = mesh.shape["gx"], mesh.shape["gy"]

    def body(right_side, coefficient, degrees):
        local = right_side.shape[3:]
        flat = (local[0] * local[1], local[2])
        smoothed, blocks = smoother(
            nx, ny,
            right_side.reshape(right_side.shape[:3] + flat),
            coefficient.reshape(flat),
            degrees.reshape((3,) + flat),
        )
        smoothed, coarse = finish(smoothed, blocks)
        coarse = jnp.transpose(coarse.reshape(CMODES**3, 4, 2, 128), (0, 2, 1, 3))
        return smoothed.reshape(right_side.shape), coarse.reshape(CMODES**3, 2, 512)

    in_specs = (
        P(None, None, None, "gx", "gy", None),
        P("gx", "gy", None),
        P(None, "gx", "gy", None),
    )
    out_specs = (P(None, None, None, "gx", "gy", None), P(None, "gx", "gy"))
    return jax.shard_map(body, mesh=mesh, in_specs=in_specs, out_specs=out_specs, check_vma=False)
```

```python
import functools

import jax
import jax.numpy as jnp
from jax import lax
from jax.experimental import pallas as pl
from jax.experimental.pallas import tpu as pltpu
from jax.sharding import PartitionSpec as P

CMODES = 4
LAM_HIGH = 6.0
LAM_LOW = 0.5
MODES = 7
MESH = pl.DeviceIdType.MESH
F32 = jnp.float32
HALF = [(2.0 * n + 1.0) / 2.0 for n in range(MODES)]
SLOPE = [n * (n + 1.0) / 2.0 for n in range(MODES)]


def chebyshev():
    centre = (LAM_HIGH + LAM_LOW) / 2.0
    radius = (LAM_HIGH - LAM_LOW) / 2.0
    ratio = centre / radius
    rho = 1.0 / ratio
    pairs = []
    for _ in range(2):
        following = 1.0 / (2.0 * ratio - rho)
        pairs.append((following * rho, 2.0 * following / radius))
        rho = following
    return 1.0 / centre, pairs


def rows(shape):
    return lax.broadcasted_iota(jnp.int32, shape, len(shape) - 2)


def lanes(shape):
    return lax.broadcasted_iota(jnp.int32, shape, len(shape) - 1)


def turn(v, shift):
    return pltpu.roll(v, shift, v.ndim - 2)


def pack_x_up(p, q):
    return jnp.where(rows(p.shape) < 4, turn(p, 4), q)


def pack_x_down(p, q):
    return jnp.where(rows(p.shape) < 4, p, turn(q, 4))


def prev_x(p, q, g):
    low = rows(p.shape) < 4
    return jnp.where(low, g, turn(p, 4)), turn(jnp.where(low, q, g), 4)


def next_x(p, q, g):
    low = rows(p.shape) < 4
    return turn(jnp.where(low, g, p), 4), jnp.where(low, turn(q, 4), g)


def halves(p):
    half = (p.shape[0] + 1) // 2
    if p.shape[0] == 1:
        return p, p
    high = p[half:]
    if p.shape[0] % 2:
        high = jnp.concatenate([high, p[half - 1:half]], axis=0)
    return p[:half], high


def pack_y_up(p, q):
    (p, p_high), (q, q_high) = halves(p), halves(q)
    r = rows(p.shape) & 3
    return jnp.where(r < 2, jnp.where(r == 0, turn(p, 5), turn(q, 6)), jnp.where(r == 2, turn(p_high, 7), q_high))


def pack_y_down(p, q):
    (p, p_high), (q, q_high) = halves(p), halves(q)
    r = rows(p.shape) & 3
    return jnp.where(r < 2, jnp.where(r == 1, turn(p_high, 1), q_high), jnp.where(r == 3, turn(p, 3), turn(q, 2)))


def open_y(g, count, shifts):
    def both(low, high):
        first = turn(g, low) if low else g
        if count == 1:
            return first
        return jnp.concatenate([first, turn(g, high)[:count - g.shape[0]]], axis=0)
    return both(shifts[0], shifts[1]), both(shifts[2], shifts[3])


def prev_y(p, q, g):
    edge = (rows(p.shape) & 3) == 0
    g = open_y(g, p.shape[0], (0, 6, 7, 5))
    return jnp.where(edge, g[0], turn(p, 1)), jnp.where(edge, g[1], turn(q, 1))


def next_y(p, q, g):
    edge = (rows(p.shape) & 3) == 3
    g = open_y(g, p.shape[0], (0, 2, 1, 3))
    return jnp.where(edge, g[0], turn(p, 7)), jnp.where(edge, g[1], turn(q, 7))


def prev_z(p):
    return jnp.where(lanes(p.shape) == 0, 0.0, pltpu.roll(p, 1, p.ndim - 1))


def next_z(p):
    end = p.shape[-1] - 1
    return jnp.where(lanes(p.shape) == end, 0.0, pltpu.roll(p, end, p.ndim - 1))


def line(u, half_coef):
    t4 = u[4] + u[6]
    t2 = u[2] + t4
    even = u[0] + t2
    t3 = u[3] + u[5]
    odd = u[1] + t3
    s2 = 6.0 * t2
    s4 = s2 + 14.0 * t4
    s6 = s4 + 22.0 * u[6]
    s1 = 2.0 * odd
    s3 = s1 + 10.0 * t3
    s5 = s3 + 18.0 * u[5]
    tp = even + odd
    tm = even - odd
    fp = half_coef * (s6 + s5)
    fm = half_coef * (s5 - s6)
    return (tp, tm, fp, fm), (None, s1, s2, s3, s4, s5, s6)


def spread(traces, before, after, geom, coef, sums, count):
    tp, tm, fp, fm = traces
    tau_a, tau_b, w_a, w_b, k_a, k_b = geom
    jump_a = tp - after[0]
    g_a = tau_a * jump_a - w_a * (fp + after[1])
    jump_b = before[0] - tm
    g_b = tau_b * jump_b - w_b * (before[1] + fm)
    kl = k_a * jump_a
    kr = k_b * jump_b
    p = (g_a - g_b, g_a + g_b)
    q = (kl - kr, kl + kr)
    out = [HALF[0] * p[0]]
    for n in range(1, count):
        out.append(HALF[n] * (coef * sums[n] + (p[n % 2] - SLOPE[n] * q[n % 2])))
    return out


def kernel(nx, ny, rhs_hbm, coef_hbm, deg_hbm, u, coarse, s, coef, deg, inv, step, acc, geo, dia, ym,
           ps, pg, xs, xg, ys, yg, xs3, xg3, ys3, yg3, kept, folds, folded, order,
           in_sem, p_send, p_recv, x_send, x_recv, y_send, y_recv, l_send, l_recv, f_send, f_recv):
    loads = [pltpu.make_async_copy(a, b, in_sem.at[i])
             for i, (a, b) in enumerate(((coef_hbm, coef), (deg_hbm, deg), (rhs_hbm, s)))]
    for load in loads:
        load.start()
    gx, gy = lax.axis_index("gx"), lax.axis_index("gy")
    exists = (gx < nx - 1, gx > 0, gy < ny - 1, gy > 0)
    target = ({"gx": gx + 1}, {"gx": gx - 1}, {"gy": gy + 1}, {"gy": gy - 1})
    source = (exists[1], exists[0], exists[3], exists[2])

    barrier = pltpu.get_barrier_semaphore()
    near = ny <= 4
    for d in range(4 if near else 2):
        @pl.when(exists[d])
        def _(d=d):
            pl.semaphore_signal(barrier, inc=1, device_id=target[d], device_id_type=MESH)
    for d in range(0 if near else ny):
        @pl.when(gy != d)
        def _(d=d):
            pl.semaphore_signal(barrier, inc=1, device_id={"gy": d}, device_id_type=MESH)
    greeted = sum(e.astype(jnp.int32) for e in (exists if near else exists[:2])) + (0 if near else ny - 1)

    def copy(src, dst, send, recv, d):
        return pltpu.make_async_remote_copy(src_ref=src, dst_ref=dst, send_sem=send, recv_sem=recv,
                                            device_id=target[d], device_id_type=MESH)

    def param_copy(d):
        return copy(ps.at[d], pg.at[d], p_send.at[d], p_recv.at[d], d)

    def x_copy(k, d, b, width=MODES):
        if k < 2:
            part = pl.ds(0, width)
            return copy(xs.at[k, d, b, part], xg.at[k, d, b, part], x_send.at[k, d, b], x_recv.at[k, d, b], d)
        return copy(xs3.at[d, b], xg3.at[d, b], x_send.at[k, d, b], x_recv.at[k, d, b], d)

    def y_copy(k, d, a):
        if k < 2:
            return copy(ys.at[k, d, a], yg.at[k, d, a], y_send.at[k, d, a], y_recv.at[k, d, a], 2 + d)
        return copy(ys3.at[d, a], yg3.at[d, a], y_send.at[k, d, a], y_recv.at[k, d, a], 2 + d)

    def late_copy(d):
        part = (1, d, pl.ds(CMODES, MODES - CMODES), pl.ds(CMODES, MODES - CMODES))
        return copy(xs.at[part], xg.at[part], l_send.at[d], l_recv.at[d], d)

    loads[0].wait()
    loads[1].wait()
    c = coef[...]
    half_coef = 0.5 * c
    depth = 128 // ny
    df = [deg[d].astype(F32) for d in range(3)]
    ps[0] = pack_x_up(c, df[0])
    ps[1] = pack_x_down(c, df[0])
    ps[2] = pack_y_up(c[None], df[1][None])[0]
    ps[3] = pack_y_down(c[None], df[1][None])[0]
    pl.semaphore_wait(barrier, greeted)
    for d in range(4):
        @pl.when(exists[d])
        def _(d=d):
            param_copy(d).start()

    for d in range(4):
        @pl.when(jnp.logical_not(source[d]))
        def _(d=d):
            pg[d] = jnp.zeros((8, 128), F32)
            ghosts = (xg, yg)[d // 2]
            ghosts3 = (xg3, yg3)[d // 2]

            def clear(i, _):
                for k in range(2):
                    ghosts[k, d % 2, i] = jnp.zeros(ghosts.shape[3:], F32)
                return 0
            lax.fori_loop(0, MODES, clear, 0)

            def clear3(i, _):
                ghosts3[d % 2, i] = jnp.zeros(ghosts3.shape[2:], F32)
                return 0
            lax.fori_loop(0, CMODES, clear3, 0)

    shape = (MODES, 8, 128)
    levels = lax.broadcasted_iota(jnp.int32, shape, 0)
    ym[...] = jnp.where(levels <= deg[1][None], 1.0, 0.0)

    def prepare(direction, before, after, first, last):
        degree = df[direction]
        wide_a = jnp.maximum(degree, after[1])
        wide_b = jnp.maximum(degree, before[1])
        tau_a = jnp.maximum(c, after[0]) * (wide_a + 1.0) * (wide_a + 2.0)
        tau_b = jnp.maximum(c, before[0]) * (wide_b + 1.0) * (wide_b + 2.0)
        w_a = jnp.where(last, 1.0, 0.5)
        w_b = jnp.where(first, 1.0, 0.5)
        for i, value in enumerate((tau_a, tau_b, w_a, w_b, w_a * c, w_b * c)):
            geo[direction, i] = value
        rest = (1.0 - (w_a + w_b)) * c
        for n in range(MODES):
            dia[direction, n] = HALF[n] * (tau_a + tau_b + (2.0 * SLOPE[n]) * rest)

    row, lane = rows((8, 128)), lanes((8, 128))
    prepare(2, (prev_z(c), prev_z(df[2])), (next_z(c), next_z(df[2])), lane == 0, lane == 127)
    for d in range(4):
        @pl.when(source[d])
        def _(d=d):
            param_copy(d).wait_recv()
    px, py = gx * 2 + (row >> 2), gy * 4 + (row & 3)
    prepare(0, prev_x(c, df[0], pg[0]), next_x(c, df[0], pg[1]), px == 0, px == 2 * nx - 1)
    before, after = prev_y(c[None], df[1][None], pg[2:3]), next_y(c[None], df[1][None], pg[3:4])
    prepare(1, [v[0] for v in before], [v[0] for v in after], py == 0, py == 4 * ny - 1)

    first_scale, pairs = chebyshev()
    odds = 2.0 * levels.astype(F32) + 1.0

    def geom(direction):
        return tuple(geo[direction, i][None] for i in range(6))

    def start(make, k, at, base):
        for d in range(2):
            @pl.when(exists[base + d])
            def _(d=d):
                make(k, d, at).start()

    def arrive(make, k, at, base):
        for d in range(2):
            @pl.when(source[base + d])
            def _(d=d):
                make(k, d, at).wait_recv()

    def send(k, g, values, width=MODES):
        count = values[0].shape[0]
        (tp, tm, fp, fm), _ = line(values, half_coef[None])
        up, down = pack_x_up(tp, fp), pack_x_down(tm, fm)
        if k < 2:
            xs[k, 0, g] = up
            xs[k, 1, g] = down
        else:
            xs3[0, g] = up
            xs3[1, g] = down
        start(functools.partial(x_copy, width=width), k, g, 0)
        (tp, tm, fp, fm), _ = line([u[0:count, n, g] for n in range(MODES)], half_coef[None])
        up, down = pack_y_up(tp, fp), pack_y_down(tm, fm)
        if k < 2:
            ys[k, 0, g] = up
            ys[k, 1, g] = down
        else:
            ys3[0, g] = up
            ys3[1, g] = down
        start(y_copy, k, g, 2)

    loads[2].wait()

    def setup(g, _):
        inside = ym[...] * jnp.where(deg[2] >= g, 1.0, 0.0)[None]
        across = dia[1] + dia[2, g][None]
        scale = odds * ((2.0 * g.astype(F32) + 1.0) / 8.0)
        fresh = []
        for a in range(MODES):
            i = jnp.where(deg[0] >= a, 1.0, 0.0)[None] * inside / (dia[0, a][None] + across)
            r = s[a, :, g] * (scale * (2.0 * a + 1.0))
            x = i * r * first_scale
            s[a, :, g] = r
            inv[a, :, g] = i
            u[a, :, g] = x
            fresh.append(x)
        send(0, g, fresh)
        return 0
    lax.fori_loop(0, MODES, setup, 0)

    def fold_copy(d, b):
        return pltpu.make_async_remote_copy(
            src_ref=folds.at[d, b], dst_ref=folded.at[gy, b], send_sem=f_send.at[d, b],
            recv_sem=f_recv.at[gy, b], device_id={"gy": d}, device_id_type=MESH)

    def fold_arrival(d, b):
        return pltpu.make_async_remote_copy(
            src_ref=folds.at[d, b], dst_ref=folded.at[d, b], send_sem=f_send.at[d, b],
            recv_sem=f_recv.at[d, b], device_id={"gy": d}, device_id_type=MESH)

    def fold(b):
        block = lanes((CMODES**2, 128)) // depth
        for x in range(2):
            by_y = [kept[b, pl.ds(x * 4 + y, CMODES**2, stride=8), :] for y in range(4)]
            for d in range(ny):
                out = jnp.zeros((CMODES**2, 128), F32)
                for y in range(4):
                    shift = ((y - d) * depth) % 128
                    out = jnp.where(block == y, pltpu.roll(by_y[y], shift, 1) if shift else by_y[y], out)
                folds[d, b, x] = out
        for d in range(ny):
            @pl.when(gy // 2 != d // 2)
            def _(d=d):
                fold_copy(d, b).start()
        for d in range(ny):
            @pl.when((gy // 2 == d // 2) & (gy != d))
            def _(d=d):
                fold_copy(d, b).start()

            @pl.when(gy == d)
            def _(d=d):
                folded[d, b] = folds[d, b]

    def x_terms(values, g_prev, g_next, count):
        traces, sums = line(values, half_coef[None])
        tp, tm, fp, fm = traces
        return spread(traces, prev_x(tp, fp, g_prev), next_x(tm, fm, g_next), geom(0), c[None], sums, count)

    def update(k, g, low, high):
        values = [u[n, low:high, g] for n in range(MODES)]
        out = x_terms(values, xg[k, 0, g, low:high], xg[k, 1, g, low:high], MODES)
        fresh = []
        for n in range(MODES):
            residual = s[n, low:high, g] - (acc[n, low:high, g] + out[n])
            last = values[n] if k < 1 else step[n, low:high, g]
            change = pairs[k][0] * last + pairs[k][1] * (inv[n, low:high, g] * residual)
            moved = values[n] + change
            if k < 1:
                step[n, low:high, g] = change
            u[n, low:high, g] = moved
            fresh.append(moved)
        return fresh

    source_lane = lax.broadcasted_iota(jnp.int32, (128, 512), 0)
    fine_lane = lax.broadcasted_iota(jnp.int32, (128, 512), 1)
    spot = (source_lane % depth) * (4 * ny) + source_lane // depth
    for d in range(ny):
        order[d * 128:(d + 1) * 128] = jnp.where(
            (source_lane < 4 * depth) & (fine_lane == spot + 4 * d), 1.0, 0.0).astype(jnp.bfloat16)

    for k in range(3):
        count = MODES if k < 2 else CMODES

        def pass_z(a, _):
            traces, sums = line([u[a, 0:count, n] for n in range(MODES)], half_coef[None])
            tp, tm, fp, fm = traces
            out = spread(traces, (prev_z(tp), prev_z(fp)), (next_z(tm), next_z(fm)),
                         geom(2), c[None], sums, count)
            for n in range(count):
                acc[a, 0:count, n] = out[n]
            return 0
        lax.fori_loop(0, count, pass_z, 0)

        def pass_xy(g, _, following=False, coarse_only=False, last=False):
            arrive(y_copy, k, g, 2)
            traces, sums = line([u[0:count, n, g] for n in range(MODES)], half_coef[None])
            tp, tm, fp, fm = traces
            g_prev = yg[k, 0, g] if k < 2 else yg3[0, g]
            g_next = yg[k, 1, g] if k < 2 else yg3[1, g]
            out = spread(traces, prev_y(tp, fp, g_prev), next_y(tm, fm, g_next),
                         geom(1), c[None], sums, count)
            for n in range(count):
                acc[0:count, n, g] += out[n]

            if k < 2:
                width = CMODES if coarse_only else MODES
                arrive(functools.partial(x_copy, width=width), k, g, 0)
                fresh = update(k, g, 0, width)
                if following:
                    keep = MODES if k < 1 else CMODES
                    send(k + 1, g, [v[0:keep] for v in fresh], CMODES if last else MODES)
            else:
                arrive(x_copy, k, g, 0)
                out = x_terms([u[n, 0:count, g] for n in range(MODES)], xg3[0, g], xg3[1, g], count)
                low = lax.broadcasted_iota(jnp.int32, (CMODES, 8, 128), 0)
                inside_y = jnp.where(low <= (deg[1] >> 1)[None], 1.0, 0.0)
                inside_z = jnp.where((deg[2] >> 1) >= g, 1.0, 0.0)
                mass = (1.0 / ((2.0 * low.astype(F32) + 1.0) * (2.0 * g.astype(F32) + 1.0))) * (
                    inside_y * inside_z[None])
                for n in range(CMODES):
                    inside = jnp.where((deg[0] >> 1) >= n, 8.0 / (2.0 * n + 1.0), 0.0)
                    residual = s[n, 0:CMODES, g] - (acc[n, 0:CMODES, g] + out[n])
                    kept[g, n * 32:(n + 1) * 32] = (residual * (mass * inside[None])).reshape(32, 128)
                fold(g)
            return 0
        if k == 0:
            lax.fori_loop(0, CMODES, functools.partial(pass_xy, following=True), 0)
            lax.fori_loop(CMODES, MODES, functools.partial(pass_xy, following=True, last=True), 0)
        elif k == 1:
            lax.fori_loop(0, CMODES, functools.partial(pass_xy, following=True), 0)
            lax.fori_loop(CMODES, MODES, functools.partial(pass_xy, coarse_only=True), 0)
            for d in range(2):
                @pl.when(exists[d])
                def _(d=d):
                    late_copy(d).start()
        else:
            lax.fori_loop(0, CMODES, pass_xy, 0)

    def gather(g, _):
        for d in range(ny):
            @pl.when(gy != d)
            def _(d=d):
                fold_copy(d, g).wait_send()
                fold_arrival(d, g).wait_recv()
        pieces = []
        rest = jnp.concatenate([folded[d, g].reshape(2 * CMODES**2, 128) for d in range(ny)], axis=1)
        for part in range(3):
            pieces.append(rest.astype(jnp.bfloat16))
            if part < 2:
                rest = rest - pieces[-1].astype(F32)
        total = jnp.dot(jnp.concatenate(pieces, axis=0), order[...], preferred_element_type=F32)
        total = total[0:32] + total[32:64] + total[64:96]
        for x in range(2):
            for a in range(CMODES):
                for j in range(4):
                    coarse[pl.ds((a * 16 + g) * 8 + j * 2 + x, CMODES, stride=32), :] = total[
                        x * 16 + a * 4:x * 16 + a * 4 + 4, j * 128:(j + 1) * 128]
        return 0
    for d in range(4):
        @pl.when(exists[d])
        def _(d=d):
            param_copy(d).wait_send()
            make = (x_copy, y_copy)[d // 2]
            for k in range(3):
                def sent(i, _, make=make):
                    make(k, d % 2, i).wait_send()
                    return 0
                if d < 2 and k == 1:
                    lax.fori_loop(0, CMODES, sent, 0)
                    lax.fori_loop(CMODES, MODES, functools.partial(
                        sent, make=functools.partial(x_copy, width=CMODES)), 0)
                else:
                    lax.fori_loop(0, MODES if k < 2 else CMODES, sent, 0)
    lax.fori_loop(0, 2, gather, 0)
    for d in range(2):
        @pl.when(source[d])
        def _(d=d):
            late_copy(d).wait_recv()

    def pass_late(g, _):
        update(1, g, CMODES, MODES)
        return 0
    lax.fori_loop(CMODES, MODES, pass_late, 0)

    for d in range(2):
        @pl.when(exists[d])
        def _(d=d):
            late_copy(d).wait_send()
    lax.fori_loop(2, CMODES, gather, 0)


def smoother(nx, ny, rhs, coef, deg):
    field = pltpu.VMEM((MODES, MODES, MODES, 8, 128), F32)
    wide = pltpu.VMEM((2, 2, MODES, MODES, 8, 128), F32)
    narrow = pltpu.VMEM((2, CMODES, CMODES, 8, 128), F32)
    wide_half = pltpu.VMEM((2, 2, MODES, (MODES + 1) // 2, 8, 128), F32)
    narrow_half = pltpu.VMEM((2, CMODES, CMODES // 2, 8, 128), F32)
    return pl.pallas_call(
        functools.partial(kernel, nx, ny),
        out_shape=(jax.ShapeDtypeStruct((MODES, MODES, MODES, 8, 128), F32),
                   jax.ShapeDtypeStruct((CMODES**3 * 8, 128), F32)),
        in_specs=[pl.BlockSpec(memory_space=pltpu.HBM)] * 3,
        out_specs=[pl.BlockSpec(memory_space=pltpu.VMEM)] * 2,
        scratch_shapes=[
            field,
            pltpu.VMEM((8, 128), F32),
            pltpu.VMEM((3, 8, 128), jnp.int32),
            field, field, field,
            pltpu.VMEM((3, 6, 8, 128), F32),
            pltpu.VMEM((3, MODES, 8, 128), F32),
            pltpu.VMEM((MODES, 8, 128), F32),
            pltpu.VMEM((4, 8, 128), F32),
            pltpu.VMEM((4, 8, 128), F32),
            wide, wide, wide_half, wide_half, narrow, narrow, narrow_half, narrow_half,
            pltpu.VMEM((CMODES, 128, 128), F32),
            pltpu.VMEM((ny, CMODES, 2, CMODES**2, 128), F32),
            pltpu.VMEM((ny, CMODES, 2, CMODES**2, 128), F32),
            pltpu.VMEM((ny * 128, 512), jnp.bfloat16),
            pltpu.SemaphoreType.DMA((3,)),
            pltpu.SemaphoreType.DMA((4,)),
            pltpu.SemaphoreType.DMA((4,)),
            pltpu.SemaphoreType.DMA((3, 2, MODES)),
            pltpu.SemaphoreType.DMA((3, 2, MODES)),
            pltpu.SemaphoreType.DMA((3, 2, MODES)),
            pltpu.SemaphoreType.DMA((3, 2, MODES)),
            pltpu.SemaphoreType.DMA((2,)),
            pltpu.SemaphoreType.DMA((2,)),
            pltpu.SemaphoreType.DMA((ny, CMODES)),
            pltpu.SemaphoreType.DMA((ny, CMODES)),
        ],
        compiler_params=pltpu.CompilerParams(
            collective_id=0, has_side_effects=True, vmem_limit_bytes=48 * 1024 * 1024
        ),
    )(*(pltpu.with_memory_space_constraint(v, pltpu.HBM) for v in (rhs, coef, deg)))


def finish_kernel(u, blocks, stored, coarse, sem):
    copies = [pltpu.make_async_copy(a, b, sem.at[i]) for i, (a, b) in enumerate(((u, stored), (blocks, coarse)))]
    for copy in copies:
        copy.start()
    for copy in copies:
        copy.wait()


def finish(u, blocks):
    return pl.pallas_call(
        finish_kernel,
        out_shape=(jax.ShapeDtypeStruct(u.shape, F32), jax.ShapeDtypeStruct(blocks.shape, F32)),
        in_specs=[pl.BlockSpec(memory_space=pl.ANY)] * 2,
        out_specs=[pl.BlockSpec(memory_space=pltpu.HBM)] * 2,
        scratch_shapes=[pltpu.SemaphoreType.DMA((2,))],
        compiler_params=pltpu.CompilerParams(vmem_limit_bytes=16 * 1024 * 1024),
    )(u, blocks)


def solution(mesh):
    nx, ny = mesh.shape["gx"], mesh.shape["gy"]

    def body(right_side, coefficient, degrees):
        local = right_side.shape[3:]
        flat = (local[0] * local[1], local[2])
        smoothed, blocks = smoother(
            nx, ny,
            right_side.reshape(right_side.shape[:3] + flat),
            coefficient.reshape(flat),
            degrees.reshape((3,) + flat),
        )
        smoothed, coarse = finish(smoothed, blocks)
        coarse = jnp.transpose(coarse.reshape(CMODES**3, 4, 2, 128), (0, 2, 1, 3))
        return smoothed.reshape(right_side.shape), coarse.reshape(CMODES**3, 2, 512)

    in_specs = (
        P(None, None, None, "gx", "gy", None),
        P("gx", "gy", None),
        P(None, "gx", "gy", None),
    )
    out_specs = (P(None, None, None, "gx", "gy", None), P(None, "gx", "gy"))
    return jax.shard_map(body, mesh=mesh, in_specs=in_specs, out_specs=out_specs, check_vma=False)
```

```python
import functools

import jax
import jax.numpy as jnp
from jax import lax
from jax.experimental import pallas as pl
from jax.experimental.pallas import tpu as pltpu
from jax.sharding import PartitionSpec as P

CMODES = 4
LAM_HIGH = 6.0
LAM_LOW = 0.5
MODES = 7
EARLY = 2
MESH = pl.DeviceIdType.MESH
F32 = jnp.float32
HALF = [(2.0 * n + 1.0) / 2.0 for n in range(MODES)]
SLOPE = [n * (n + 1.0) / 2.0 for n in range(MODES)]


def chebyshev():
    centre = (LAM_HIGH + LAM_LOW) / 2.0
    radius = (LAM_HIGH - LAM_LOW) / 2.0
    ratio = centre / radius
    rho = 1.0 / ratio
    pairs = []
    for _ in range(2):
        following = 1.0 / (2.0 * ratio - rho)
        pairs.append((following * rho, 2.0 * following / radius))
        rho = following
    return 1.0 / centre, pairs


def rows(shape):
    return lax.broadcasted_iota(jnp.int32, shape, len(shape) - 2)


def lanes(shape):
    return lax.broadcasted_iota(jnp.int32, shape, len(shape) - 1)


def turn(v, shift):
    return pltpu.roll(v, shift, v.ndim - 2)


def pack_x_up(p, q):
    return jnp.where(rows(p.shape) < 4, turn(p, 4), q)


def pack_x_down(p, q):
    return jnp.where(rows(p.shape) < 4, p, turn(q, 4))


def prev_x(p, q, g):
    low = rows(p.shape) < 4
    return jnp.where(low, g, turn(p, 4)), turn(jnp.where(low, q, g), 4)


def next_x(p, q, g):
    low = rows(p.shape) < 4
    return turn(jnp.where(low, g, p), 4), jnp.where(low, turn(q, 4), g)


def halves(p):
    half = (p.shape[0] + 1) // 2
    if p.shape[0] == 1:
        return p, p
    high = p[half:]
    if p.shape[0] % 2:
        high = jnp.concatenate([high, p[half - 1:half]], axis=0)
    return p[:half], high


def pack_y_up(p, q):
    (p, p_high), (q, q_high) = halves(p), halves(q)
    r = rows(p.shape) & 3
    return jnp.where(r < 2, jnp.where(r == 0, turn(p, 5), turn(q, 6)), jnp.where(r == 2, turn(p_high, 7), q_high))


def pack_y_down(p, q):
    (p, p_high), (q, q_high) = halves(p), halves(q)
    r = rows(p.shape) & 3
    return jnp.where(r < 2, jnp.where(r == 1, turn(p_high, 1), q_high), jnp.where(r == 3, turn(p, 3), turn(q, 2)))


def open_y(g, count, shifts):
    def both(low, high):
        first = turn(g, low) if low else g
        if count == 1:
            return first
        return jnp.concatenate([first, turn(g, high)[:count - g.shape[0]]], axis=0)
    return both(shifts[0], shifts[1]), both(shifts[2], shifts[3])


def prev_y(p, q, g):
    edge = (rows(p.shape) & 3) == 0
    g = open_y(g, p.shape[0], (0, 6, 7, 5))
    return jnp.where(edge, g[0], turn(p, 1)), jnp.where(edge, g[1], turn(q, 1))


def next_y(p, q, g):
    edge = (rows(p.shape) & 3) == 3
    g = open_y(g, p.shape[0], (0, 2, 1, 3))
    return jnp.where(edge, g[0], turn(p, 7)), jnp.where(edge, g[1], turn(q, 7))


def prev_z(p):
    return jnp.where(lanes(p.shape) == 0, 0.0, pltpu.roll(p, 1, p.ndim - 1))


def next_z(p):
    end = p.shape[-1] - 1
    return jnp.where(lanes(p.shape) == end, 0.0, pltpu.roll(p, end, p.ndim - 1))


def line(u, half_coef):
    t4 = u[4] + u[6]
    t2 = u[2] + t4
    even = u[0] + t2
    t3 = u[3] + u[5]
    odd = u[1] + t3
    s2 = 6.0 * t2
    s4 = s2 + 14.0 * t4
    s6 = s4 + 22.0 * u[6]
    s1 = 2.0 * odd
    s3 = s1 + 10.0 * t3
    s5 = s3 + 18.0 * u[5]
    tp = even + odd
    tm = even - odd
    fp = half_coef * (s6 + s5)
    fm = half_coef * (s5 - s6)
    return (tp, tm, fp, fm), (None, s1, s2, s3, s4, s5, s6)


def spread(traces, before, after, geom, coef, sums, count):
    tp, tm, fp, fm = traces
    tau_a, tau_b, w_a, w_b, k_a, k_b = geom
    jump_a = tp - after[0]
    g_a = tau_a * jump_a - w_a * (fp + after[1])
    jump_b = before[0] - tm
    g_b = tau_b * jump_b - w_b * (before[1] + fm)
    kl = k_a * jump_a
    kr = k_b * jump_b
    p = (g_a - g_b, g_a + g_b)
    q = (kl - kr, kl + kr)
    out = [HALF[0] * p[0]]
    for n in range(1, count):
        out.append(HALF[n] * (coef * sums[n] + (p[n % 2] - SLOPE[n] * q[n % 2])))
    return out


def kernel(nx, ny, rhs_hbm, coef_hbm, deg_hbm, u, coarse, s, coef, deg, inv, step, acc, geo, dia, ym,
           ps, pg, xs, xg, ys, yg, xs3, xg3, ys3, yg3, kept, folds, folded, order,
           in_sem, p_send, p_recv, x_send, x_recv, y_send, y_recv, l_send, l_recv, f_send, f_recv):
    loads = [pltpu.make_async_copy(a, b, in_sem.at[i])
             for i, (a, b) in enumerate(((coef_hbm, coef), (deg_hbm, deg), (rhs_hbm, s)))]
    for load in loads:
        load.start()
    gx, gy = lax.axis_index("gx"), lax.axis_index("gy")
    exists = (gx < nx - 1, gx > 0, gy < ny - 1, gy > 0)
    target = ({"gx": gx + 1}, {"gx": gx - 1}, {"gy": gy + 1}, {"gy": gy - 1})
    source = (exists[1], exists[0], exists[3], exists[2])

    barrier = pltpu.get_barrier_semaphore()
    near = ny <= 4
    for d in range(4 if near else 2):
        @pl.when(exists[d])
        def _(d=d):
            pl.semaphore_signal(barrier, inc=1, device_id=target[d], device_id_type=MESH)
    for d in range(0 if near else ny):
        @pl.when(gy != d)
        def _(d=d):
            pl.semaphore_signal(barrier, inc=1, device_id={"gy": d}, device_id_type=MESH)
    greeted = sum(e.astype(jnp.int32) for e in (exists if near else exists[:2])) + (0 if near else ny - 1)

    def copy(src, dst, send, recv, d):
        return pltpu.make_async_remote_copy(src_ref=src, dst_ref=dst, send_sem=send, recv_sem=recv,
                                            device_id=target[d], device_id_type=MESH)

    def param_copy(d):
        return copy(ps.at[d], pg.at[d], p_send.at[d], p_recv.at[d], d)

    def x_copy(k, d, b, width=MODES):
        if k < 2:
            part = pl.ds(0, width)
            return copy(xs.at[k, d, b, part], xg.at[k, d, b, part], x_send.at[k, d, b], x_recv.at[k, d, b], d)
        return copy(xs3.at[d, b], xg3.at[d, b], x_send.at[k, d, b], x_recv.at[k, d, b], d)

    def y_copy(k, d, a):
        if k < 2:
            return copy(ys.at[k, d, a], yg.at[k, d, a], y_send.at[k, d, a], y_recv.at[k, d, a], 2 + d)
        return copy(ys3.at[d, a], yg3.at[d, a], y_send.at[k, d, a], y_recv.at[k, d, a], 2 + d)

    def late_copy(d):
        part = (1, d, pl.ds(CMODES, MODES - CMODES), pl.ds(CMODES, MODES - CMODES))
        return copy(xs.at[part], xg.at[part], l_send.at[d], l_recv.at[d], d)

    loads[0].wait()
    loads[1].wait()
    c = coef[...]
    half_coef = 0.5 * c
    depth = 128 // ny
    df = [deg[d].astype(F32) for d in range(3)]
    ps[0] = pack_x_up(c, df[0])
    ps[1] = pack_x_down(c, df[0])
    ps[2] = pack_y_up(c[None], df[1][None])[0]
    ps[3] = pack_y_down(c[None], df[1][None])[0]
    pl.semaphore_wait(barrier, greeted)
    for d in range(4):
        @pl.when(exists[d])
        def _(d=d):
            param_copy(d).start()

    for d in range(4):
        @pl.when(jnp.logical_not(source[d]))
        def _(d=d):
            pg[d] = jnp.zeros((8, 128), F32)
            ghosts = (xg, yg)[d // 2]
            ghosts3 = (xg3, yg3)[d // 2]

            def clear(i, _):
                for k in range(2):
                    ghosts[k, d % 2, i] = jnp.zeros(ghosts.shape[3:], F32)
                return 0
            lax.fori_loop(0, MODES, clear, 0)

            def clear3(i, _):
                ghosts3[d % 2, i] = jnp.zeros(ghosts3.shape[2:], F32)
                return 0
            lax.fori_loop(0, CMODES, clear3, 0)

    shape = (MODES, 8, 128)
    levels = lax.broadcasted_iota(jnp.int32, shape, 0)
    ym[...] = jnp.where(levels <= deg[1][None], 1.0, 0.0)

    def prepare(direction, before, after, first, last):
        degree = df[direction]
        wide_a = jnp.maximum(degree, after[1])
        wide_b = jnp.maximum(degree, before[1])
        tau_a = jnp.maximum(c, after[0]) * (wide_a + 1.0) * (wide_a + 2.0)
        tau_b = jnp.maximum(c, before[0]) * (wide_b + 1.0) * (wide_b + 2.0)
        w_a = jnp.where(last, 1.0, 0.5)
        w_b = jnp.where(first, 1.0, 0.5)
        for i, value in enumerate((tau_a, tau_b, w_a, w_b, w_a * c, w_b * c)):
            geo[direction, i] = value
        rest = (1.0 - (w_a + w_b)) * c
        for n in range(MODES):
            dia[direction, n] = HALF[n] * (tau_a + tau_b + (2.0 * SLOPE[n]) * rest)

    row, lane = rows((8, 128)), lanes((8, 128))
    prepare(2, (prev_z(c), prev_z(df[2])), (next_z(c), next_z(df[2])), lane == 0, lane == 127)
    odd = gx % 2

    def params(d, want):
        @pl.when(want)
        def _():
            param_copy(d).wait_recv()

    params(2, source[2])
    params(3, source[3])
    params(0, source[0] & (odd == 1))
    params(1, source[1] & (odd == 0))
    px, py = gx * 2 + (row >> 2), gy * 4 + (row & 3)

    def prepare_x(low, high):
        prepare(0, prev_x(c, df[0], low), next_x(c, df[0], high), px == 0, px == 2 * nx - 1)

    before, after = prev_y(c[None], df[1][None], pg[2:3]), next_y(c[None], df[1][None], pg[3:4])
    prepare(1, [v[0] for v in before], [v[0] for v in after], py == 0, py == 4 * ny - 1)
    beside = pg[1 - odd]
    prepare_x(beside, beside)

    first_scale, pairs = chebyshev()
    odds = 2.0 * levels.astype(F32) + 1.0

    def geom(direction):
        return tuple(geo[direction, i][None] for i in range(6))

    def start(make, k, at, base):
        for d in range(2):
            @pl.when(exists[base + d])
            def _(d=d):
                make(k, d, at).start()

    def arrive(make, k, at, base):
        for d in range(2):
            @pl.when(source[base + d])
            def _(d=d):
                make(k, d, at).wait_recv()

    def send(k, g, values, width=MODES, begun=False):
        count = values[0].shape[0]
        (tp, tm, fp, fm), _ = line(values, half_coef[None])
        up, down = pack_x_up(tp, fp), pack_x_down(tm, fm)
        if begun:
            xs[k, 1 - odd, g] = jnp.where(odd == 0, down, up)
            start_side(k, g, 1 - odd)
        elif k < 2:
            xs[k, 0, g] = up
            xs[k, 1, g] = down
        else:
            xs3[0, g] = up
            xs3[1, g] = down
        if not begun:
            start(functools.partial(x_copy, width=width), k, g, 0)
        (tp, tm, fp, fm), _ = line([u[0:count, n, g] for n in range(MODES)], half_coef[None])
        up, down = pack_y_up(tp, fp), pack_y_down(tm, fm)
        if k < 2:
            ys[k, 0, g] = up
            ys[k, 1, g] = down
        else:
            ys3[0, g] = up
            ys3[1, g] = down
        start(y_copy, k, g, 2)

    def start_side(k, g, side):
        for d in range(2):
            @pl.when(exists[d] & (side == d))
            def _(d=d):
                x_copy(k, d, g).start()

    loads[2].wait()

    def first(g):
        inside = ym[...] * jnp.where(deg[2] >= g, 1.0, 0.0)[None]
        across = dia[1] + dia[2, g][None]
        scale = odds * ((2.0 * g.astype(F32) + 1.0) / 8.0)
        for a in range(MODES):
            i = jnp.where(deg[0] >= a, 1.0, 0.0)[None] * inside / (dia[0, a][None] + across)
            r = s[a, :, g] * (scale * (2.0 * a + 1.0))
            yield i, r, i * r * first_scale

    def begin(g, _):
        (tp, tm, fp, fm), _ = line([x for _, _, x in first(g)], half_coef[None])
        xs[0, odd, g] = jnp.where(odd == 0, pack_x_up(tp, fp), pack_x_down(tm, fm))
        start_side(0, g, odd)
        return 0
    lax.fori_loop(0, EARLY, begin, 0)

    params(0, source[0] & (odd == 0))
    params(1, source[1] & (odd == 1))
    prepare_x(pg[0], pg[1])

    def setup(g, _, begun=False):
        fresh = []
        for a, (i, r, x) in enumerate(first(g)):
            s[a, :, g] = r
            inv[a, :, g] = i
            u[a, :, g] = x
            fresh.append(x)
        send(0, g, fresh, begun=begun)
        return 0
    lax.fori_loop(0, EARLY, functools.partial(setup, begun=True), 0)
    lax.fori_loop(EARLY, MODES, setup, 0)

    def fold_copy(d, b):
        return pltpu.make_async_remote_copy(
            src_ref=folds.at[d, b], dst_ref=folded.at[gy, b], send_sem=f_send.at[d, b],
            recv_sem=f_recv.at[gy, b], device_id={"gy": d}, device_id_type=MESH)

    def fold_arrival(d, b):
        return pltpu.make_async_remote_copy(
            src_ref=folds.at[d, b], dst_ref=folded.at[d, b], send_sem=f_send.at[d, b],
            recv_sem=f_recv.at[d, b], device_id={"gy": d}, device_id_type=MESH)

    def fold(b):
        block = lanes((CMODES**2, 128)) // depth
        for x in range(2):
            by_y = [kept[b, pl.ds(x * 4 + y, CMODES**2, stride=8), :] for y in range(4)]
            for d in range(ny):
                out = jnp.zeros((CMODES**2, 128), F32)
                for y in range(4):
                    shift = ((y - d) * depth) % 128
                    out = jnp.where(block == y, pltpu.roll(by_y[y], shift, 1) if shift else by_y[y], out)
                folds[d, b, x] = out
        for d in range(ny):
            @pl.when(gy // 2 != d // 2)
            def _(d=d):
                fold_copy(d, b).start()
        for d in range(ny):
            @pl.when((gy // 2 == d // 2) & (gy != d))
            def _(d=d):
                fold_copy(d, b).start()

            @pl.when(gy == d)
            def _(d=d):
                folded[d, b] = folds[d, b]

    def x_terms(values, g_prev, g_next, count):
        traces, sums = line(values, half_coef[None])
        tp, tm, fp, fm = traces
        return spread(traces, prev_x(tp, fp, g_prev), next_x(tm, fm, g_next), geom(0), c[None], sums, count)

    def update(k, g, low, high):
        values = [u[n, low:high, g] for n in range(MODES)]
        out = x_terms(values, xg[k, 0, g, low:high], xg[k, 1, g, low:high], MODES)
        fresh = []
        for n in range(MODES):
            residual = s[n, low:high, g] - (acc[n, low:high, g] + out[n])
            last = values[n] if k < 1 else step[n, low:high, g]
            change = pairs[k][0] * last + pairs[k][1] * (inv[n, low:high, g] * residual)
            moved = values[n] + change
            if k < 1:
                step[n, low:high, g] = change
            u[n, low:high, g] = moved
            fresh.append(moved)
        return fresh

    source_lane = lax.broadcasted_iota(jnp.int32, (128, 512), 0)
    fine_lane = lax.broadcasted_iota(jnp.int32, (128, 512), 1)
    spot = (source_lane % depth) * (4 * ny) + source_lane // depth
    for d in range(ny):
        order[d * 128:(d + 1) * 128] = jnp.where(
            (source_lane < 4 * depth) & (fine_lane == spot + 4 * d), 1.0, 0.0).astype(jnp.bfloat16)

    for k in range(3):
        count = MODES if k < 2 else CMODES

        def pass_z(a, _):
            traces, sums = line([u[a, 0:count, n] for n in range(MODES)], half_coef[None])
            tp, tm, fp, fm = traces
            out = spread(traces, (prev_z(tp), prev_z(fp)), (next_z(tm), next_z(fm)),
                         geom(2), c[None], sums, count)
            for n in range(count):
                acc[a, 0:count, n] = out[n]
            return 0
        lax.fori_loop(0, count, pass_z, 0)

        def pass_xy(g, _, following=False, coarse_only=False, last=False):
            arrive(y_copy, k, g, 2)
            traces, sums = line([u[0:count, n, g] for n in range(MODES)], half_coef[None])
            tp, tm, fp, fm = traces
            g_prev = yg[k, 0, g] if k < 2 else yg3[0, g]
            g_next = yg[k, 1, g] if k < 2 else yg3[1, g]
            out = spread(traces, prev_y(tp, fp, g_prev), next_y(tm, fm, g_next),
                         geom(1), c[None], sums, count)
            for n in range(count):
                acc[0:count, n, g] += out[n]

            if k < 2:
                width = CMODES if coarse_only else MODES
                arrive(functools.partial(x_copy, width=width), k, g, 0)
                fresh = update(k, g, 0, width)
                if following:
                    keep = MODES if k < 1 else CMODES
                    send(k + 1, g, [v[0:keep] for v in fresh], CMODES if last else MODES)
            else:
                arrive(x_copy, k, g, 0)
                out = x_terms([u[n, 0:count, g] for n in range(MODES)], xg3[0, g], xg3[1, g], count)
                low = lax.broadcasted_iota(jnp.int32, (CMODES, 8, 128), 0)
                inside_y = jnp.where(low <= (deg[1] >> 1)[None], 1.0, 0.0)
                inside_z = jnp.where((deg[2] >> 1) >= g, 1.0, 0.0)
                mass = (1.0 / ((2.0 * low.astype(F32) + 1.0) * (2.0 * g.astype(F32) + 1.0))) * (
                    inside_y * inside_z[None])
                for n in range(CMODES):
                    inside = jnp.where((deg[0] >> 1) >= n, 8.0 / (2.0 * n + 1.0), 0.0)
                    residual = s[n, 0:CMODES, g] - (acc[n, 0:CMODES, g] + out[n])
                    kept[g, n * 32:(n + 1) * 32] = (residual * (mass * inside[None])).reshape(32, 128)
                fold(g)
            return 0
        if k == 0:
            lax.fori_loop(0, CMODES, functools.partial(pass_xy, following=True), 0)
            lax.fori_loop(CMODES, MODES, functools.partial(pass_xy, following=True, last=True), 0)
        elif k == 1:
            lax.fori_loop(0, CMODES, functools.partial(pass_xy, following=True), 0)
            lax.fori_loop(CMODES, MODES, functools.partial(pass_xy, coarse_only=True), 0)
            for d in range(2):
                @pl.when(exists[d])
                def _(d=d):
                    late_copy(d).start()
        else:
            lax.fori_loop(0, CMODES, pass_xy, 0)

    def gather(g, _):
        for d in range(ny):
            @pl.when(gy != d)
            def _(d=d):
                fold_copy(d, g).wait_send()
                fold_arrival(d, g).wait_recv()
        pieces = []
        rest = jnp.concatenate([folded[d, g].reshape(2 * CMODES**2, 128) for d in range(ny)], axis=1)
        for part in range(3):
            pieces.append(rest.astype(jnp.bfloat16))
            if part < 2:
                rest = rest - pieces[-1].astype(F32)
        total = jnp.dot(jnp.concatenate(pieces, axis=0), order[...], preferred_element_type=F32)
        total = total[0:32] + total[32:64] + total[64:96]
        for x in range(2):
            for a in range(CMODES):
                for j in range(4):
                    coarse[pl.ds((a * 16 + g) * 8 + j * 2 + x, CMODES, stride=32), :] = total[
                        x * 16 + a * 4:x * 16 + a * 4 + 4, j * 128:(j + 1) * 128]
        return 0
    for d in range(4):
        @pl.when(exists[d])
        def _(d=d):
            param_copy(d).wait_send()
            make = (x_copy, y_copy)[d // 2]
            for k in range(3):
                def sent(i, _, make=make):
                    make(k, d % 2, i).wait_send()
                    return 0
                if d < 2 and k == 1:
                    lax.fori_loop(0, CMODES, sent, 0)
                    lax.fori_loop(CMODES, MODES, functools.partial(
                        sent, make=functools.partial(x_copy, width=CMODES)), 0)
                else:
                    lax.fori_loop(0, MODES if k < 2 else CMODES, sent, 0)
    lax.fori_loop(0, 2, gather, 0)
    for d in range(2):
        @pl.when(source[d])
        def _(d=d):
            late_copy(d).wait_recv()

    def pass_late(g, _):
        update(1, g, CMODES, MODES)
        return 0
    lax.fori_loop(CMODES, MODES, pass_late, 0)

    for d in range(2):
        @pl.when(exists[d])
        def _(d=d):
            late_copy(d).wait_send()
    lax.fori_loop(2, CMODES, gather, 0)


def smoother(nx, ny, rhs, coef, deg):
    field = pltpu.VMEM((MODES, MODES, MODES, 8, 128), F32)
    wide = pltpu.VMEM((2, 2, MODES, MODES, 8, 128), F32)
    narrow = pltpu.VMEM((2, CMODES, CMODES, 8, 128), F32)
    wide_half = pltpu.VMEM((2, 2, MODES, (MODES + 1) // 2, 8, 128), F32)
    narrow_half = pltpu.VMEM((2, CMODES, CMODES // 2, 8, 128), F32)
    return pl.pallas_call(
        functools.partial(kernel, nx, ny),
        out_shape=(jax.ShapeDtypeStruct((MODES, MODES, MODES, 8, 128), F32),
                   jax.ShapeDtypeStruct((CMODES**3 * 8, 128), F32)),
        in_specs=[pl.BlockSpec(memory_space=pltpu.HBM)] * 3,
        out_specs=[pl.BlockSpec(memory_space=pltpu.VMEM)] * 2,
        scratch_shapes=[
            field,
            pltpu.VMEM((8, 128), F32),
            pltpu.VMEM((3, 8, 128), jnp.int32),
            field, field, field,
            pltpu.VMEM((3, 6, 8, 128), F32),
            pltpu.VMEM((3, MODES, 8, 128), F32),
            pltpu.VMEM((MODES, 8, 128), F32),
            pltpu.VMEM((4, 8, 128), F32),
            pltpu.VMEM((4, 8, 128), F32),
            wide, wide, wide_half, wide_half, narrow, narrow, narrow_half, narrow_half,
            pltpu.VMEM((CMODES, 128, 128), F32),
            pltpu.VMEM((ny, CMODES, 2, CMODES**2, 128), F32),
            pltpu.VMEM((ny, CMODES, 2, CMODES**2, 128), F32),
            pltpu.VMEM((ny * 128, 512), jnp.bfloat16),
            pltpu.SemaphoreType.DMA((3,)),
            pltpu.SemaphoreType.DMA((4,)),
            pltpu.SemaphoreType.DMA((4,)),
            pltpu.SemaphoreType.DMA((3, 2, MODES)),
            pltpu.SemaphoreType.DMA((3, 2, MODES)),
            pltpu.SemaphoreType.DMA((3, 2, MODES)),
            pltpu.SemaphoreType.DMA((3, 2, MODES)),
            pltpu.SemaphoreType.DMA((2,)),
            pltpu.SemaphoreType.DMA((2,)),
            pltpu.SemaphoreType.DMA((ny, CMODES)),
            pltpu.SemaphoreType.DMA((ny, CMODES)),
        ],
        compiler_params=pltpu.CompilerParams(
            collective_id=0, has_side_effects=True, vmem_limit_bytes=48 * 1024 * 1024
        ),
    )(*(pltpu.with_memory_space_constraint(v, pltpu.HBM) for v in (rhs, coef, deg)))


def finish_kernel(u, blocks, stored, coarse, sem):
    copies = [pltpu.make_async_copy(a, b, sem.at[i]) for i, (a, b) in enumerate(((u, stored), (blocks, coarse)))]
    for copy in copies:
        copy.start()
    for copy in copies:
        copy.wait()


def finish(u, blocks):
    return pl.pallas_call(
        finish_kernel,
        out_shape=(jax.ShapeDtypeStruct(u.shape, F32), jax.ShapeDtypeStruct(blocks.shape, F32)),
        in_specs=[pl.BlockSpec(memory_space=pl.ANY)] * 2,
        out_specs=[pl.BlockSpec(memory_space=pltpu.HBM)] * 2,
        scratch_shapes=[pltpu.SemaphoreType.DMA((2,))],
        compiler_params=pltpu.CompilerParams(vmem_limit_bytes=16 * 1024 * 1024),
    )(u, blocks)


def solution(mesh):
    nx, ny = mesh.shape["gx"], mesh.shape["gy"]

    def body(right_side, coefficient, degrees):
        local = right_side.shape[3:]
        flat = (local[0] * local[1], local[2])
        smoothed, blocks = smoother(
            nx, ny,
            right_side.reshape(right_side.shape[:3] + flat),
            coefficient.reshape(flat),
            degrees.reshape((3,) + flat),
        )
        smoothed, coarse = finish(smoothed, blocks)
        coarse = jnp.transpose(coarse.reshape(CMODES**3, 4, 2, 128), (0, 2, 1, 3))
        return smoothed.reshape(right_side.shape), coarse.reshape(CMODES**3, 2, 512)

    in_specs = (
        P(None, None, None, "gx", "gy", None),
        P("gx", "gy", None),
        P(None, "gx", "gy", None),
    )
    out_specs = (P(None, None, None, "gx", "gy", None), P(None, "gx", "gy"))
    return jax.shard_map(body, mesh=mesh, in_specs=in_specs, out_specs=out_specs, check_vma=False)
```

```python
import functools

import jax
import jax.numpy as jnp
from jax import lax
from jax.experimental import pallas as pl
from jax.experimental.pallas import tpu as pltpu
from jax.sharding import PartitionSpec as P

CMODES = 4
LAM_HIGH = 6.0
LAM_LOW = 0.5
MODES = 7
EARLY = 2
MESH = pl.DeviceIdType.MESH
F32 = jnp.float32
HALF = [(2.0 * n + 1.0) / 2.0 for n in range(MODES)]
SLOPE = [n * (n + 1.0) / 2.0 for n in range(MODES)]


def chebyshev():
    centre = (LAM_HIGH + LAM_LOW) / 2.0
    radius = (LAM_HIGH - LAM_LOW) / 2.0
    ratio = centre / radius
    rho = 1.0 / ratio
    pairs = []
    for _ in range(2):
        following = 1.0 / (2.0 * ratio - rho)
        pairs.append((following * rho, 2.0 * following / radius))
        rho = following
    return 1.0 / centre, pairs


def rows(shape):
    return lax.broadcasted_iota(jnp.int32, shape, len(shape) - 2)


def lanes(shape):
    return lax.broadcasted_iota(jnp.int32, shape, len(shape) - 1)


def turn(v, shift):
    return pltpu.roll(v, shift, v.ndim - 2)


def pack_x_up(p, q):
    return jnp.where(rows(p.shape) < 4, turn(p, 4), q)


def pack_x_down(p, q):
    return jnp.where(rows(p.shape) < 4, p, turn(q, 4))


def prev_x(p, q, g):
    low = rows(p.shape) < 4
    return jnp.where(low, g, turn(p, 4)), turn(jnp.where(low, q, g), 4)


def next_x(p, q, g):
    low = rows(p.shape) < 4
    return turn(jnp.where(low, g, p), 4), jnp.where(low, turn(q, 4), g)


def halves(p):
    half = (p.shape[0] + 1) // 2
    if p.shape[0] == 1:
        return p, p
    high = p[half:]
    if p.shape[0] % 2:
        high = jnp.concatenate([high, p[half - 1:half]], axis=0)
    return p[:half], high


def pack_y_up(p, q):
    (p, p_high), (q, q_high) = halves(p), halves(q)
    r = rows(p.shape) & 3
    return jnp.where(r < 2, jnp.where(r == 0, turn(p, 5), turn(q, 6)), jnp.where(r == 2, turn(p_high, 7), q_high))


def pack_y_down(p, q):
    (p, p_high), (q, q_high) = halves(p), halves(q)
    r = rows(p.shape) & 3
    return jnp.where(r < 2, jnp.where(r == 1, turn(p_high, 1), q_high), jnp.where(r == 3, turn(p, 3), turn(q, 2)))


def open_y(g, count, shifts):
    def both(low, high):
        first = turn(g, low) if low else g
        if count == 1:
            return first
        return jnp.concatenate([first, turn(g, high)[:count - g.shape[0]]], axis=0)
    return both(shifts[0], shifts[1]), both(shifts[2], shifts[3])


def prev_y(p, q, g):
    edge = (rows(p.shape) & 3) == 0
    g = open_y(g, p.shape[0], (0, 6, 7, 5))
    return jnp.where(edge, g[0], turn(p, 1)), jnp.where(edge, g[1], turn(q, 1))


def next_y(p, q, g):
    edge = (rows(p.shape) & 3) == 3
    g = open_y(g, p.shape[0], (0, 2, 1, 3))
    return jnp.where(edge, g[0], turn(p, 7)), jnp.where(edge, g[1], turn(q, 7))


def prev_z(p):
    return jnp.where(lanes(p.shape) == 0, 0.0, pltpu.roll(p, 1, p.ndim - 1))


def next_z(p):
    end = p.shape[-1] - 1
    return jnp.where(lanes(p.shape) == end, 0.0, pltpu.roll(p, end, p.ndim - 1))


def line(u, half_coef):
    t4 = u[4] + u[6]
    t2 = u[2] + t4
    even = u[0] + t2
    t3 = u[3] + u[5]
    odd = u[1] + t3
    s2 = 6.0 * t2
    s4 = s2 + 14.0 * t4
    s6 = s4 + 22.0 * u[6]
    s1 = 2.0 * odd
    s3 = s1 + 10.0 * t3
    s5 = s3 + 18.0 * u[5]
    tp = even + odd
    tm = even - odd
    fp = half_coef * (s6 + s5)
    fm = half_coef * (s5 - s6)
    return (tp, tm, fp, fm), (None, s1, s2, s3, s4, s5, s6)


def spread(traces, before, after, geom, coef, sums, count):
    tp, tm, fp, fm = traces
    tau_a, tau_b, w_a, w_b, k_a, k_b = geom
    jump_a = tp - after[0]
    g_a = tau_a * jump_a - w_a * (fp + after[1])
    jump_b = before[0] - tm
    g_b = tau_b * jump_b - w_b * (before[1] + fm)
    kl = k_a * jump_a
    kr = k_b * jump_b
    p = (g_a - g_b, g_a + g_b)
    q = (kl - kr, kl + kr)
    out = [HALF[0] * p[0]]
    for n in range(1, count):
        out.append(HALF[n] * (coef * sums[n] + (p[n % 2] - SLOPE[n] * q[n % 2])))
    return out


def kernel(nx, ny, rhs_hbm, coef_hbm, deg_hbm, u, coarse, s, coef, deg, inv, step, acc, geo, dia, ym,
           ps, pg, xs, xg, ys, yg, xs3, xg3, ys3, yg3, kept, folds, folded, order,
           in_sem, p_send, p_recv, x_send, x_recv, y_send, y_recv, l_send, l_recv, f_send, f_recv):
    loads = [pltpu.make_async_copy(a, b, in_sem.at[i])
             for i, (a, b) in enumerate(((coef_hbm, coef), (deg_hbm, deg), (rhs_hbm, s)))]
    for load in loads:
        load.start()
    gx, gy = lax.axis_index("gx"), lax.axis_index("gy")
    exists = (gx < nx - 1, gx > 0, gy < ny - 1, gy > 0)
    target = ({"gx": gx + 1}, {"gx": gx - 1}, {"gy": gy + 1}, {"gy": gy - 1})
    source = (exists[1], exists[0], exists[3], exists[2])

    barrier = pltpu.get_barrier_semaphore()
    near = ny <= 4
    for d in range(4 if near else 2):
        @pl.when(exists[d])
        def _(d=d):
            pl.semaphore_signal(barrier, inc=1, device_id=target[d], device_id_type=MESH)
    for d in range(0 if near else ny):
        @pl.when(gy != d)
        def _(d=d):
            pl.semaphore_signal(barrier, inc=1, device_id={"gy": d}, device_id_type=MESH)
    greeted = sum(e.astype(jnp.int32) for e in (exists if near else exists[:2])) + (0 if near else ny - 1)

    def copy(src, dst, send, recv, d):
        return pltpu.make_async_remote_copy(src_ref=src, dst_ref=dst, send_sem=send, recv_sem=recv,
                                            device_id=target[d], device_id_type=MESH)

    def param_copy(d):
        return copy(ps.at[d], pg.at[d], p_send.at[d], p_recv.at[d], d)

    def x_copy(k, d, b, width=MODES):
        if k < 2:
            part = pl.ds(0, width)
            return copy(xs.at[k, d, b, part], xg.at[k, d, b, part], x_send.at[k, d, b], x_recv.at[k, d, b], d)
        return copy(xs3.at[d, b], xg3.at[d, b], x_send.at[k, d, b], x_recv.at[k, d, b], d)

    def y_copy(k, d, a):
        if k < 2:
            return copy(ys.at[k, d, a], yg.at[k, d, a], y_send.at[k, d, a], y_recv.at[k, d, a], 2 + d)
        return copy(ys3.at[d, a], yg3.at[d, a], y_send.at[k, d, a], y_recv.at[k, d, a], 2 + d)

    def late_copy(d):
        part = (1, d, pl.ds(CMODES, MODES - CMODES), pl.ds(CMODES, MODES - CMODES))
        return copy(xs.at[part], xg.at[part], l_send.at[d], l_recv.at[d], d)

    loads[0].wait()
    loads[1].wait()
    c = coef[...]
    half_coef = 0.5 * c
    depth = 128 // ny
    df = [deg[d].astype(F32) for d in range(3)]
    ps[0] = pack_x_up(c, df[0])
    ps[1] = pack_x_down(c, df[0])
    ps[2] = pack_y_up(c[None], df[1][None])[0]
    ps[3] = pack_y_down(c[None], df[1][None])[0]
    pl.semaphore_wait(barrier, greeted)
    for d in range(4):
        @pl.when(exists[d])
        def _(d=d):
            param_copy(d).start()

    for d in range(4):
        @pl.when(jnp.logical_not(source[d]))
        def _(d=d):
            pg[d] = jnp.zeros((8, 128), F32)
            ghosts = (xg, yg)[d // 2]
            ghosts3 = (xg3, yg3)[d // 2]

            def clear(i, _):
                for k in range(2):
                    ghosts[k, d % 2, i] = jnp.zeros(ghosts.shape[3:], F32)
                return 0
            lax.fori_loop(0, MODES, clear, 0)

            def clear3(i, _):
                ghosts3[d % 2, i] = jnp.zeros(ghosts3.shape[2:], F32)
                return 0
            lax.fori_loop(0, CMODES, clear3, 0)

    shape = (MODES, 8, 128)
    levels = lax.broadcasted_iota(jnp.int32, shape, 0)
    ym[...] = jnp.where(levels <= deg[1][None], 1.0, 0.0)

    def prepare(direction, before, after, first, last):
        degree = df[direction]
        wide_a = jnp.maximum(degree, after[1])
        wide_b = jnp.maximum(degree, before[1])
        tau_a = jnp.maximum(c, after[0]) * (wide_a + 1.0) * (wide_a + 2.0)
        tau_b = jnp.maximum(c, before[0]) * (wide_b + 1.0) * (wide_b + 2.0)
        w_a = jnp.where(last, 1.0, 0.5)
        w_b = jnp.where(first, 1.0, 0.5)
        for i, value in enumerate((tau_a, tau_b, w_a, w_b, w_a * c, w_b * c)):
            geo[direction, i] = value
        rest = (1.0 - (w_a + w_b)) * c
        for n in range(MODES):
            dia[direction, n] = HALF[n] * (tau_a + tau_b + (2.0 * SLOPE[n]) * rest)

    row, lane = rows((8, 128)), lanes((8, 128))
    prepare(2, (prev_z(c), prev_z(df[2])), (next_z(c), next_z(df[2])), lane == 0, lane == 127)
    odd = gx % 2

    def params(d, want):
        @pl.when(want)
        def _():
            param_copy(d).wait_recv()

    params(2, source[2])
    params(3, source[3])
    params(0, source[0] & (odd == 1))
    params(1, source[1] & (odd == 0))
    px, py = gx * 2 + (row >> 2), gy * 4 + (row & 3)

    def prepare_x(low, high):
        prepare(0, prev_x(c, df[0], low), next_x(c, df[0], high), px == 0, px == 2 * nx - 1)

    before, after = prev_y(c[None], df[1][None], pg[2:3]), next_y(c[None], df[1][None], pg[3:4])
    prepare(1, [v[0] for v in before], [v[0] for v in after], py == 0, py == 4 * ny - 1)
    beside = pg[1 - odd]
    prepare_x(beside, beside)

    first_scale, pairs = chebyshev()
    odds = 2.0 * levels.astype(F32) + 1.0

    def geom(direction):
        return tuple(geo[direction, i][None] for i in range(6))

    def start(make, k, at, base):
        for d in range(2):
            @pl.when(exists[base + d])
            def _(d=d):
                make(k, d, at).start()

    def arrive(make, k, at, base):
        for d in range(2):
            @pl.when(source[base + d])
            def _(d=d):
                make(k, d, at).wait_recv()

    def send(k, g, values, width=MODES, begun=False):
        count = values[0].shape[0]
        (tp, tm, fp, fm), _ = line(values, half_coef[None])
        up, down = pack_x_up(tp, fp), pack_x_down(tm, fm)
        if begun:
            xs[k, 1 - odd, g] = jnp.where(odd == 0, down, up)
            start_side(k, g, 1 - odd)
        elif k < 2:
            xs[k, 0, g] = up
            xs[k, 1, g] = down
        else:
            xs3[0, g] = up
            xs3[1, g] = down
        if not begun:
            start(functools.partial(x_copy, width=width), k, g, 0)
        (tp, tm, fp, fm), _ = line([u[0:count, n, g] for n in range(MODES)], half_coef[None])
        up, down = pack_y_up(tp, fp), pack_y_down(tm, fm)
        if k < 2:
            ys[k, 0, g] = up
            ys[k, 1, g] = down
        else:
            ys3[0, g] = up
            ys3[1, g] = down
        start(y_copy, k, g, 2)

    def start_side(k, g, side):
        for d in range(2):
            @pl.when(exists[d] & (side == d))
            def _(d=d):
                x_copy(k, d, g).start()

    loads[2].wait()

    def first(g):
        inside = ym[...] * jnp.where(deg[2] >= g, 1.0, 0.0)[None]
        across = dia[1] + dia[2, g][None]
        scale = odds * ((2.0 * g.astype(F32) + 1.0) / 8.0)
        for a in range(MODES):
            i = jnp.where(deg[0] >= a, 1.0, 0.0)[None] * inside / (dia[0, a][None] + across)
            r = s[a, :, g] * (scale * (2.0 * a + 1.0))
            yield i, r, i * r * first_scale

    def begin(g, _):
        (tp, tm, fp, fm), _ = line([x for _, _, x in first(g)], half_coef[None])
        xs[0, odd, g] = jnp.where(odd == 0, pack_x_up(tp, fp), pack_x_down(tm, fm))
        start_side(0, g, odd)
        return 0
    lax.fori_loop(0, EARLY, begin, 0)

    params(0, source[0] & (odd == 0))
    params(1, source[1] & (odd == 1))
    prepare_x(pg[0], pg[1])

    def setup(g, _, begun=False):
        fresh = []
        for a, (i, r, x) in enumerate(first(g)):
            s[a, :, g] = r
            inv[a, :, g] = i
            u[a, :, g] = x
            fresh.append(x)
        send(0, g, fresh, begun=begun)
        return 0
    lax.fori_loop(0, EARLY, functools.partial(setup, begun=True), 0)
    lax.fori_loop(EARLY, MODES, setup, 0)

    def fold_copy(d, b):
        return pltpu.make_async_remote_copy(
            src_ref=folds.at[d, b], dst_ref=folded.at[gy, b], send_sem=f_send.at[d, b],
            recv_sem=f_recv.at[gy, b], device_id={"gy": d}, device_id_type=MESH)

    def fold_arrival(d, b):
        return pltpu.make_async_remote_copy(
            src_ref=folds.at[d, b], dst_ref=folded.at[d, b], send_sem=f_send.at[d, b],
            recv_sem=f_recv.at[d, b], device_id={"gy": d}, device_id_type=MESH)

    def fold(b):
        block = lanes((CMODES**2, 128)) // depth
        for x in range(2):
            by_y = [kept[b, pl.ds(x * 4 + y, CMODES**2, stride=8), :] for y in range(4)]
            for d in range(ny):
                out = jnp.zeros((CMODES**2, 128), F32)
                for y in range(4):
                    shift = ((y - d) * depth) % 128
                    out = jnp.where(block == y, pltpu.roll(by_y[y], shift, 1) if shift else by_y[y], out)
                folds[d, b, x] = out
        for d in range(ny):
            @pl.when(gy // 2 != d // 2)
            def _(d=d):
                fold_copy(d, b).start()
        for d in range(ny):
            @pl.when((gy // 2 == d // 2) & (gy != d))
            def _(d=d):
                fold_copy(d, b).start()

            @pl.when(gy == d)
            def _(d=d):
                folded[d, b] = folds[d, b]

    def x_terms(values, g_prev, g_next, count):
        traces, sums = line(values, half_coef[None])
        tp, tm, fp, fm = traces
        return spread(traces, prev_x(tp, fp, g_prev), next_x(tm, fm, g_next), geom(0), c[None], sums, count)

    def update(k, g, low, high):
        values = [u[n, low:high, g] for n in range(MODES)]
        out = x_terms(values, xg[k, 0, g, low:high], xg[k, 1, g, low:high], MODES)
        fresh = []
        for n in range(MODES):
            residual = s[n, low:high, g] - (acc[n, low:high, g] + out[n])
            last = values[n] if k < 1 else step[n, low:high, g]
            change = pairs[k][0] * last + pairs[k][1] * (inv[n, low:high, g] * residual)
            moved = values[n] + change
            if k < 1:
                step[n, low:high, g] = change
            u[n, low:high, g] = moved
            fresh.append(moved)
        return fresh

    source_lane = lax.broadcasted_iota(jnp.int32, (128, 512), 0)
    fine_lane = lax.broadcasted_iota(jnp.int32, (128, 512), 1)
    spot = (source_lane % depth) * (4 * ny) + source_lane // depth
    for d in range(ny):
        order[d * 128:(d + 1) * 128] = jnp.where(
            (source_lane < 4 * depth) & (fine_lane == spot + 4 * d), 1.0, 0.0).astype(jnp.bfloat16)

    for k in range(3):
        count = MODES if k < 2 else CMODES

        def pass_z(a, _):
            traces, sums = line([u[a, 0:count, n] for n in range(MODES)], half_coef[None])
            tp, tm, fp, fm = traces
            out = spread(traces, (prev_z(tp), prev_z(fp)), (next_z(tm), next_z(fm)),
                         geom(2), c[None], sums, count)
            for n in range(count):
                acc[a, 0:count, n] = out[n]
            return 0
        lax.fori_loop(0, count, pass_z, 0)
        if k == 2:
            for d in range(2):
                @pl.when(exists[d])
                def _(d=d):
                    late_copy(d).start()

        def pass_xy(g, _, following=False, coarse_only=False, last=False):
            arrive(y_copy, k, g, 2)
            traces, sums = line([u[0:count, n, g] for n in range(MODES)], half_coef[None])
            tp, tm, fp, fm = traces
            g_prev = yg[k, 0, g] if k < 2 else yg3[0, g]
            g_next = yg[k, 1, g] if k < 2 else yg3[1, g]
            out = spread(traces, prev_y(tp, fp, g_prev), next_y(tm, fm, g_next),
                         geom(1), c[None], sums, count)
            for n in range(count):
                acc[0:count, n, g] += out[n]

            if k < 2:
                width = CMODES if coarse_only else MODES
                arrive(functools.partial(x_copy, width=width), k, g, 0)
                fresh = update(k, g, 0, width)
                if following:
                    keep = MODES if k < 1 else CMODES
                    send(k + 1, g, [v[0:keep] for v in fresh], CMODES if last else MODES)
            else:
                arrive(x_copy, k, g, 0)
                out = x_terms([u[n, 0:count, g] for n in range(MODES)], xg3[0, g], xg3[1, g], count)
                low = lax.broadcasted_iota(jnp.int32, (CMODES, 8, 128), 0)
                inside_y = jnp.where(low <= (deg[1] >> 1)[None], 1.0, 0.0)
                inside_z = jnp.where((deg[2] >> 1) >= g, 1.0, 0.0)
                mass = (1.0 / ((2.0 * low.astype(F32) + 1.0) * (2.0 * g.astype(F32) + 1.0))) * (
                    inside_y * inside_z[None])
                for n in range(CMODES):
                    inside = jnp.where((deg[0] >> 1) >= n, 8.0 / (2.0 * n + 1.0), 0.0)
                    residual = s[n, 0:CMODES, g] - (acc[n, 0:CMODES, g] + out[n])
                    kept[g, n * 32:(n + 1) * 32] = (residual * (mass * inside[None])).reshape(32, 128)
                fold(g)
            return 0
        if k == 0:
            lax.fori_loop(0, CMODES, functools.partial(pass_xy, following=True), 0)
            lax.fori_loop(CMODES, MODES, functools.partial(pass_xy, following=True, last=True), 0)
        elif k == 1:
            lax.fori_loop(0, CMODES, functools.partial(pass_xy, following=True), 0)
            lax.fori_loop(CMODES, MODES, functools.partial(pass_xy, coarse_only=True), 0)
        else:
            lax.fori_loop(0, CMODES, pass_xy, 0)

    def gather(g, _):
        for d in range(ny):
            @pl.when(gy != d)
            def _(d=d):
                fold_copy(d, g).wait_send()
                fold_arrival(d, g).wait_recv()
        pieces = []
        rest = jnp.concatenate([folded[d, g].reshape(2 * CMODES**2, 128) for d in range(ny)], axis=1)
        for part in range(3):
            pieces.append(rest.astype(jnp.bfloat16))
            if part < 2:
                rest = rest - pieces[-1].astype(F32)
        total = jnp.dot(jnp.concatenate(pieces, axis=0), order[...], preferred_element_type=F32)
        total = total[0:32] + total[32:64] + total[64:96]
        for x in range(2):
            for a in range(CMODES):
                for j in range(4):
                    coarse[pl.ds((a * 16 + g) * 8 + j * 2 + x, CMODES, stride=32), :] = total[
                        x * 16 + a * 4:x * 16 + a * 4 + 4, j * 128:(j + 1) * 128]
        return 0
    for d in range(4):
        @pl.when(exists[d])
        def _(d=d):
            param_copy(d).wait_send()
            make = (x_copy, y_copy)[d // 2]
            for k in range(3):
                def sent(i, _, make=make):
                    make(k, d % 2, i).wait_send()
                    return 0
                if d < 2 and k == 1:
                    lax.fori_loop(0, CMODES, sent, 0)
                    lax.fori_loop(CMODES, MODES, functools.partial(
                        sent, make=functools.partial(x_copy, width=CMODES)), 0)
                else:
                    lax.fori_loop(0, MODES if k < 2 else CMODES, sent, 0)
    lax.fori_loop(0, 2, gather, 0)
    for d in range(2):
        @pl.when(source[d])
        def _(d=d):
            late_copy(d).wait_recv()

    def pass_late(g, _):
        update(1, g, CMODES, MODES)
        return 0
    lax.fori_loop(CMODES, MODES, pass_late, 0)

    for d in range(2):
        @pl.when(exists[d])
        def _(d=d):
            late_copy(d).wait_send()
    lax.fori_loop(2, CMODES, gather, 0)


def smoother(nx, ny, rhs, coef, deg):
    field = pltpu.VMEM((MODES, MODES, MODES, 8, 128), F32)
    wide = pltpu.VMEM((2, 2, MODES, MODES, 8, 128), F32)
    narrow = pltpu.VMEM((2, CMODES, CMODES, 8, 128), F32)
    wide_half = pltpu.VMEM((2, 2, MODES, (MODES + 1) // 2, 8, 128), F32)
    narrow_half = pltpu.VMEM((2, CMODES, CMODES // 2, 8, 128), F32)
    return pl.pallas_call(
        functools.partial(kernel, nx, ny),
        out_shape=(jax.ShapeDtypeStruct((MODES, MODES, MODES, 8, 128), F32),
                   jax.ShapeDtypeStruct((CMODES**3 * 8, 128), F32)),
        in_specs=[pl.BlockSpec(memory_space=pltpu.HBM)] * 3,
        out_specs=[pl.BlockSpec(memory_space=pltpu.VMEM)] * 2,
        scratch_shapes=[
            field,
            pltpu.VMEM((8, 128), F32),
            pltpu.VMEM((3, 8, 128), jnp.int32),
            field, field, field,
            pltpu.VMEM((3, 6, 8, 128), F32),
            pltpu.VMEM((3, MODES, 8, 128), F32),
            pltpu.VMEM((MODES, 8, 128), F32),
            pltpu.VMEM((4, 8, 128), F32),
            pltpu.VMEM((4, 8, 128), F32),
            wide, wide, wide_half, wide_half, narrow, narrow, narrow_half, narrow_half,
            pltpu.VMEM((CMODES, 128, 128), F32),
            pltpu.VMEM((ny, CMODES, 2, CMODES**2, 128), F32),
            pltpu.VMEM((ny, CMODES, 2, CMODES**2, 128), F32),
            pltpu.VMEM((ny * 128, 512), jnp.bfloat16),
            pltpu.SemaphoreType.DMA((3,)),
            pltpu.SemaphoreType.DMA((4,)),
            pltpu.SemaphoreType.DMA((4,)),
            pltpu.SemaphoreType.DMA((3, 2, MODES)),
            pltpu.SemaphoreType.DMA((3, 2, MODES)),
            pltpu.SemaphoreType.DMA((3, 2, MODES)),
            pltpu.SemaphoreType.DMA((3, 2, MODES)),
            pltpu.SemaphoreType.DMA((2,)),
            pltpu.SemaphoreType.DMA((2,)),
            pltpu.SemaphoreType.DMA((ny, CMODES)),
            pltpu.SemaphoreType.DMA((ny, CMODES)),
        ],
        compiler_params=pltpu.CompilerParams(
            collective_id=0, has_side_effects=True, vmem_limit_bytes=48 * 1024 * 1024
        ),
    )(*(pltpu.with_memory_space_constraint(v, pltpu.HBM) for v in (rhs, coef, deg)))


def finish_kernel(u, blocks, stored, coarse, sem):
    copies = [pltpu.make_async_copy(a, b, sem.at[i]) for i, (a, b) in enumerate(((u, stored), (blocks, coarse)))]
    for copy in copies:
        copy.start()
    for copy in copies:
        copy.wait()


def finish(u, blocks):
    return pl.pallas_call(
        finish_kernel,
        out_shape=(jax.ShapeDtypeStruct(u.shape, F32), jax.ShapeDtypeStruct(blocks.shape, F32)),
        in_specs=[pl.BlockSpec(memory_space=pl.ANY)] * 2,
        out_specs=[pl.BlockSpec(memory_space=pltpu.HBM)] * 2,
        scratch_shapes=[pltpu.SemaphoreType.DMA((2,))],
        compiler_params=pltpu.CompilerParams(vmem_limit_bytes=16 * 1024 * 1024),
    )(u, blocks)


def solution(mesh):
    nx, ny = mesh.shape["gx"], mesh.shape["gy"]

    def body(right_side, coefficient, degrees):
        local = right_side.shape[3:]
        flat = (local[0] * local[1], local[2])
        smoothed, blocks = smoother(
            nx, ny,
            right_side.reshape(right_side.shape[:3] + flat),
            coefficient.reshape(flat),
            degrees.reshape((3,) + flat),
        )
        smoothed, coarse = finish(smoothed, blocks)
        coarse = jnp.transpose(coarse.reshape(CMODES**3, 4, 2, 128), (0, 2, 1, 3))
        return smoothed.reshape(right_side.shape), coarse.reshape(CMODES**3, 2, 512)

    in_specs = (
        P(None, None, None, "gx", "gy", None),
        P("gx", "gy", None),
        P(None, "gx", "gy", None),
    )
    out_specs = (P(None, None, None, "gx", "gy", None), P(None, "gx", "gy"))
    return jax.shard_map(body, mesh=mesh, in_specs=in_specs, out_specs=out_specs, check_vma=False)
```

```python
import functools

import jax
import jax.numpy as jnp
from jax import lax
from jax.experimental import pallas as pl
from jax.experimental.pallas import tpu as pltpu
from jax.sharding import PartitionSpec as P

CMODES = 4
LAM_HIGH = 6.0
LAM_LOW = 0.5
MODES = 7
EARLY = 2
MESH = pl.DeviceIdType.MESH
F32 = jnp.float32
HALF = [(2.0 * n + 1.0) / 2.0 for n in range(MODES)]
SLOPE = [n * (n + 1.0) / 2.0 for n in range(MODES)]


def chebyshev():
    centre = (LAM_HIGH + LAM_LOW) / 2.0
    radius = (LAM_HIGH - LAM_LOW) / 2.0
    ratio = centre / radius
    rho = 1.0 / ratio
    pairs = []
    for _ in range(2):
        following = 1.0 / (2.0 * ratio - rho)
        pairs.append((following * rho, 2.0 * following / radius))
        rho = following
    return 1.0 / centre, pairs


def rows(shape):
    return lax.broadcasted_iota(jnp.int32, shape, len(shape) - 2)


def lanes(shape):
    return lax.broadcasted_iota(jnp.int32, shape, len(shape) - 1)


def turn(v, shift):
    return pltpu.roll(v, shift, v.ndim - 2)


def pack_x_up(p, q):
    return jnp.where(rows(p.shape) < 4, turn(p, 4), q)


def pack_x_down(p, q):
    return jnp.where(rows(p.shape) < 4, p, turn(q, 4))


def prev_x(p, q, g):
    low = rows(p.shape) < 4
    return jnp.where(low, g, turn(p, 4)), turn(jnp.where(low, q, g), 4)


def next_x(p, q, g):
    low = rows(p.shape) < 4
    return turn(jnp.where(low, g, p), 4), jnp.where(low, turn(q, 4), g)


def halves(p):
    half = (p.shape[0] + 1) // 2
    if p.shape[0] == 1:
        return p, p
    high = p[half:]
    if p.shape[0] % 2:
        high = jnp.concatenate([high, p[half - 1:half]], axis=0)
    return p[:half], high


def pack_y_up(p, q):
    (p, p_high), (q, q_high) = halves(p), halves(q)
    r = rows(p.shape) & 3
    return jnp.where(r < 2, jnp.where(r == 0, turn(p, 5), turn(q, 6)), jnp.where(r == 2, turn(p_high, 7), q_high))


def pack_y_down(p, q):
    (p, p_high), (q, q_high) = halves(p), halves(q)
    r = rows(p.shape) & 3
    return jnp.where(r < 2, jnp.where(r == 1, turn(p_high, 1), q_high), jnp.where(r == 3, turn(p, 3), turn(q, 2)))


def open_y(g, count, shifts):
    def both(low, high):
        first = turn(g, low) if low else g
        if count == 1:
            return first
        return jnp.concatenate([first, turn(g, high)[:count - g.shape[0]]], axis=0)
    return both(shifts[0], shifts[1]), both(shifts[2], shifts[3])


def prev_y(p, q, g):
    edge = (rows(p.shape) & 3) == 0
    g = open_y(g, p.shape[0], (0, 6, 7, 5))
    return jnp.where(edge, g[0], turn(p, 1)), jnp.where(edge, g[1], turn(q, 1))


def next_y(p, q, g):
    edge = (rows(p.shape) & 3) == 3
    g = open_y(g, p.shape[0], (0, 2, 1, 3))
    return jnp.where(edge, g[0], turn(p, 7)), jnp.where(edge, g[1], turn(q, 7))


def prev_z(p):
    return jnp.where(lanes(p.shape) == 0, 0.0, pltpu.roll(p, 1, p.ndim - 1))


def next_z(p):
    end = p.shape[-1] - 1
    return jnp.where(lanes(p.shape) == end, 0.0, pltpu.roll(p, end, p.ndim - 1))


def line(u, half_coef):
    t4 = u[4] + u[6]
    t2 = u[2] + t4
    even = u[0] + t2
    t3 = u[3] + u[5]
    odd = u[1] + t3
    s2 = 6.0 * t2
    s4 = s2 + 14.0 * t4
    s6 = s4 + 22.0 * u[6]
    s1 = 2.0 * odd
    s3 = s1 + 10.0 * t3
    s5 = s3 + 18.0 * u[5]
    tp = even + odd
    tm = even - odd
    fp = half_coef * (s6 + s5)
    fm = half_coef * (s5 - s6)
    return (tp, tm, fp, fm), (None, s1, s2, s3, s4, s5, s6)


def spread(traces, before, after, geom, coef, sums, count):
    tp, tm, fp, fm = traces
    tau_a, tau_b, w_a, w_b, k_a, k_b = geom
    jump_a = tp - after[0]
    g_a = tau_a * jump_a - w_a * (fp + after[1])
    jump_b = before[0] - tm
    g_b = tau_b * jump_b - w_b * (before[1] + fm)
    kl = k_a * jump_a
    kr = k_b * jump_b
    p = (g_a - g_b, g_a + g_b)
    q = (kl - kr, kl + kr)
    out = [HALF[0] * p[0]]
    for n in range(1, count):
        out.append(HALF[n] * (coef * sums[n] + (p[n % 2] - SLOPE[n] * q[n % 2])))
    return out


def kernel(nx, ny, rhs_hbm, coef_hbm, deg_hbm, u, coarse, s, coef, deg, inv, step, acc, geo, dia, ym,
           ps, pg, xs, xg, ys, yg, xs3, xg3, ys3, yg3, kept, folds, folded,
           in_sem, p_send, p_recv, x_send, x_recv, y_send, y_recv, l_send, l_recv, f_send, f_recv):
    loads = [pltpu.make_async_copy(a, b, in_sem.at[i])
             for i, (a, b) in enumerate(((coef_hbm, coef), (deg_hbm, deg), (rhs_hbm, s)))]
    for load in loads:
        load.start()
    gx, gy = lax.axis_index("gx"), lax.axis_index("gy")
    exists = (gx < nx - 1, gx > 0, gy < ny - 1, gy > 0)
    target = ({"gx": gx + 1}, {"gx": gx - 1}, {"gy": gy + 1}, {"gy": gy - 1})
    source = (exists[1], exists[0], exists[3], exists[2])

    barrier = pltpu.get_barrier_semaphore()
    near = ny <= 4
    for d in range(4 if near else 2):
        @pl.when(exists[d])
        def _(d=d):
            pl.semaphore_signal(barrier, inc=1, device_id=target[d], device_id_type=MESH)
    for d in range(0 if near else ny):
        @pl.when(gy != d)
        def _(d=d):
            pl.semaphore_signal(barrier, inc=1, device_id={"gy": d}, device_id_type=MESH)
    greeted = sum(e.astype(jnp.int32) for e in (exists if near else exists[:2])) + (0 if near else ny - 1)

    def copy(src, dst, send, recv, d):
        return pltpu.make_async_remote_copy(src_ref=src, dst_ref=dst, send_sem=send, recv_sem=recv,
                                            device_id=target[d], device_id_type=MESH)

    def param_copy(d):
        return copy(ps.at[d], pg.at[d], p_send.at[d], p_recv.at[d], d)

    def x_copy(k, d, b, width=MODES):
        if k < 2:
            part = pl.ds(0, width)
            return copy(xs.at[k, d, b, part], xg.at[k, d, b, part], x_send.at[k, d, b], x_recv.at[k, d, b], d)
        return copy(xs3.at[d, b], xg3.at[d, b], x_send.at[k, d, b], x_recv.at[k, d, b], d)

    def y_copy(k, d, a):
        if k < 2:
            return copy(ys.at[k, d, a], yg.at[k, d, a], y_send.at[k, d, a], y_recv.at[k, d, a], 2 + d)
        return copy(ys3.at[d, a], yg3.at[d, a], y_send.at[k, d, a], y_recv.at[k, d, a], 2 + d)

    def late_copy(d):
        part = (1, d, pl.ds(CMODES, MODES - CMODES), pl.ds(CMODES, MODES - CMODES))
        return copy(xs.at[part], xg.at[part], l_send.at[d], l_recv.at[d], d)

    loads[0].wait()
    loads[1].wait()
    c = coef[...]
    half_coef = 0.5 * c
    depth = 128 // ny
    df = [deg[d].astype(F32) for d in range(3)]
    ps[0] = pack_x_up(c, df[0])
    ps[1] = pack_x_down(c, df[0])
    ps[2] = pack_y_up(c[None], df[1][None])[0]
    ps[3] = pack_y_down(c[None], df[1][None])[0]
    pl.semaphore_wait(barrier, greeted)
    for d in range(4):
        @pl.when(exists[d])
        def _(d=d):
            param_copy(d).start()

    for d in range(4):
        @pl.when(jnp.logical_not(source[d]))
        def _(d=d):
            pg[d] = jnp.zeros((8, 128), F32)
            ghosts = (xg, yg)[d // 2]
            ghosts3 = (xg3, yg3)[d // 2]

            def clear(i, _):
                for k in range(2):
                    ghosts[k, d % 2, i] = jnp.zeros(ghosts.shape[3:], F32)
                return 0
            lax.fori_loop(0, MODES, clear, 0)

            def clear3(i, _):
                ghosts3[d % 2, i] = jnp.zeros(ghosts3.shape[2:], F32)
                return 0
            lax.fori_loop(0, CMODES, clear3, 0)

    shape = (MODES, 8, 128)
    levels = lax.broadcasted_iota(jnp.int32, shape, 0)
    ym[...] = jnp.where(levels <= deg[1][None], 1.0, 0.0)

    def prepare(direction, before, after, first, last):
        degree = df[direction]
        wide_a = jnp.maximum(degree, after[1])
        wide_b = jnp.maximum(degree, before[1])
        tau_a = jnp.maximum(c, after[0]) * (wide_a + 1.0) * (wide_a + 2.0)
        tau_b = jnp.maximum(c, before[0]) * (wide_b + 1.0) * (wide_b + 2.0)
        w_a = jnp.where(last, 1.0, 0.5)
        w_b = jnp.where(first, 1.0, 0.5)
        for i, value in enumerate((tau_a, tau_b, w_a, w_b, w_a * c, w_b * c)):
            geo[direction, i] = value
        rest = (1.0 - (w_a + w_b)) * c
        for n in range(MODES):
            dia[direction, n] = HALF[n] * (tau_a + tau_b + (2.0 * SLOPE[n]) * rest)

    row, lane = rows((8, 128)), lanes((8, 128))
    prepare(2, (prev_z(c), prev_z(df[2])), (next_z(c), next_z(df[2])), lane == 0, lane == 127)
    odd = gx % 2

    def params(d, want):
        @pl.when(want)
        def _():
            param_copy(d).wait_recv()

    params(2, source[2])
    params(3, source[3])
    params(0, source[0] & (odd == 1))
    params(1, source[1] & (odd == 0))
    px, py = gx * 2 + (row >> 2), gy * 4 + (row & 3)

    def prepare_x(low, high):
        prepare(0, prev_x(c, df[0], low), next_x(c, df[0], high), px == 0, px == 2 * nx - 1)

    before, after = prev_y(c[None], df[1][None], pg[2:3]), next_y(c[None], df[1][None], pg[3:4])
    prepare(1, [v[0] for v in before], [v[0] for v in after], py == 0, py == 4 * ny - 1)
    beside = pg[1 - odd]
    prepare_x(beside, beside)

    first_scale, pairs = chebyshev()
    odds = 2.0 * levels.astype(F32) + 1.0

    def geom(direction):
        return tuple(geo[direction, i][None] for i in range(6))

    def start(make, k, at, base):
        for d in range(2):
            @pl.when(exists[base + d])
            def _(d=d):
                make(k, d, at).start()

    def arrive(make, k, at, base):
        for d in range(2):
            @pl.when(source[base + d])
            def _(d=d):
                make(k, d, at).wait_recv()

    def send(k, g, values, width=MODES, begun=False):
        count = values[0].shape[0]
        (tp, tm, fp, fm), _ = line(values, half_coef[None])
        up, down = pack_x_up(tp, fp), pack_x_down(tm, fm)
        if begun:
            xs[k, 1 - odd, g] = jnp.where(odd == 0, down, up)
            start_side(k, g, 1 - odd)
        elif k < 2:
            xs[k, 0, g] = up
            xs[k, 1, g] = down
        else:
            xs3[0, g] = up
            xs3[1, g] = down
        if not begun:
            start(functools.partial(x_copy, width=width), k, g, 0)
        (tp, tm, fp, fm), _ = line([u[0:count, n, g] for n in range(MODES)], half_coef[None])
        up, down = pack_y_up(tp, fp), pack_y_down(tm, fm)
        if k < 2:
            ys[k, 0, g] = up
            ys[k, 1, g] = down
        else:
            ys3[0, g] = up
            ys3[1, g] = down
        start(y_copy, k, g, 2)

    def start_side(k, g, side):
        for d in range(2):
            @pl.when(exists[d] & (side == d))
            def _(d=d):
                x_copy(k, d, g).start()

    loads[2].wait()

    def first(g):
        inside = ym[...] * jnp.where(deg[2] >= g, 1.0, 0.0)[None]
        across = dia[1] + dia[2, g][None]
        scale = odds * ((2.0 * g.astype(F32) + 1.0) / 8.0)
        for a in range(MODES):
            i = jnp.where(deg[0] >= a, 1.0, 0.0)[None] * inside / (dia[0, a][None] + across)
            r = s[a, :, g] * (scale * (2.0 * a + 1.0))
            yield i, r, i * r * first_scale

    def begin(g, _):
        (tp, tm, fp, fm), _ = line([x for _, _, x in first(g)], half_coef[None])
        xs[0, odd, g] = jnp.where(odd == 0, pack_x_up(tp, fp), pack_x_down(tm, fm))
        start_side(0, g, odd)
        return 0
    lax.fori_loop(0, EARLY, begin, 0)

    params(0, source[0] & (odd == 0))
    params(1, source[1] & (odd == 1))
    prepare_x(pg[0], pg[1])

    def setup(g, _, begun=False):
        fresh = []
        for a, (i, r, x) in enumerate(first(g)):
            s[a, :, g] = r
            inv[a, :, g] = i
            u[a, :, g] = x
            fresh.append(x)
        send(0, g, fresh, begun=begun)
        return 0
    lax.fori_loop(0, EARLY, functools.partial(setup, begun=True), 0)
    lax.fori_loop(EARLY, MODES, setup, 0)

    def fold_copy(d, b):
        return pltpu.make_async_remote_copy(
            src_ref=folds.at[d, b], dst_ref=folded.at[gy, b], send_sem=f_send.at[d, b],
            recv_sem=f_recv.at[gy, b], device_id={"gy": d}, device_id_type=MESH)

    def fold_arrival(d, b):
        return pltpu.make_async_remote_copy(
            src_ref=folds.at[d, b], dst_ref=folded.at[d, b], send_sem=f_send.at[d, b],
            recv_sem=f_recv.at[d, b], device_id={"gy": d}, device_id_type=MESH)

    def fold(b):
        block = lanes((CMODES**2, 128)) // depth
        for x in range(2):
            by_y = [kept[b, pl.ds(x * 4 + y, CMODES**2, stride=8), :] for y in range(4)]
            for d in range(ny):
                out = jnp.zeros((CMODES**2, 128), F32)
                for y in range(4):
                    shift = ((y - d) * depth) % 128
                    out = jnp.where(block == y, pltpu.roll(by_y[y], shift, 1) if shift else by_y[y], out)
                folds[d, b, x] = out
        for d in range(ny):
            @pl.when(gy // 2 != d // 2)
            def _(d=d):
                fold_copy(d, b).start()
        for d in range(ny):
            @pl.when((gy // 2 == d // 2) & (gy != d))
            def _(d=d):
                fold_copy(d, b).start()

            @pl.when(gy == d)
            def _(d=d):
                folded[d, b] = folds[d, b]

    def x_terms(values, g_prev, g_next, count):
        traces, sums = line(values, half_coef[None])
        tp, tm, fp, fm = traces
        return spread(traces, prev_x(tp, fp, g_prev), next_x(tm, fm, g_next), geom(0), c[None], sums, count)

    def update(k, g, low, high):
        values = [u[n, low:high, g] for n in range(MODES)]
        out = x_terms(values, xg[k, 0, g, low:high], xg[k, 1, g, low:high], MODES)
        fresh = []
        for n in range(MODES):
            residual = s[n, low:high, g] - (acc[n, low:high, g] + out[n])
            last = values[n] if k < 1 else step[n, low:high, g]
            change = pairs[k][0] * last + pairs[k][1] * (inv[n, low:high, g] * residual)
            moved = values[n] + change
            if k < 1:
                step[n, low:high, g] = change
            u[n, low:high, g] = moved
            fresh.append(moved)
        return fresh

    for k in range(3):
        count = MODES if k < 2 else CMODES

        def pass_z(a, _):
            traces, sums = line([u[a, 0:count, n] for n in range(MODES)], half_coef[None])
            tp, tm, fp, fm = traces
            out = spread(traces, (prev_z(tp), prev_z(fp)), (next_z(tm), next_z(fm)),
                         geom(2), c[None], sums, count)
            for n in range(count):
                acc[a, 0:count, n] = out[n]
            return 0
        lax.fori_loop(0, count, pass_z, 0)
        if k == 2:
            for d in range(2):
                @pl.when(exists[d])
                def _(d=d):
                    late_copy(d).start()

        def pass_xy(g, _, following=False, coarse_only=False, last=False):
            arrive(y_copy, k, g, 2)
            traces, sums = line([u[0:count, n, g] for n in range(MODES)], half_coef[None])
            tp, tm, fp, fm = traces
            g_prev = yg[k, 0, g] if k < 2 else yg3[0, g]
            g_next = yg[k, 1, g] if k < 2 else yg3[1, g]
            out = spread(traces, prev_y(tp, fp, g_prev), next_y(tm, fm, g_next),
                         geom(1), c[None], sums, count)
            for n in range(count):
                acc[0:count, n, g] += out[n]

            if k < 2:
                width = CMODES if coarse_only else MODES
                arrive(functools.partial(x_copy, width=width), k, g, 0)
                fresh = update(k, g, 0, width)
                if following:
                    keep = MODES if k < 1 else CMODES
                    send(k + 1, g, [v[0:keep] for v in fresh], CMODES if last else MODES)
            else:
                arrive(x_copy, k, g, 0)
                out = x_terms([u[n, 0:count, g] for n in range(MODES)], xg3[0, g], xg3[1, g], count)
                low = lax.broadcasted_iota(jnp.int32, (CMODES, 8, 128), 0)
                inside_y = jnp.where(low <= (deg[1] >> 1)[None], 1.0, 0.0)
                inside_z = jnp.where((deg[2] >> 1) >= g, 1.0, 0.0)
                mass = (1.0 / ((2.0 * low.astype(F32) + 1.0) * (2.0 * g.astype(F32) + 1.0))) * (
                    inside_y * inside_z[None])
                for n in range(CMODES):
                    inside = jnp.where((deg[0] >> 1) >= n, 8.0 / (2.0 * n + 1.0), 0.0)
                    residual = s[n, 0:CMODES, g] - (acc[n, 0:CMODES, g] + out[n])
                    kept[g, n * 32:(n + 1) * 32] = (residual * (mass * inside[None])).reshape(32, 128)
                fold(g)
            return 0
        if k == 0:
            lax.fori_loop(0, CMODES, functools.partial(pass_xy, following=True), 0)
            lax.fori_loop(CMODES, MODES, functools.partial(pass_xy, following=True, last=True), 0)
        elif k == 1:
            lax.fori_loop(0, CMODES, functools.partial(pass_xy, following=True), 0)
            lax.fori_loop(CMODES, MODES, functools.partial(pass_xy, coarse_only=True), 0)
        else:
            lax.fori_loop(0, CMODES, pass_xy, 0)

    def gather(g, _):
        for d in range(ny):
            @pl.when(gy != d)
            def _(d=d):
                fold_copy(d, g).wait_send()
                fold_arrival(d, g).wait_recv()
        lane = lanes((2 * CMODES**2, 128))
        owner = (lane % (4 * ny)) // 4
        spread_z = 128 // (4 * ny)
        blocks = [folded[d, g].reshape(2 * CMODES**2, 128) for d in range(ny)]
        total = []
        for j in range(4):
            at = (lane % 4) * depth + j * spread_z + lane // (4 * ny)
            tile = jnp.take_along_axis(blocks[0], at, axis=1)
            for d in range(1, ny):
                tile = jnp.where(owner == d, jnp.take_along_axis(blocks[d], at, axis=1), tile)
            total.append(tile)
        for x in range(2):
            for a in range(CMODES):
                for j in range(4):
                    coarse[pl.ds((a * 16 + g) * 8 + j * 2 + x, CMODES, stride=32), :] = total[j][
                        x * 16 + a * 4:x * 16 + a * 4 + 4]
        return 0
    for d in range(4):
        @pl.when(exists[d])
        def _(d=d):
            param_copy(d).wait_send()
            make = (x_copy, y_copy)[d // 2]
            for k in range(3):
                def sent(i, _, make=make):
                    make(k, d % 2, i).wait_send()
                    return 0
                if d < 2 and k == 1:
                    lax.fori_loop(0, CMODES, sent, 0)
                    lax.fori_loop(CMODES, MODES, functools.partial(
                        sent, make=functools.partial(x_copy, width=CMODES)), 0)
                else:
                    lax.fori_loop(0, MODES if k < 2 else CMODES, sent, 0)
    lax.fori_loop(0, 2, gather, 0)
    for d in range(2):
        @pl.when(source[d])
        def _(d=d):
            late_copy(d).wait_recv()

    def pass_late(g, _):
        update(1, g, CMODES, MODES)
        return 0
    lax.fori_loop(CMODES, MODES, pass_late, 0)

    for d in range(2):
        @pl.when(exists[d])
        def _(d=d):
            late_copy(d).wait_send()
    lax.fori_loop(2, CMODES, gather, 0)


def smoother(nx, ny, rhs, coef, deg):
    field = pltpu.VMEM((MODES, MODES, MODES, 8, 128), F32)
    wide = pltpu.VMEM((2, 2, MODES, MODES, 8, 128), F32)
    narrow = pltpu.VMEM((2, CMODES, CMODES, 8, 128), F32)
    wide_half = pltpu.VMEM((2, 2, MODES, (MODES + 1) // 2, 8, 128), F32)
    narrow_half = pltpu.VMEM((2, CMODES, CMODES // 2, 8, 128), F32)
    return pl.pallas_call(
        functools.partial(kernel, nx, ny),
        out_shape=(jax.ShapeDtypeStruct((MODES, MODES, MODES, 8, 128), F32),
                   jax.ShapeDtypeStruct((CMODES**3 * 8, 128), F32)),
        in_specs=[pl.BlockSpec(memory_space=pltpu.HBM)] * 3,
        out_specs=[pl.BlockSpec(memory_space=pltpu.VMEM)] * 2,
        scratch_shapes=[
            field,
            pltpu.VMEM((8, 128), F32),
            pltpu.VMEM((3, 8, 128), jnp.int32),
            field, field, field,
            pltpu.VMEM((3, 6, 8, 128), F32),
            pltpu.VMEM((3, MODES, 8, 128), F32),
            pltpu.VMEM((MODES, 8, 128), F32),
            pltpu.VMEM((4, 8, 128), F32),
            pltpu.VMEM((4, 8, 128), F32),
            wide, wide, wide_half, wide_half, narrow, narrow, narrow_half, narrow_half,
            pltpu.VMEM((CMODES, 128, 128), F32),
            pltpu.VMEM((ny, CMODES, 2, CMODES**2, 128), F32),
            pltpu.VMEM((ny, CMODES, 2, CMODES**2, 128), F32),
            pltpu.SemaphoreType.DMA((3,)),
            pltpu.SemaphoreType.DMA((4,)),
            pltpu.SemaphoreType.DMA((4,)),
            pltpu.SemaphoreType.DMA((3, 2, MODES)),
            pltpu.SemaphoreType.DMA((3, 2, MODES)),
            pltpu.SemaphoreType.DMA((3, 2, MODES)),
            pltpu.SemaphoreType.DMA((3, 2, MODES)),
            pltpu.SemaphoreType.DMA((2,)),
            pltpu.SemaphoreType.DMA((2,)),
            pltpu.SemaphoreType.DMA((ny, CMODES)),
            pltpu.SemaphoreType.DMA((ny, CMODES)),
        ],
        compiler_params=pltpu.CompilerParams(
            collective_id=0, has_side_effects=True, vmem_limit_bytes=48 * 1024 * 1024
        ),
    )(*(pltpu.with_memory_space_constraint(v, pltpu.HBM) for v in (rhs, coef, deg)))


def finish_kernel(u, blocks, stored, coarse, sem):
    copies = [pltpu.make_async_copy(a, b, sem.at[i]) for i, (a, b) in enumerate(((u, stored), (blocks, coarse)))]
    for copy in copies:
        copy.start()
    for copy in copies:
        copy.wait()


def finish(u, blocks):
    return pl.pallas_call(
        finish_kernel,
        out_shape=(jax.ShapeDtypeStruct(u.shape, F32), jax.ShapeDtypeStruct(blocks.shape, F32)),
        in_specs=[pl.BlockSpec(memory_space=pl.ANY)] * 2,
        out_specs=[pl.BlockSpec(memory_space=pltpu.HBM)] * 2,
        scratch_shapes=[pltpu.SemaphoreType.DMA((2,))],
        compiler_params=pltpu.CompilerParams(vmem_limit_bytes=16 * 1024 * 1024),
    )(u, blocks)


def solution(mesh):
    nx, ny = mesh.shape["gx"], mesh.shape["gy"]

    def body(right_side, coefficient, degrees):
        local = right_side.shape[3:]
        flat = (local[0] * local[1], local[2])
        smoothed, blocks = smoother(
            nx, ny,
            right_side.reshape(right_side.shape[:3] + flat),
            coefficient.reshape(flat),
            degrees.reshape((3,) + flat),
        )
        smoothed, coarse = finish(smoothed, blocks)
        coarse = jnp.transpose(coarse.reshape(CMODES**3, 4, 2, 128), (0, 2, 1, 3))
        return smoothed.reshape(right_side.shape), coarse.reshape(CMODES**3, 2, 512)

    in_specs = (
        P(None, None, None, "gx", "gy", None),
        P("gx", "gy", None),
        P(None, "gx", "gy", None),
    )
    out_specs = (P(None, None, None, "gx", "gy", None), P(None, "gx", "gy"))
    return jax.shard_map(body, mesh=mesh, in_specs=in_specs, out_specs=out_specs, check_vma=False)
```

```python
import functools

import jax
import jax.numpy as jnp
from jax import lax
from jax.experimental import pallas as pl
from jax.experimental.pallas import tpu as pltpu
from jax.sharding import PartitionSpec as P

CMODES = 4
LAM_HIGH = 6.0
LAM_LOW = 0.5
MODES = 7
EARLY = 2
MESH = pl.DeviceIdType.MESH
F32 = jnp.float32
HALF = [(2.0 * n + 1.0) / 2.0 for n in range(MODES)]
SLOPE = [n * (n + 1.0) / 2.0 for n in range(MODES)]


def chebyshev():
    centre = (LAM_HIGH + LAM_LOW) / 2.0
    radius = (LAM_HIGH - LAM_LOW) / 2.0
    ratio = centre / radius
    rho = 1.0 / ratio
    pairs = []
    for _ in range(2):
        following = 1.0 / (2.0 * ratio - rho)
        pairs.append((following * rho, 2.0 * following / radius))
        rho = following
    return 1.0 / centre, pairs


def rows(shape):
    return lax.broadcasted_iota(jnp.int32, shape, len(shape) - 2)


def lanes(shape):
    return lax.broadcasted_iota(jnp.int32, shape, len(shape) - 1)


def turn(v, shift):
    return pltpu.roll(v, shift, v.ndim - 2)


def pack_x_up(p, q):
    return jnp.where(rows(p.shape) < 4, turn(p, 4), q)


def pack_x_down(p, q):
    return jnp.where(rows(p.shape) < 4, p, turn(q, 4))


def prev_x(p, q, g):
    low = rows(p.shape) < 4
    return jnp.where(low, g, turn(p, 4)), turn(jnp.where(low, q, g), 4)


def next_x(p, q, g):
    low = rows(p.shape) < 4
    return turn(jnp.where(low, g, p), 4), jnp.where(low, turn(q, 4), g)


def halves(p):
    half = (p.shape[0] + 1) // 2
    if p.shape[0] == 1:
        return p, p
    high = p[half:]
    if p.shape[0] % 2:
        high = jnp.concatenate([high, p[half - 1:half]], axis=0)
    return p[:half], high


def pack_y_up(p, q):
    (p, p_high), (q, q_high) = halves(p), halves(q)
    r = rows(p.shape) & 3
    return jnp.where(r < 2, jnp.where(r == 0, turn(p, 5), turn(q, 6)), jnp.where(r == 2, turn(p_high, 7), q_high))


def pack_y_down(p, q):
    (p, p_high), (q, q_high) = halves(p), halves(q)
    r = rows(p.shape) & 3
    return jnp.where(r < 2, jnp.where(r == 1, turn(p_high, 1), q_high), jnp.where(r == 3, turn(p, 3), turn(q, 2)))


def open_y(g, count, shifts):
    def both(low, high):
        first = turn(g, low) if low else g
        if count == 1:
            return first
        return jnp.concatenate([first, turn(g, high)[:count - g.shape[0]]], axis=0)
    return both(shifts[0], shifts[1]), both(shifts[2], shifts[3])


def prev_y(p, q, g):
    edge = (rows(p.shape) & 3) == 0
    g = open_y(g, p.shape[0], (0, 6, 7, 5))
    return jnp.where(edge, g[0], turn(p, 1)), jnp.where(edge, g[1], turn(q, 1))


def next_y(p, q, g):
    edge = (rows(p.shape) & 3) == 3
    g = open_y(g, p.shape[0], (0, 2, 1, 3))
    return jnp.where(edge, g[0], turn(p, 7)), jnp.where(edge, g[1], turn(q, 7))


def prev_z(p):
    return jnp.where(lanes(p.shape) == 0, 0.0, pltpu.roll(p, 1, p.ndim - 1))


def next_z(p):
    end = p.shape[-1] - 1
    return jnp.where(lanes(p.shape) == end, 0.0, pltpu.roll(p, end, p.ndim - 1))


def line(u, half_coef):
    t4 = u[4] + u[6]
    t2 = u[2] + t4
    even = u[0] + t2
    t3 = u[3] + u[5]
    odd = u[1] + t3
    s2 = 6.0 * t2
    s4 = s2 + 14.0 * t4
    s6 = s4 + 22.0 * u[6]
    s1 = 2.0 * odd
    s3 = s1 + 10.0 * t3
    s5 = s3 + 18.0 * u[5]
    tp = even + odd
    tm = even - odd
    fp = half_coef * (s6 + s5)
    fm = half_coef * (s5 - s6)
    return (tp, tm, fp, fm), (None, s1, s2, s3, s4, s5, s6)


def spread(traces, before, after, geom, coef, sums, count):
    tp, tm, fp, fm = traces
    tau_a, tau_b, w_a, w_b, k_a, k_b = geom
    jump_a = tp - after[0]
    g_a = tau_a * jump_a - w_a * (fp + after[1])
    jump_b = before[0] - tm
    g_b = tau_b * jump_b - w_b * (before[1] + fm)
    kl = k_a * jump_a
    kr = k_b * jump_b
    p = (g_a - g_b, g_a + g_b)
    q = (kl - kr, kl + kr)
    out = [HALF[0] * p[0]]
    for n in range(1, count):
        out.append(HALF[n] * (coef * sums[n] + (p[n % 2] - SLOPE[n] * q[n % 2])))
    return out


def kernel(nx, ny, rhs_hbm, coef_hbm, deg_hbm, u, coarse, s, coef, deg, inv, step, acc, geo, dia, ym,
           ps, pg, xs, xg, ys, yg, xs3, xg3, ys3, yg3, kept, folds, folded,
           in_sem, p_send, p_recv, x_send, x_recv, y_send, y_recv, l_send, l_recv, f_send, f_recv):
    loads = [pltpu.make_async_copy(a, b, in_sem.at[i])
             for i, (a, b) in enumerate(((coef_hbm, coef), (deg_hbm, deg), (rhs_hbm, s)))]
    for load in loads:
        load.start()
    gx, gy = lax.axis_index("gx"), lax.axis_index("gy")
    exists = (gx < nx - 1, gx > 0, gy < ny - 1, gy > 0)
    target = ({"gx": gx + 1}, {"gx": gx - 1}, {"gy": gy + 1}, {"gy": gy - 1})
    source = (exists[1], exists[0], exists[3], exists[2])

    barrier = pltpu.get_barrier_semaphore()
    near = ny <= 4
    for d in range(4 if near else 2):
        @pl.when(exists[d])
        def _(d=d):
            pl.semaphore_signal(barrier, inc=1, device_id=target[d], device_id_type=MESH)
    for d in range(0 if near else ny):
        @pl.when(gy != d)
        def _(d=d):
            pl.semaphore_signal(barrier, inc=1, device_id={"gy": d}, device_id_type=MESH)
    greeted = sum(e.astype(jnp.int32) for e in (exists if near else exists[:2])) + (0 if near else ny - 1)

    def copy(src, dst, send, recv, d):
        return pltpu.make_async_remote_copy(src_ref=src, dst_ref=dst, send_sem=send, recv_sem=recv,
                                            device_id=target[d], device_id_type=MESH)

    def param_copy(d):
        return copy(ps.at[d], pg.at[d], p_send.at[d], p_recv.at[d], d)

    def x_copy(k, d, b, width=MODES):
        if k < 2:
            part = pl.ds(0, width)
            return copy(xs.at[k, d, b, part], xg.at[k, d, b, part], x_send.at[k, d, b], x_recv.at[k, d, b], d)
        return copy(xs3.at[d, b], xg3.at[d, b], x_send.at[k, d, b], x_recv.at[k, d, b], d)

    def y_copy(k, d, a):
        if k < 2:
            return copy(ys.at[k, d, a], yg.at[k, d, a], y_send.at[k, d, a], y_recv.at[k, d, a], 2 + d)
        return copy(ys3.at[d, a], yg3.at[d, a], y_send.at[k, d, a], y_recv.at[k, d, a], 2 + d)

    def late_copy(d):
        part = (1, d, pl.ds(CMODES, MODES - CMODES), pl.ds(CMODES, MODES - CMODES))
        return copy(xs.at[part], xg.at[part], l_send.at[d], l_recv.at[d], d)

    loads[0].wait()
    loads[1].wait()
    c = coef[...]
    half_coef = 0.5 * c
    depth = 128 // ny
    df = [deg[d].astype(F32) for d in range(3)]
    ps[0] = pack_x_up(c, df[0])
    ps[1] = pack_x_down(c, df[0])
    ps[2] = pack_y_up(c[None], df[1][None])[0]
    ps[3] = pack_y_down(c[None], df[1][None])[0]
    pl.semaphore_wait(barrier, greeted)
    for d in range(4):
        @pl.when(exists[d])
        def _(d=d):
            param_copy(d).start()

    for d in range(4):
        @pl.when(jnp.logical_not(source[d]))
        def _(d=d):
            pg[d] = jnp.zeros((8, 128), F32)
            ghosts = (xg, yg)[d // 2]
            ghosts3 = (xg3, yg3)[d // 2]

            def clear(i, _):
                for k in range(2):
                    ghosts[k, d % 2, i] = jnp.zeros(ghosts.shape[3:], F32)
                return 0
            lax.fori_loop(0, MODES, clear, 0)

            def clear3(i, _):
                ghosts3[d % 2, i] = jnp.zeros(ghosts3.shape[2:], F32)
                return 0
            lax.fori_loop(0, CMODES, clear3, 0)

    shape = (MODES, 8, 128)
    levels = lax.broadcasted_iota(jnp.int32, shape, 0)
    ym[...] = jnp.where(levels <= deg[1][None], 1.0, 0.0)

    def prepare(direction, before, after, first, last):
        degree = df[direction]
        wide_a = jnp.maximum(degree, after[1])
        wide_b = jnp.maximum(degree, before[1])
        tau_a = jnp.maximum(c, after[0]) * (wide_a + 1.0) * (wide_a + 2.0)
        tau_b = jnp.maximum(c, before[0]) * (wide_b + 1.0) * (wide_b + 2.0)
        w_a = jnp.where(last, 1.0, 0.5)
        w_b = jnp.where(first, 1.0, 0.5)
        for i, value in enumerate((tau_a, tau_b, w_a, w_b, w_a * c, w_b * c)):
            geo[direction, i] = value
        rest = (1.0 - (w_a + w_b)) * c
        for n in range(MODES):
            dia[direction, n] = HALF[n] * (tau_a + tau_b + (2.0 * SLOPE[n]) * rest)

    row, lane = rows((8, 128)), lanes((8, 128))
    prepare(2, (prev_z(c), prev_z(df[2])), (next_z(c), next_z(df[2])), lane == 0, lane == 127)
    odd = gx % 2

    def params(d, want):
        @pl.when(want)
        def _():
            param_copy(d).wait_recv()

    params(2, source[2])
    params(3, source[3])
    params(0, source[0] & (odd == 1))
    params(1, source[1] & (odd == 0))
    px, py = gx * 2 + (row >> 2), gy * 4 + (row & 3)

    def prepare_x(low, high):
        prepare(0, prev_x(c, df[0], low), next_x(c, df[0], high), px == 0, px == 2 * nx - 1)

    before, after = prev_y(c[None], df[1][None], pg[2:3]), next_y(c[None], df[1][None], pg[3:4])
    prepare(1, [v[0] for v in before], [v[0] for v in after], py == 0, py == 4 * ny - 1)
    beside = pg[1 - odd]
    prepare_x(beside, beside)

    first_scale, pairs = chebyshev()
    odds = 2.0 * levels.astype(F32) + 1.0

    def geom(direction):
        return tuple(geo[direction, i][None] for i in range(6))

    def start(make, k, at, base):
        for d in range(2):
            @pl.when(exists[base + d])
            def _(d=d):
                make(k, d, at).start()

    def arrive(make, k, at, base):
        for d in range(2):
            @pl.when(source[base + d])
            def _(d=d):
                make(k, d, at).wait_recv()

    def send(k, g, values, width=MODES, begun=False):
        count = values[0].shape[0]
        (tp, tm, fp, fm), _ = line(values, half_coef[None])
        up, down = pack_x_up(tp, fp), pack_x_down(tm, fm)
        if begun:
            xs[k, 1 - odd, g] = jnp.where(odd == 0, down, up)
            start_side(k, g, 1 - odd)
        elif k < 2:
            xs[k, 0, g] = up
            xs[k, 1, g] = down
        else:
            xs3[0, g] = up
            xs3[1, g] = down
        if not begun:
            start(functools.partial(x_copy, width=width), k, g, 0)
        (tp, tm, fp, fm), _ = line([u[0:count, n, g] for n in range(MODES)], half_coef[None])
        up, down = pack_y_up(tp, fp), pack_y_down(tm, fm)
        if k < 2:
            ys[k, 0, g] = up
            ys[k, 1, g] = down
        else:
            ys3[0, g] = up
            ys3[1, g] = down
        start(y_copy, k, g, 2)

    def start_side(k, g, side):
        for d in range(2):
            @pl.when(exists[d] & (side == d))
            def _(d=d):
                x_copy(k, d, g).start()

    loads[2].wait()

    def first(g):
        inside = ym[...] * jnp.where(deg[2] >= g, 1.0, 0.0)[None]
        across = dia[1] + dia[2, g][None]
        scale = odds * ((2.0 * g.astype(F32) + 1.0) / 8.0)
        for a in range(MODES):
            i = jnp.where(deg[0] >= a, 1.0, 0.0)[None] * inside / (dia[0, a][None] + across)
            r = s[a, :, g] * (scale * (2.0 * a + 1.0))
            yield i, r, i * r * first_scale

    def begin(g, _):
        (tp, tm, fp, fm), _ = line([x for _, _, x in first(g)], half_coef[None])
        xs[0, odd, g] = jnp.where(odd == 0, pack_x_up(tp, fp), pack_x_down(tm, fm))
        start_side(0, g, odd)
        return 0
    lax.fori_loop(0, EARLY, begin, 0)

    params(0, source[0] & (odd == 0))
    params(1, source[1] & (odd == 1))
    prepare_x(pg[0], pg[1])

    def setup(g, _, begun=False):
        fresh = []
        for a, (i, r, x) in enumerate(first(g)):
            s[a, :, g] = r
            inv[a, :, g] = i
            u[a, :, g] = x
            fresh.append(x)
        send(0, g, fresh, begun=begun)
        return 0
    lax.fori_loop(0, EARLY, functools.partial(setup, begun=True), 0)
    lax.fori_loop(EARLY, MODES, setup, 0)

    def fold_copy(d, b):
        return pltpu.make_async_remote_copy(
            src_ref=folds.at[d, b], dst_ref=folded.at[gy, b], send_sem=f_send.at[d, b],
            recv_sem=f_recv.at[gy, b], device_id={"gy": d}, device_id_type=MESH)

    def fold_arrival(d, b):
        return pltpu.make_async_remote_copy(
            src_ref=folds.at[d, b], dst_ref=folded.at[d, b], send_sem=f_send.at[d, b],
            recv_sem=f_recv.at[d, b], device_id={"gy": d}, device_id_type=MESH)

    def fold(b):
        block = lanes((CMODES**2, 128)) // depth
        turned = []
        for x in range(2):
            by_y = [kept[b, pl.ds(x * 4 + y, CMODES**2, stride=8), :] for y in range(4)]
            turned.append([pltpu.roll(v, y * depth, 1) if y else v for y, v in enumerate(by_y)])

        def fill(ref, d):
            for x in range(2):
                out = turned[x][0]
                for y in range(1, 4):
                    out = jnp.where(block == (d + y) % ny, turned[x][y], out)
                ref[d, b, x] = out

        chip = gy // 2
        for step in range(1, ny // 2):
            for core in range(2):
                d = (chip + step) % (ny // 2) * 2 + core
                fill(folds, d)
                fold_copy(d, b).start()
        d = chip * 2 + 1 - gy % 2
        fill(folds, d)
        fold_copy(d, b).start()
        fill(folded, gy)

    def x_terms(values, g_prev, g_next, count):
        traces, sums = line(values, half_coef[None])
        tp, tm, fp, fm = traces
        return spread(traces, prev_x(tp, fp, g_prev), next_x(tm, fm, g_next), geom(0), c[None], sums, count)

    def update(k, g, low, high):
        values = [u[n, low:high, g] for n in range(MODES)]
        out = x_terms(values, xg[k, 0, g, low:high], xg[k, 1, g, low:high], MODES)
        fresh = []
        for n in range(MODES):
            residual = s[n, low:high, g] - (acc[n, low:high, g] + out[n])
            last = values[n] if k < 1 else step[n, low:high, g]
            change = pairs[k][0] * last + pairs[k][1] * (inv[n, low:high, g] * residual)
            moved = values[n] + change
            if k < 1:
                step[n, low:high, g] = change
            u[n, low:high, g] = moved
            fresh.append(moved)
        return fresh

    for k in range(3):
        count = MODES if k < 2 else CMODES

        def pass_z(a, _):
            traces, sums = line([u[a, 0:count, n] for n in range(MODES)], half_coef[None])
            tp, tm, fp, fm = traces
            out = spread(traces, (prev_z(tp), prev_z(fp)), (next_z(tm), next_z(fm)),
                         geom(2), c[None], sums, count)
            for n in range(count):
                acc[a, 0:count, n] = out[n]
            return 0
        lax.fori_loop(0, count, pass_z, 0)
        if k == 2:
            for d in range(2):
                @pl.when(exists[d])
                def _(d=d):
                    late_copy(d).start()

        def pass_xy(g, _, following=False, coarse_only=False, last=False):
            arrive(y_copy, k, g, 2)
            traces, sums = line([u[0:count, n, g] for n in range(MODES)], half_coef[None])
            tp, tm, fp, fm = traces
            g_prev = yg[k, 0, g] if k < 2 else yg3[0, g]
            g_next = yg[k, 1, g] if k < 2 else yg3[1, g]
            out = spread(traces, prev_y(tp, fp, g_prev), next_y(tm, fm, g_next),
                         geom(1), c[None], sums, count)
            for n in range(count):
                acc[0:count, n, g] += out[n]

            if k < 2:
                width = CMODES if coarse_only else MODES
                arrive(functools.partial(x_copy, width=width), k, g, 0)
                fresh = update(k, g, 0, width)
                if following:
                    keep = MODES if k < 1 else CMODES
                    send(k + 1, g, [v[0:keep] for v in fresh], CMODES if last else MODES)
            else:
                arrive(x_copy, k, g, 0)
                out = x_terms([u[n, 0:count, g] for n in range(MODES)], xg3[0, g], xg3[1, g], count)
                low = lax.broadcasted_iota(jnp.int32, (CMODES, 8, 128), 0)
                inside_y = jnp.where(low <= (deg[1] >> 1)[None], 1.0, 0.0)
                inside_z = jnp.where((deg[2] >> 1) >= g, 1.0, 0.0)
                mass = (1.0 / ((2.0 * low.astype(F32) + 1.0) * (2.0 * g.astype(F32) + 1.0))) * (
                    inside_y * inside_z[None])
                for n in range(CMODES):
                    inside = jnp.where((deg[0] >> 1) >= n, 8.0 / (2.0 * n + 1.0), 0.0)
                    residual = s[n, 0:CMODES, g] - (acc[n, 0:CMODES, g] + out[n])
                    kept[g, n * 32:(n + 1) * 32] = (residual * (mass * inside[None])).reshape(32, 128)
                fold(g)
            return 0
        if k == 0:
            lax.fori_loop(0, CMODES, functools.partial(pass_xy, following=True), 0)
            lax.fori_loop(CMODES, MODES, functools.partial(pass_xy, following=True, last=True), 0)
        elif k == 1:
            lax.fori_loop(0, CMODES, functools.partial(pass_xy, following=True), 0)
            lax.fori_loop(CMODES, MODES, functools.partial(pass_xy, coarse_only=True), 0)
        else:
            lax.fori_loop(0, CMODES, pass_xy, 0)

    def gather(g, _):
        for d in range(ny):
            @pl.when(gy != d)
            def _(d=d):
                fold_copy(d, g).wait_send()
                fold_arrival(d, g).wait_recv()
        lane = lanes((2 * CMODES**2, 128))
        owner = (lane % (4 * ny)) // 4
        spread_z = 128 // (4 * ny)
        blocks = [folded[d, g].reshape(2 * CMODES**2, 128) for d in range(ny)]
        total = []
        for j in range(4):
            at = (lane % 4 + gy) % ny * depth + j * spread_z + lane // (4 * ny)
            tile = jnp.take_along_axis(blocks[0], at, axis=1)
            for d in range(1, ny):
                tile = jnp.where(owner == d, jnp.take_along_axis(blocks[d], at, axis=1), tile)
            total.append(tile)
        for x in range(2):
            for a in range(CMODES):
                for j in range(4):
                    coarse[pl.ds((a * 16 + g) * 8 + j * 2 + x, CMODES, stride=32), :] = total[j][
                        x * 16 + a * 4:x * 16 + a * 4 + 4]
        return 0
    for d in range(4):
        @pl.when(exists[d])
        def _(d=d):
            param_copy(d).wait_send()
            make = (x_copy, y_copy)[d // 2]
            for k in range(3):
                def sent(i, _, make=make):
                    make(k, d % 2, i).wait_send()
                    return 0
                if d < 2 and k == 1:
                    lax.fori_loop(0, CMODES, sent, 0)
                    lax.fori_loop(CMODES, MODES, functools.partial(
                        sent, make=functools.partial(x_copy, width=CMODES)), 0)
                else:
                    lax.fori_loop(0, MODES if k < 2 else CMODES, sent, 0)
    lax.fori_loop(0, 2, gather, 0)
    for d in range(2):
        @pl.when(source[d])
        def _(d=d):
            late_copy(d).wait_recv()

    def pass_late(g, _):
        update(1, g, CMODES, MODES)
        return 0
    lax.fori_loop(CMODES, MODES, pass_late, 0)

    for d in range(2):
        @pl.when(exists[d])
        def _(d=d):
            late_copy(d).wait_send()
    lax.fori_loop(2, CMODES, gather, 0)


def smoother(nx, ny, rhs, coef, deg):
    field = pltpu.VMEM((MODES, MODES, MODES, 8, 128), F32)
    wide = pltpu.VMEM((2, 2, MODES, MODES, 8, 128), F32)
    narrow = pltpu.VMEM((2, CMODES, CMODES, 8, 128), F32)
    wide_half = pltpu.VMEM((2, 2, MODES, (MODES + 1) // 2, 8, 128), F32)
    narrow_half = pltpu.VMEM((2, CMODES, CMODES // 2, 8, 128), F32)
    return pl.pallas_call(
        functools.partial(kernel, nx, ny),
        out_shape=(jax.ShapeDtypeStruct((MODES, MODES, MODES, 8, 128), F32),
                   jax.ShapeDtypeStruct((CMODES**3 * 8, 128), F32)),
        in_specs=[pl.BlockSpec(memory_space=pltpu.HBM)] * 3,
        out_specs=[pl.BlockSpec(memory_space=pltpu.VMEM)] * 2,
        scratch_shapes=[
            field,
            pltpu.VMEM((8, 128), F32),
            pltpu.VMEM((3, 8, 128), jnp.int32),
            field, field, field,
            pltpu.VMEM((3, 6, 8, 128), F32),
            pltpu.VMEM((3, MODES, 8, 128), F32),
            pltpu.VMEM((MODES, 8, 128), F32),
            pltpu.VMEM((4, 8, 128), F32),
            pltpu.VMEM((4, 8, 128), F32),
            wide, wide, wide_half, wide_half, narrow, narrow, narrow_half, narrow_half,
            pltpu.VMEM((CMODES, 128, 128), F32),
            pltpu.VMEM((ny, CMODES, 2, CMODES**2, 128), F32),
            pltpu.VMEM((ny, CMODES, 2, CMODES**2, 128), F32),
            pltpu.SemaphoreType.DMA((3,)),
            pltpu.SemaphoreType.DMA((4,)),
            pltpu.SemaphoreType.DMA((4,)),
            pltpu.SemaphoreType.DMA((3, 2, MODES)),
            pltpu.SemaphoreType.DMA((3, 2, MODES)),
            pltpu.SemaphoreType.DMA((3, 2, MODES)),
            pltpu.SemaphoreType.DMA((3, 2, MODES)),
            pltpu.SemaphoreType.DMA((2,)),
            pltpu.SemaphoreType.DMA((2,)),
            pltpu.SemaphoreType.DMA((ny, CMODES)),
            pltpu.SemaphoreType.DMA((ny, CMODES)),
        ],
        compiler_params=pltpu.CompilerParams(
            collective_id=0, has_side_effects=True, vmem_limit_bytes=48 * 1024 * 1024
        ),
    )(*(pltpu.with_memory_space_constraint(v, pltpu.HBM) for v in (rhs, coef, deg)))


def finish_kernel(u, blocks, stored, coarse, sem):
    copies = [pltpu.make_async_copy(a, b, sem.at[i]) for i, (a, b) in enumerate(((u, stored), (blocks, coarse)))]
    for copy in copies:
        copy.start()
    for copy in copies:
        copy.wait()


def finish(u, blocks):
    return pl.pallas_call(
        finish_kernel,
        out_shape=(jax.ShapeDtypeStruct(u.shape, F32), jax.ShapeDtypeStruct(blocks.shape, F32)),
        in_specs=[pl.BlockSpec(memory_space=pl.ANY)] * 2,
        out_specs=[pl.BlockSpec(memory_space=pltpu.HBM)] * 2,
        scratch_shapes=[pltpu.SemaphoreType.DMA((2,))],
        compiler_params=pltpu.CompilerParams(vmem_limit_bytes=16 * 1024 * 1024),
    )(u, blocks)


def solution(mesh):
    nx, ny = mesh.shape["gx"], mesh.shape["gy"]

    def body(right_side, coefficient, degrees):
        local = right_side.shape[3:]
        flat = (local[0] * local[1], local[2])
        smoothed, blocks = smoother(
            nx, ny,
            right_side.reshape(right_side.shape[:3] + flat),
            coefficient.reshape(flat),
            degrees.reshape((3,) + flat),
        )
        smoothed, coarse = finish(smoothed, blocks)
        coarse = jnp.transpose(coarse.reshape(CMODES**3, 4, 2, 128), (0, 2, 1, 3))
        return smoothed.reshape(right_side.shape), coarse.reshape(CMODES**3, 2, 512)

    in_specs = (
        P(None, None, None, "gx", "gy", None),
        P("gx", "gy", None),
        P(None, "gx", "gy", None),
    )
    out_specs = (P(None, None, None, "gx", "gy", None), P(None, "gx", "gy"))
    return jax.shard_map(body, mesh=mesh, in_specs=in_specs, out_specs=out_specs, check_vma=False)
```

```python
import functools

import jax
import jax.numpy as jnp
from jax import lax
from jax.experimental import pallas as pl
from jax.experimental.pallas import tpu as pltpu
from jax.sharding import PartitionSpec as P

CMODES = 4
LAM_HIGH = 6.0
LAM_LOW = 0.5
MODES = 7
EARLY = 2
MESH = pl.DeviceIdType.MESH
F32 = jnp.float32
HALF = [(2.0 * n + 1.0) / 2.0 for n in range(MODES)]
SLOPE = [n * (n + 1.0) / 2.0 for n in range(MODES)]


def chebyshev():
    centre = (LAM_HIGH + LAM_LOW) / 2.0
    radius = (LAM_HIGH - LAM_LOW) / 2.0
    ratio = centre / radius
    rho = 1.0 / ratio
    pairs = []
    for _ in range(2):
        following = 1.0 / (2.0 * ratio - rho)
        pairs.append((following * rho, 2.0 * following / radius))
        rho = following
    return 1.0 / centre, pairs


def rows(shape):
    return lax.broadcasted_iota(jnp.int32, shape, len(shape) - 2)


def lanes(shape):
    return lax.broadcasted_iota(jnp.int32, shape, len(shape) - 1)


def turn(v, shift):
    return pltpu.roll(v, shift, v.ndim - 2)


def pack_x_up(p, q):
    return jnp.where(rows(p.shape) < 4, turn(p, 4), q)


def pack_x_down(p, q):
    return jnp.where(rows(p.shape) < 4, p, turn(q, 4))


def prev_x(p, q, g):
    low = rows(p.shape) < 4
    return jnp.where(low, g, turn(p, 4)), turn(jnp.where(low, q, g), 4)


def next_x(p, q, g):
    low = rows(p.shape) < 4
    return turn(jnp.where(low, g, p), 4), jnp.where(low, turn(q, 4), g)


def halves(p):
    half = (p.shape[0] + 1) // 2
    if p.shape[0] == 1:
        return p, p
    high = p[half:]
    if p.shape[0] % 2:
        high = jnp.concatenate([high, p[half - 1:half]], axis=0)
    return p[:half], high


def pack_y_up(p, q):
    (p, p_high), (q, q_high) = halves(p), halves(q)
    r = rows(p.shape) & 3
    return jnp.where(r < 2, jnp.where(r == 0, turn(p, 5), turn(q, 6)), jnp.where(r == 2, turn(p_high, 7), q_high))


def pack_y_down(p, q):
    (p, p_high), (q, q_high) = halves(p), halves(q)
    r = rows(p.shape) & 3
    return jnp.where(r < 2, jnp.where(r == 1, turn(p_high, 1), q_high), jnp.where(r == 3, turn(p, 3), turn(q, 2)))


def open_y(g, count, shifts):
    def both(low, high):
        first = turn(g, low) if low else g
        if count == 1:
            return first
        return jnp.concatenate([first, turn(g, high)[:count - g.shape[0]]], axis=0)
    return both(shifts[0], shifts[1]), both(shifts[2], shifts[3])


def prev_y(p, q, g):
    edge = (rows(p.shape) & 3) == 0
    g = open_y(g, p.shape[0], (0, 6, 7, 5))
    return jnp.where(edge, g[0], turn(p, 1)), jnp.where(edge, g[1], turn(q, 1))


def next_y(p, q, g):
    edge = (rows(p.shape) & 3) == 3
    g = open_y(g, p.shape[0], (0, 2, 1, 3))
    return jnp.where(edge, g[0], turn(p, 7)), jnp.where(edge, g[1], turn(q, 7))


def prev_z(p):
    return jnp.where(lanes(p.shape) == 0, 0.0, pltpu.roll(p, 1, p.ndim - 1))


def next_z(p):
    end = p.shape[-1] - 1
    return jnp.where(lanes(p.shape) == end, 0.0, pltpu.roll(p, end, p.ndim - 1))


def line(u, half_coef):
    t4 = u[4] + u[6]
    t2 = u[2] + t4
    even = u[0] + t2
    t3 = u[3] + u[5]
    odd = u[1] + t3
    s2 = 6.0 * t2
    s4 = s2 + 14.0 * t4
    s6 = s4 + 22.0 * u[6]
    s1 = 2.0 * odd
    s3 = s1 + 10.0 * t3
    s5 = s3 + 18.0 * u[5]
    tp = even + odd
    tm = even - odd
    fp = half_coef * (s6 + s5)
    fm = half_coef * (s5 - s6)
    return (tp, tm, fp, fm), (None, s1, s2, s3, s4, s5, s6)


def spread(traces, before, after, geom, coef, sums, count):
    tp, tm, fp, fm = traces
    tau_a, tau_b, w_a, w_b, k_a, k_b = geom
    jump_a = tp - after[0]
    g_a = tau_a * jump_a - w_a * (fp + after[1])
    jump_b = before[0] - tm
    g_b = tau_b * jump_b - w_b * (before[1] + fm)
    kl = k_a * jump_a
    kr = k_b * jump_b
    p = (g_a - g_b, g_a + g_b)
    q = (kl - kr, kl + kr)
    out = [HALF[0] * p[0]]
    for n in range(1, count):
        out.append(HALF[n] * (coef * sums[n] + (p[n % 2] - SLOPE[n] * q[n % 2])))
    return out


def kernel(nx, ny, rhs_hbm, coef_hbm, deg_hbm, u, coarse, s, coef, deg, inv, step, acc, geo, dia, ym,
           ps, pg, xs, xg, ys, yg, xs3, xg3, ys3, yg3, kept, folds, folded,
           in_sem, p_send, p_recv, x_send, x_recv, y_send, y_recv, l_send, l_recv, f_send, f_recv):
    gx, gy = lax.axis_index("gx"), lax.axis_index("gy")
    exists = (gx < nx - 1, gx > 0, gy < ny - 1, gy > 0)
    target = ({"gx": gx + 1}, {"gx": gx - 1}, {"gy": gy + 1}, {"gy": gy - 1})
    source = (exists[1], exists[0], exists[3], exists[2])

    barrier = pltpu.get_barrier_semaphore()
    near = ny <= 4
    for d in range(4 if near else 2):
        @pl.when(exists[d])
        def _(d=d):
            pl.semaphore_signal(barrier, inc=1, device_id=target[d], device_id_type=MESH)
    for d in range(0 if near else ny):
        @pl.when(gy != d)
        def _(d=d):
            pl.semaphore_signal(barrier, inc=1, device_id={"gy": d}, device_id_type=MESH)
    greeted = sum(e.astype(jnp.int32) for e in (exists if near else exists[:2])) + (0 if near else ny - 1)

    loads = [pltpu.make_async_copy(a, b, in_sem.at[i])
             for i, (a, b) in enumerate(((coef_hbm, coef), (deg_hbm, deg), (rhs_hbm, s)))]
    for load in loads:
        load.start()
    def copy(src, dst, send, recv, d):
        return pltpu.make_async_remote_copy(src_ref=src, dst_ref=dst, send_sem=send, recv_sem=recv,
                                            device_id=target[d], device_id_type=MESH)

    def param_copy(d):
        return copy(ps.at[d], pg.at[d], p_send.at[d], p_recv.at[d], d)

    def x_copy(k, d, b, width=MODES):
        if k < 2:
            part = pl.ds(0, width)
            return copy(xs.at[k, d, b, part], xg.at[k, d, b, part], x_send.at[k, d, b], x_recv.at[k, d, b], d)
        return copy(xs3.at[d, b], xg3.at[d, b], x_send.at[k, d, b], x_recv.at[k, d, b], d)

    def y_copy(k, d, a):
        if k < 2:
            return copy(ys.at[k, d, a], yg.at[k, d, a], y_send.at[k, d, a], y_recv.at[k, d, a], 2 + d)
        return copy(ys3.at[d, a], yg3.at[d, a], y_send.at[k, d, a], y_recv.at[k, d, a], 2 + d)

    def late_copy(d):
        part = (1, d, pl.ds(CMODES, MODES - CMODES), pl.ds(CMODES, MODES - CMODES))
        return copy(xs.at[part], xg.at[part], l_send.at[d], l_recv.at[d], d)

    loads[0].wait()
    loads[1].wait()
    c = coef[...]
    half_coef = 0.5 * c
    depth = 128 // ny
    df = [deg[d].astype(F32) for d in range(3)]
    ps[0] = pack_x_up(c, df[0])
    ps[1] = pack_x_down(c, df[0])
    ps[2] = pack_y_up(c[None], df[1][None])[0]
    ps[3] = pack_y_down(c[None], df[1][None])[0]
    pl.semaphore_wait(barrier, greeted)
    for d in range(4):
        @pl.when(exists[d])
        def _(d=d):
            param_copy(d).start()

    for d in range(4):
        @pl.when(jnp.logical_not(source[d]))
        def _(d=d):
            pg[d] = jnp.zeros((8, 128), F32)
            ghosts = (xg, yg)[d // 2]
            ghosts3 = (xg3, yg3)[d // 2]

            def clear(i, _):
                for k in range(2):
                    ghosts[k, d % 2, i] = jnp.zeros(ghosts.shape[3:], F32)
                return 0
            lax.fori_loop(0, MODES, clear, 0)

            def clear3(i, _):
                ghosts3[d % 2, i] = jnp.zeros(ghosts3.shape[2:], F32)
                return 0
            lax.fori_loop(0, CMODES, clear3, 0)

    shape = (MODES, 8, 128)
    levels = lax.broadcasted_iota(jnp.int32, shape, 0)
    ym[...] = jnp.where(levels <= deg[1][None], 1.0, 0.0)

    def prepare(direction, before, after, first, last):
        degree = df[direction]
        wide_a = jnp.maximum(degree, after[1])
        wide_b = jnp.maximum(degree, before[1])
        tau_a = jnp.maximum(c, after[0]) * (wide_a + 1.0) * (wide_a + 2.0)
        tau_b = jnp.maximum(c, before[0]) * (wide_b + 1.0) * (wide_b + 2.0)
        w_a = jnp.where(last, 1.0, 0.5)
        w_b = jnp.where(first, 1.0, 0.5)
        for i, value in enumerate((tau_a, tau_b, w_a, w_b, w_a * c, w_b * c)):
            geo[direction, i] = value
        rest = (1.0 - (w_a + w_b)) * c
        for n in range(MODES):
            dia[direction, n] = HALF[n] * (tau_a + tau_b + (2.0 * SLOPE[n]) * rest)

    row, lane = rows((8, 128)), lanes((8, 128))
    prepare(2, (prev_z(c), prev_z(df[2])), (next_z(c), next_z(df[2])), lane == 0, lane == 127)
    odd = gx % 2

    def params(d, want):
        @pl.when(want)
        def _():
            param_copy(d).wait_recv()

    params(2, source[2])
    params(3, source[3])
    params(0, source[0] & (odd == 1))
    params(1, source[1] & (odd == 0))
    px, py = gx * 2 + (row >> 2), gy * 4 + (row & 3)

    def prepare_x(low, high):
        prepare(0, prev_x(c, df[0], low), next_x(c, df[0], high), px == 0, px == 2 * nx - 1)

    before, after = prev_y(c[None], df[1][None], pg[2:3]), next_y(c[None], df[1][None], pg[3:4])
    prepare(1, [v[0] for v in before], [v[0] for v in after], py == 0, py == 4 * ny - 1)
    beside = pg[1 - odd]
    prepare_x(beside, beside)

    first_scale, pairs = chebyshev()
    odds = 2.0 * levels.astype(F32) + 1.0

    def geom(direction):
        return tuple(geo[direction, i][None] for i in range(6))

    def start(make, k, at, base):
        for d in range(2):
            @pl.when(exists[base + d])
            def _(d=d):
                make(k, d, at).start()

    def arrive(make, k, at, base):
        for d in range(2):
            @pl.when(source[base + d])
            def _(d=d):
                make(k, d, at).wait_recv()

    def send(k, g, values, width=MODES, begun=False):
        count = values[0].shape[0]
        (tp, tm, fp, fm), _ = line(values, half_coef[None])
        up, down = pack_x_up(tp, fp), pack_x_down(tm, fm)
        if begun:
            xs[k, 1 - odd, g] = jnp.where(odd == 0, down, up)
            start_side(k, g, 1 - odd)
        elif k < 2:
            xs[k, 0, g] = up
            xs[k, 1, g] = down
        else:
            xs3[0, g] = up
            xs3[1, g] = down
        if not begun:
            start(functools.partial(x_copy, width=width), k, g, 0)
        (tp, tm, fp, fm), _ = line([u[0:count, n, g] for n in range(MODES)], half_coef[None])
        up, down = pack_y_up(tp, fp), pack_y_down(tm, fm)
        if k < 2:
            ys[k, 0, g] = up
            ys[k, 1, g] = down
        else:
            ys3[0, g] = up
            ys3[1, g] = down
        start(y_copy, k, g, 2)

    def start_side(k, g, side):
        for d in range(2):
            @pl.when(exists[d] & (side == d))
            def _(d=d):
                x_copy(k, d, g).start()

    loads[2].wait()

    def first(g):
        inside = ym[...] * jnp.where(deg[2] >= g, 1.0, 0.0)[None]
        across = dia[1] + dia[2, g][None]
        scale = odds * ((2.0 * g.astype(F32) + 1.0) / 8.0)
        for a in range(MODES):
            i = jnp.where(deg[0] >= a, 1.0, 0.0)[None] * inside / (dia[0, a][None] + across)
            r = s[a, :, g] * (scale * (2.0 * a + 1.0))
            yield i, r, i * r * first_scale

    def begin(g, _):
        (tp, tm, fp, fm), _ = line([x for _, _, x in first(g)], half_coef[None])
        xs[0, odd, g] = jnp.where(odd == 0, pack_x_up(tp, fp), pack_x_down(tm, fm))
        start_side(0, g, odd)
        return 0
    lax.fori_loop(0, EARLY, begin, 0)

    params(0, source[0] & (odd == 0))
    params(1, source[1] & (odd == 1))
    prepare_x(pg[0], pg[1])

    def setup(g, _, begun=False):
        fresh = []
        for a, (i, r, x) in enumerate(first(g)):
            s[a, :, g] = r
            inv[a, :, g] = i
            u[a, :, g] = x
            fresh.append(x)
        send(0, g, fresh, begun=begun)
        return 0
    lax.fori_loop(0, EARLY, functools.partial(setup, begun=True), 0)
    lax.fori_loop(EARLY, MODES, setup, 0)

    def fold_copy(d, b):
        return pltpu.make_async_remote_copy(
            src_ref=folds.at[d, b], dst_ref=folded.at[gy, b], send_sem=f_send.at[d, b],
            recv_sem=f_recv.at[gy, b], device_id={"gy": d}, device_id_type=MESH)

    def fold_arrival(d, b):
        return pltpu.make_async_remote_copy(
            src_ref=folds.at[d, b], dst_ref=folded.at[d, b], send_sem=f_send.at[d, b],
            recv_sem=f_recv.at[d, b], device_id={"gy": d}, device_id_type=MESH)

    def fold(b):
        block = lanes((CMODES**2, 128)) // depth
        turned = []
        for x in range(2):
            by_y = [kept[b, pl.ds(x * 4 + y, CMODES**2, stride=8), :] for y in range(4)]
            turned.append([pltpu.roll(v, y * depth, 1) if y else v for y, v in enumerate(by_y)])

        def fill(ref, d):
            for x in range(2):
                out = turned[x][0]
                for y in range(1, 4):
                    out = jnp.where(block == (d + y) % ny, turned[x][y], out)
                ref[d, b, x] = out

        chip = gy // 2
        for step in range(1, ny // 2):
            for core in range(2):
                d = (chip + step) % (ny // 2) * 2 + core
                fill(folds, d)
                fold_copy(d, b).start()
        d = chip * 2 + 1 - gy % 2
        fill(folds, d)
        fold_copy(d, b).start()
        fill(folded, gy)

    def x_terms(values, g_prev, g_next, count):
        traces, sums = line(values, half_coef[None])
        tp, tm, fp, fm = traces
        return spread(traces, prev_x(tp, fp, g_prev), next_x(tm, fm, g_next), geom(0), c[None], sums, count)

    def update(k, g, low, high):
        values = [u[n, low:high, g] for n in range(MODES)]
        out = x_terms(values, xg[k, 0, g, low:high], xg[k, 1, g, low:high], MODES)
        fresh = []
        for n in range(MODES):
            residual = s[n, low:high, g] - (acc[n, low:high, g] + out[n])
            last = values[n] if k < 1 else step[n, low:high, g]
            change = pairs[k][0] * last + pairs[k][1] * (inv[n, low:high, g] * residual)
            moved = values[n] + change
            if k < 1:
                step[n, low:high, g] = change
            u[n, low:high, g] = moved
            fresh.append(moved)
        return fresh

    for k in range(3):
        count = MODES if k < 2 else CMODES

        def pass_z(a, _):
            traces, sums = line([u[a, 0:count, n] for n in range(MODES)], half_coef[None])
            tp, tm, fp, fm = traces
            out = spread(traces, (prev_z(tp), prev_z(fp)), (next_z(tm), next_z(fm)),
                         geom(2), c[None], sums, count)
            for n in range(count):
                acc[a, 0:count, n] = out[n]
            return 0
        lax.fori_loop(0, count, pass_z, 0)
        if k == 2:
            for d in range(2):
                @pl.when(exists[d])
                def _(d=d):
                    late_copy(d).start()

        def pass_xy(g, _, following=False, coarse_only=False, last=False):
            arrive(y_copy, k, g, 2)
            traces, sums = line([u[0:count, n, g] for n in range(MODES)], half_coef[None])
            tp, tm, fp, fm = traces
            g_prev = yg[k, 0, g] if k < 2 else yg3[0, g]
            g_next = yg[k, 1, g] if k < 2 else yg3[1, g]
            out = spread(traces, prev_y(tp, fp, g_prev), next_y(tm, fm, g_next),
                         geom(1), c[None], sums, count)
            for n in range(count):
                acc[0:count, n, g] += out[n]

            if k < 2:
                width = CMODES if coarse_only else MODES
                arrive(functools.partial(x_copy, width=width), k, g, 0)
                fresh = update(k, g, 0, width)
                if following:
                    keep = MODES if k < 1 else CMODES
                    send(k + 1, g, [v[0:keep] for v in fresh], CMODES if last else MODES)
            else:
                arrive(x_copy, k, g, 0)
                out = x_terms([u[n, 0:count, g] for n in range(MODES)], xg3[0, g], xg3[1, g], count)
                low = lax.broadcasted_iota(jnp.int32, (CMODES, 8, 128), 0)
                inside_y = jnp.where(low <= (deg[1] >> 1)[None], 1.0, 0.0)
                inside_z = jnp.where((deg[2] >> 1) >= g, 1.0, 0.0)
                mass = (1.0 / ((2.0 * low.astype(F32) + 1.0) * (2.0 * g.astype(F32) + 1.0))) * (
                    inside_y * inside_z[None])
                for n in range(CMODES):
                    inside = jnp.where((deg[0] >> 1) >= n, 8.0 / (2.0 * n + 1.0), 0.0)
                    residual = s[n, 0:CMODES, g] - (acc[n, 0:CMODES, g] + out[n])
                    kept[g, n * 32:(n + 1) * 32] = (residual * (mass * inside[None])).reshape(32, 128)
                fold(g)
            return 0
        if k == 0:
            lax.fori_loop(0, CMODES, functools.partial(pass_xy, following=True), 0)
            lax.fori_loop(CMODES, MODES, functools.partial(pass_xy, following=True, last=True), 0)
        elif k == 1:
            lax.fori_loop(0, CMODES, functools.partial(pass_xy, following=True), 0)
            lax.fori_loop(CMODES, MODES, functools.partial(pass_xy, coarse_only=True), 0)
        else:
            lax.fori_loop(0, CMODES, pass_xy, 0)

    def gather(g, _):
        for d in range(ny):
            @pl.when(gy != d)
            def _(d=d):
                fold_copy(d, g).wait_send()
                fold_arrival(d, g).wait_recv()
        lane = lanes((2 * CMODES**2, 128))
        owner = (lane % (4 * ny)) // 4
        spread_z = 128 // (4 * ny)
        blocks = [folded[d, g].reshape(2 * CMODES**2, 128) for d in range(ny)]
        total = []
        for j in range(4):
            at = (lane % 4 + gy) % ny * depth + j * spread_z + lane // (4 * ny)
            tile = jnp.take_along_axis(blocks[0], at, axis=1)
            for d in range(1, ny):
                tile = jnp.where(owner == d, jnp.take_along_axis(blocks[d], at, axis=1), tile)
            total.append(tile)
        for x in range(2):
            for a in range(CMODES):
                for j in range(4):
                    coarse[pl.ds((a * 16 + g) * 8 + j * 2 + x, CMODES, stride=32), :] = total[j][
                        x * 16 + a * 4:x * 16 + a * 4 + 4]
        return 0
    for d in range(4):
        @pl.when(exists[d])
        def _(d=d):
            param_copy(d).wait_send()
            make = (x_copy, y_copy)[d // 2]
            for k in range(3):
                def sent(i, _, make=make):
                    make(k, d % 2, i).wait_send()
                    return 0
                if d < 2 and k == 1:
                    lax.fori_loop(0, CMODES, sent, 0)
                    lax.fori_loop(CMODES, MODES, functools.partial(
                        sent, make=functools.partial(x_copy, width=CMODES)), 0)
                else:
                    lax.fori_loop(0, MODES if k < 2 else CMODES, sent, 0)
    lax.fori_loop(0, 2, gather, 0)
    for d in range(2):
        @pl.when(source[d])
        def _(d=d):
            late_copy(d).wait_recv()

    def pass_late(g, _):
        update(1, g, CMODES, MODES)
        return 0
    lax.fori_loop(CMODES, MODES, pass_late, 0)

    for d in range(2):
        @pl.when(exists[d])
        def _(d=d):
            late_copy(d).wait_send()
    lax.fori_loop(2, CMODES, gather, 0)


def smoother(nx, ny, rhs, coef, deg):
    field = pltpu.VMEM((MODES, MODES, MODES, 8, 128), F32)
    wide = pltpu.VMEM((2, 2, MODES, MODES, 8, 128), F32)
    narrow = pltpu.VMEM((2, CMODES, CMODES, 8, 128), F32)
    wide_half = pltpu.VMEM((2, 2, MODES, (MODES + 1) // 2, 8, 128), F32)
    narrow_half = pltpu.VMEM((2, CMODES, CMODES // 2, 8, 128), F32)
    return pl.pallas_call(
        functools.partial(kernel, nx, ny),
        out_shape=(jax.ShapeDtypeStruct((MODES, MODES, MODES, 8, 128), F32),
                   jax.ShapeDtypeStruct((CMODES**3 * 8, 128), F32)),
        in_specs=[pl.BlockSpec(memory_space=pltpu.HBM)] * 3,
        out_specs=[pl.BlockSpec(memory_space=pltpu.VMEM)] * 2,
        scratch_shapes=[
            field,
            pltpu.VMEM((8, 128), F32),
            pltpu.VMEM((3, 8, 128), jnp.int32),
            field, field, field,
            pltpu.VMEM((3, 6, 8, 128), F32),
            pltpu.VMEM((3, MODES, 8, 128), F32),
            pltpu.VMEM((MODES, 8, 128), F32),
            pltpu.VMEM((4, 8, 128), F32),
            pltpu.VMEM((4, 8, 128), F32),
            wide, wide, wide_half, wide_half, narrow, narrow, narrow_half, narrow_half,
            pltpu.VMEM((CMODES, 128, 128), F32),
            pltpu.VMEM((ny, CMODES, 2, CMODES**2, 128), F32),
            pltpu.VMEM((ny, CMODES, 2, CMODES**2, 128), F32),
            pltpu.SemaphoreType.DMA((3,)),
            pltpu.SemaphoreType.DMA((4,)),
            pltpu.SemaphoreType.DMA((4,)),
            pltpu.SemaphoreType.DMA((3, 2, MODES)),
            pltpu.SemaphoreType.DMA((3, 2, MODES)),
            pltpu.SemaphoreType.DMA((3, 2, MODES)),
            pltpu.SemaphoreType.DMA((3, 2, MODES)),
            pltpu.SemaphoreType.DMA((2,)),
            pltpu.SemaphoreType.DMA((2,)),
            pltpu.SemaphoreType.DMA((ny, CMODES)),
            pltpu.SemaphoreType.DMA((ny, CMODES)),
        ],
        compiler_params=pltpu.CompilerParams(
            collective_id=0, has_side_effects=True, vmem_limit_bytes=48 * 1024 * 1024
        ),
    )(*(pltpu.with_memory_space_constraint(v, pltpu.HBM) for v in (rhs, coef, deg)))


def finish_kernel(u, blocks, stored, coarse, sem):
    copies = [pltpu.make_async_copy(a, b, sem.at[i]) for i, (a, b) in enumerate(((u, stored), (blocks, coarse)))]
    for copy in copies:
        copy.start()
    for copy in copies:
        copy.wait()


def finish(u, blocks):
    return pl.pallas_call(
        finish_kernel,
        out_shape=(jax.ShapeDtypeStruct(u.shape, F32), jax.ShapeDtypeStruct(blocks.shape, F32)),
        in_specs=[pl.BlockSpec(memory_space=pl.ANY)] * 2,
        out_specs=[pl.BlockSpec(memory_space=pltpu.HBM)] * 2,
        scratch_shapes=[pltpu.SemaphoreType.DMA((2,))],
        compiler_params=pltpu.CompilerParams(vmem_limit_bytes=16 * 1024 * 1024),
    )(u, blocks)


def solution(mesh):
    nx, ny = mesh.shape["gx"], mesh.shape["gy"]

    def body(right_side, coefficient, degrees):
        local = right_side.shape[3:]
        flat = (local[0] * local[1], local[2])
        smoothed, blocks = smoother(
            nx, ny,
            right_side.reshape(right_side.shape[:3] + flat),
            coefficient.reshape(flat),
            degrees.reshape((3,) + flat),
        )
        smoothed, coarse = finish(smoothed, blocks)
        coarse = jnp.transpose(coarse.reshape(CMODES**3, 4, 2, 128), (0, 2, 1, 3))
        return smoothed.reshape(right_side.shape), coarse.reshape(CMODES**3, 2, 512)

    in_specs = (
        P(None, None, None, "gx", "gy", None),
        P("gx", "gy", None),
        P(None, "gx", "gy", None),
    )
    out_specs = (P(None, None, None, "gx", "gy", None), P(None, "gx", "gy"))
    return jax.shard_map(body, mesh=mesh, in_specs=in_specs, out_specs=out_specs, check_vma=False)
```

```python
import functools

import jax
import jax.numpy as jnp
from jax import lax
from jax.experimental import pallas as pl
from jax.experimental.pallas import tpu as pltpu
from jax.sharding import PartitionSpec as P

CMODES = 4
LAM_HIGH = 6.0
LAM_LOW = 0.5
MODES = 7
EARLY = 3
MESH = pl.DeviceIdType.MESH
F32 = jnp.float32
HALF = [(2.0 * n + 1.0) / 2.0 for n in range(MODES)]
SLOPE = [n * (n + 1.0) / 2.0 for n in range(MODES)]


def chebyshev():
    centre = (LAM_HIGH + LAM_LOW) / 2.0
    radius = (LAM_HIGH - LAM_LOW) / 2.0
    ratio = centre / radius
    rho = 1.0 / ratio
    pairs = []
    for _ in range(2):
        following = 1.0 / (2.0 * ratio - rho)
        pairs.append((following * rho, 2.0 * following / radius))
        rho = following
    return 1.0 / centre, pairs


def rows(shape):
    return lax.broadcasted_iota(jnp.int32, shape, len(shape) - 2)


def lanes(shape):
    return lax.broadcasted_iota(jnp.int32, shape, len(shape) - 1)


def turn(v, shift):
    return pltpu.roll(v, shift, v.ndim - 2)


def pack_x_up(p, q):
    return jnp.where(rows(p.shape) < 4, turn(p, 4), q)


def pack_x_down(p, q):
    return jnp.where(rows(p.shape) < 4, p, turn(q, 4))


def prev_x(p, q, g):
    low = rows(p.shape) < 4
    return jnp.where(low, g, turn(p, 4)), turn(jnp.where(low, q, g), 4)


def next_x(p, q, g):
    low = rows(p.shape) < 4
    return turn(jnp.where(low, g, p), 4), jnp.where(low, turn(q, 4), g)


def halves(p):
    half = (p.shape[0] + 1) // 2
    if p.shape[0] == 1:
        return p, p
    high = p[half:]
    if p.shape[0] % 2:
        high = jnp.concatenate([high, p[half - 1:half]], axis=0)
    return p[:half], high


def pack_y_up(p, q):
    (p, p_high), (q, q_high) = halves(p), halves(q)
    r = rows(p.shape) & 3
    return jnp.where(r < 2, jnp.where(r == 0, turn(p, 5), turn(q, 6)), jnp.where(r == 2, turn(p_high, 7), q_high))


def pack_y_down(p, q):
    (p, p_high), (q, q_high) = halves(p), halves(q)
    r = rows(p.shape) & 3
    return jnp.where(r < 2, jnp.where(r == 1, turn(p_high, 1), q_high), jnp.where(r == 3, turn(p, 3), turn(q, 2)))


def open_y(g, count, shifts):
    def both(low, high):
        first = turn(g, low) if low else g
        if count == 1:
            return first
        return jnp.concatenate([first, turn(g, high)[:count - g.shape[0]]], axis=0)
    return both(shifts[0], shifts[1]), both(shifts[2], shifts[3])


def prev_y(p, q, g):
    edge = (rows(p.shape) & 3) == 0
    g = open_y(g, p.shape[0], (0, 6, 7, 5))
    return jnp.where(edge, g[0], turn(p, 1)), jnp.where(edge, g[1], turn(q, 1))


def next_y(p, q, g):
    edge = (rows(p.shape) & 3) == 3
    g = open_y(g, p.shape[0], (0, 2, 1, 3))
    return jnp.where(edge, g[0], turn(p, 7)), jnp.where(edge, g[1], turn(q, 7))


def prev_z(p):
    return jnp.where(lanes(p.shape) == 0, 0.0, pltpu.roll(p, 1, p.ndim - 1))


def next_z(p):
    end = p.shape[-1] - 1
    return jnp.where(lanes(p.shape) == end, 0.0, pltpu.roll(p, end, p.ndim - 1))


def line(u, half_coef):
    t4 = u[4] + u[6]
    t2 = u[2] + t4
    even = u[0] + t2
    t3 = u[3] + u[5]
    odd = u[1] + t3
    s2 = 6.0 * t2
    s4 = s2 + 14.0 * t4
    s6 = s4 + 22.0 * u[6]
    s1 = 2.0 * odd
    s3 = s1 + 10.0 * t3
    s5 = s3 + 18.0 * u[5]
    tp = even + odd
    tm = even - odd
    fp = half_coef * (s6 + s5)
    fm = half_coef * (s5 - s6)
    return (tp, tm, fp, fm), (None, s1, s2, s3, s4, s5, s6)


def spread(traces, before, after, geom, coef, sums, count):
    tp, tm, fp, fm = traces
    tau_a, tau_b, w_a, w_b, k_a, k_b = geom
    jump_a = tp - after[0]
    g_a = tau_a * jump_a - w_a * (fp + after[1])
    jump_b = before[0] - tm
    g_b = tau_b * jump_b - w_b * (before[1] + fm)
    kl = k_a * jump_a
    kr = k_b * jump_b
    p = (g_a - g_b, g_a + g_b)
    q = (kl - kr, kl + kr)
    out = [HALF[0] * p[0]]
    for n in range(1, count):
        out.append(HALF[n] * (coef * sums[n] + (p[n % 2] - SLOPE[n] * q[n % 2])))
    return out


def kernel(nx, ny, rhs_hbm, coef_hbm, deg_hbm, u, coarse, s, coef, deg, inv, step, acc, geo, dia, ym,
           ps, pg, xs, xg, ys, yg, xs3, xg3, ys3, yg3, kept, folds, folded,
           in_sem, p_send, p_recv, x_send, x_recv, y_send, y_recv, l_send, l_recv, f_send, f_recv):
    gx, gy = lax.axis_index("gx"), lax.axis_index("gy")
    exists = (gx < nx - 1, gx > 0, gy < ny - 1, gy > 0)
    target = ({"gx": gx + 1}, {"gx": gx - 1}, {"gy": gy + 1}, {"gy": gy - 1})
    source = (exists[1], exists[0], exists[3], exists[2])

    barrier = pltpu.get_barrier_semaphore()
    near = ny <= 4
    for d in range(4 if near else 2):
        @pl.when(exists[d])
        def _(d=d):
            pl.semaphore_signal(barrier, inc=1, device_id=target[d], device_id_type=MESH)
    for d in range(0 if near else ny):
        @pl.when(gy != d)
        def _(d=d):
            pl.semaphore_signal(barrier, inc=1, device_id={"gy": d}, device_id_type=MESH)
    greeted = sum(e.astype(jnp.int32) for e in (exists if near else exists[:2])) + (0 if near else ny - 1)

    loads = [pltpu.make_async_copy(a, b, in_sem.at[i])
             for i, (a, b) in enumerate(((coef_hbm, coef), (deg_hbm, deg), (rhs_hbm, s)))]
    for load in loads:
        load.start()
    def copy(src, dst, send, recv, d):
        return pltpu.make_async_remote_copy(src_ref=src, dst_ref=dst, send_sem=send, recv_sem=recv,
                                            device_id=target[d], device_id_type=MESH)

    def param_copy(d):
        return copy(ps.at[d], pg.at[d], p_send.at[d], p_recv.at[d], d)

    def x_copy(k, d, b, width=MODES):
        if k < 2:
            part = pl.ds(0, width)
            return copy(xs.at[k, d, b, part], xg.at[k, d, b, part], x_send.at[k, d, b], x_recv.at[k, d, b], d)
        return copy(xs3.at[d, b], xg3.at[d, b], x_send.at[k, d, b], x_recv.at[k, d, b], d)

    def y_copy(k, d, a):
        if k < 2:
            return copy(ys.at[k, d, a], yg.at[k, d, a], y_send.at[k, d, a], y_recv.at[k, d, a], 2 + d)
        return copy(ys3.at[d, a], yg3.at[d, a], y_send.at[k, d, a], y_recv.at[k, d, a], 2 + d)

    def late_copy(d):
        part = (1, d, pl.ds(CMODES, MODES - CMODES), pl.ds(CMODES, MODES - CMODES))
        return copy(xs.at[part], xg.at[part], l_send.at[d], l_recv.at[d], d)

    loads[0].wait()
    loads[1].wait()
    c = coef[...]
    half_coef = 0.5 * c
    depth = 128 // ny
    df = [deg[d].astype(F32) for d in range(3)]
    ps[0] = pack_x_up(c, df[0])
    ps[1] = pack_x_down(c, df[0])
    ps[2] = pack_y_up(c[None], df[1][None])[0]
    ps[3] = pack_y_down(c[None], df[1][None])[0]
    pl.semaphore_wait(barrier, greeted)
    for d in range(4):
        @pl.when(exists[d])
        def _(d=d):
            param_copy(d).start()

    for d in range(4):
        @pl.when(jnp.logical_not(source[d]))
        def _(d=d):
            pg[d] = jnp.zeros((8, 128), F32)
            ghosts = (xg, yg)[d // 2]
            ghosts3 = (xg3, yg3)[d // 2]

            def clear(i, _):
                for k in range(2):
                    ghosts[k, d % 2, i] = jnp.zeros(ghosts.shape[3:], F32)
                return 0
            lax.fori_loop(0, MODES, clear, 0)

            def clear3(i, _):
                ghosts3[d % 2, i] = jnp.zeros(ghosts3.shape[2:], F32)
                return 0
            lax.fori_loop(0, CMODES, clear3, 0)

    shape = (MODES, 8, 128)
    levels = lax.broadcasted_iota(jnp.int32, shape, 0)
    ym[...] = jnp.where(levels <= deg[1][None], 1.0, 0.0)

    def prepare(direction, before, after, first, last):
        degree = df[direction]
        wide_a = jnp.maximum(degree, after[1])
        wide_b = jnp.maximum(degree, before[1])
        tau_a = jnp.maximum(c, after[0]) * (wide_a + 1.0) * (wide_a + 2.0)
        tau_b = jnp.maximum(c, before[0]) * (wide_b + 1.0) * (wide_b + 2.0)
        w_a = jnp.where(last, 1.0, 0.5)
        w_b = jnp.where(first, 1.0, 0.5)
        for i, value in enumerate((tau_a, tau_b, w_a, w_b, w_a * c, w_b * c)):
            geo[direction, i] = value
        rest = (1.0 - (w_a + w_b)) * c
        for n in range(MODES):
            dia[direction, n] = HALF[n] * (tau_a + tau_b + (2.0 * SLOPE[n]) * rest)

    row, lane = rows((8, 128)), lanes((8, 128))
    prepare(2, (prev_z(c), prev_z(df[2])), (next_z(c), next_z(df[2])), lane == 0, lane == 127)
    odd = gx % 2

    def params(d, want):
        @pl.when(want)
        def _():
            param_copy(d).wait_recv()

    params(2, source[2])
    params(3, source[3])
    params(0, source[0] & (odd == 1))
    params(1, source[1] & (odd == 0))
    px, py = gx * 2 + (row >> 2), gy * 4 + (row & 3)

    def prepare_x(low, high):
        prepare(0, prev_x(c, df[0], low), next_x(c, df[0], high), px == 0, px == 2 * nx - 1)

    before, after = prev_y(c[None], df[1][None], pg[2:3]), next_y(c[None], df[1][None], pg[3:4])
    prepare(1, [v[0] for v in before], [v[0] for v in after], py == 0, py == 4 * ny - 1)
    beside = pg[1 - odd]
    prepare_x(beside, beside)

    first_scale, pairs = chebyshev()
    odds = 2.0 * levels.astype(F32) + 1.0

    def geom(direction):
        return tuple(geo[direction, i][None] for i in range(6))

    def start(make, k, at, base):
        for d in range(2):
            @pl.when(exists[base + d])
            def _(d=d):
                make(k, d, at).start()

    def arrive(make, k, at, base):
        for d in range(2):
            @pl.when(source[base + d])
            def _(d=d):
                make(k, d, at).wait_recv()

    def send(k, g, values, width=MODES, begun=False):
        count = values[0].shape[0]
        (tp, tm, fp, fm), _ = line(values, half_coef[None])
        up, down = pack_x_up(tp, fp), pack_x_down(tm, fm)
        if begun:
            xs[k, 1 - odd, g] = jnp.where(odd == 0, down, up)
            start_side(k, g, 1 - odd)
        elif k < 2:
            xs[k, 0, g] = up
            xs[k, 1, g] = down
        else:
            xs3[0, g] = up
            xs3[1, g] = down
        if not begun:
            start(functools.partial(x_copy, width=width), k, g, 0)
        (tp, tm, fp, fm), _ = line([u[0:count, n, g] for n in range(MODES)], half_coef[None])
        up, down = pack_y_up(tp, fp), pack_y_down(tm, fm)
        if k < 2:
            ys[k, 0, g] = up
            ys[k, 1, g] = down
        else:
            ys3[0, g] = up
            ys3[1, g] = down
        start(y_copy, k, g, 2)

    def start_side(k, g, side):
        for d in range(2):
            @pl.when(exists[d] & (side == d))
            def _(d=d):
                x_copy(k, d, g).start()

    loads[2].wait()

    def first(g):
        inside = ym[...] * jnp.where(deg[2] >= g, 1.0, 0.0)[None]
        across = dia[1] + dia[2, g][None]
        scale = odds * ((2.0 * g.astype(F32) + 1.0) / 8.0)
        for a in range(MODES):
            i = jnp.where(deg[0] >= a, 1.0, 0.0)[None] * inside / (dia[0, a][None] + across)
            r = s[a, :, g] * (scale * (2.0 * a + 1.0))
            yield i, r, i * r * first_scale

    def begin(g, _):
        (tp, tm, fp, fm), _ = line([x for _, _, x in first(g)], half_coef[None])
        xs[0, odd, g] = jnp.where(odd == 0, pack_x_up(tp, fp), pack_x_down(tm, fm))
        start_side(0, g, odd)
        return 0
    lax.fori_loop(0, EARLY, begin, 0)

    params(0, source[0] & (odd == 0))
    params(1, source[1] & (odd == 1))
    prepare_x(pg[0], pg[1])

    def setup(g, _, begun=False):
        fresh = []
        for a, (i, r, x) in enumerate(first(g)):
            s[a, :, g] = r
            inv[a, :, g] = i
            u[a, :, g] = x
            fresh.append(x)
        send(0, g, fresh, begun=begun)
        return 0
    lax.fori_loop(0, EARLY, functools.partial(setup, begun=True), 0)
    lax.fori_loop(EARLY, MODES, setup, 0)

    def fold_copy(d, b):
        return pltpu.make_async_remote_copy(
            src_ref=folds.at[d, b], dst_ref=folded.at[gy, b], send_sem=f_send.at[d, b],
            recv_sem=f_recv.at[gy, b], device_id={"gy": d}, device_id_type=MESH)

    def fold_arrival(d, b):
        return pltpu.make_async_remote_copy(
            src_ref=folds.at[d, b], dst_ref=folded.at[d, b], send_sem=f_send.at[d, b],
            recv_sem=f_recv.at[d, b], device_id={"gy": d}, device_id_type=MESH)

    def fold(b):
        block = lanes((CMODES**2, 128)) // depth
        turned = []
        for x in range(2):
            by_y = [kept[b, pl.ds(x * 4 + y, CMODES**2, stride=8), :] for y in range(4)]
            turned.append([pltpu.roll(v, y * depth, 1) if y else v for y, v in enumerate(by_y)])

        def fill(ref, d):
            for x in range(2):
                out = turned[x][0]
                for y in range(1, 4):
                    out = jnp.where(block == (d + y) % ny, turned[x][y], out)
                ref[d, b, x] = out

        chip = gy // 2
        for step in range(1, ny // 2):
            for core in range(2):
                d = (chip + step) % (ny // 2) * 2 + core
                fill(folds, d)
                fold_copy(d, b).start()
        d = chip * 2 + 1 - gy % 2
        fill(folds, d)
        fold_copy(d, b).start()
        fill(folded, gy)

    def x_terms(values, g_prev, g_next, count):
        traces, sums = line(values, half_coef[None])
        tp, tm, fp, fm = traces
        return spread(traces, prev_x(tp, fp, g_prev), next_x(tm, fm, g_next), geom(0), c[None], sums, count)

    def update(k, g, low, high):
        values = [u[n, low:high, g] for n in range(MODES)]
        out = x_terms(values, xg[k, 0, g, low:high], xg[k, 1, g, low:high], MODES)
        fresh = []
        for n in range(MODES):
            residual = s[n, low:high, g] - (acc[n, low:high, g] + out[n])
            last = values[n] if k < 1 else step[n, low:high, g]
            change = pairs[k][0] * last + pairs[k][1] * (inv[n, low:high, g] * residual)
            moved = values[n] + change
            if k < 1:
                step[n, low:high, g] = change
            u[n, low:high, g] = moved
            fresh.append(moved)
        return fresh

    for k in range(3):
        count = MODES if k < 2 else CMODES

        def pass_z(a, _):
            traces, sums = line([u[a, 0:count, n] for n in range(MODES)], half_coef[None])
            tp, tm, fp, fm = traces
            out = spread(traces, (prev_z(tp), prev_z(fp)), (next_z(tm), next_z(fm)),
                         geom(2), c[None], sums, count)
            for n in range(count):
                acc[a, 0:count, n] = out[n]
            return 0
        lax.fori_loop(0, count, pass_z, 0)
        if k == 2:
            for d in range(2):
                @pl.when(exists[d])
                def _(d=d):
                    late_copy(d).start()

        def pass_xy(g, _, following=False, coarse_only=False, last=False):
            arrive(y_copy, k, g, 2)
            traces, sums = line([u[0:count, n, g] for n in range(MODES)], half_coef[None])
            tp, tm, fp, fm = traces
            g_prev = yg[k, 0, g] if k < 2 else yg3[0, g]
            g_next = yg[k, 1, g] if k < 2 else yg3[1, g]
            out = spread(traces, prev_y(tp, fp, g_prev), next_y(tm, fm, g_next),
                         geom(1), c[None], sums, count)
            for n in range(count):
                acc[0:count, n, g] += out[n]

            if k < 2:
                width = CMODES if coarse_only else MODES
                arrive(functools.partial(x_copy, width=width), k, g, 0)
                fresh = update(k, g, 0, width)
                if following:
                    keep = MODES if k < 1 else CMODES
                    send(k + 1, g, [v[0:keep] for v in fresh], CMODES if last else MODES)
            else:
                arrive(x_copy, k, g, 0)
                out = x_terms([u[n, 0:count, g] for n in range(MODES)], xg3[0, g], xg3[1, g], count)
                low = lax.broadcasted_iota(jnp.int32, (CMODES, 8, 128), 0)
                inside_y = jnp.where(low <= (deg[1] >> 1)[None], 1.0, 0.0)
                inside_z = jnp.where((deg[2] >> 1) >= g, 1.0, 0.0)
                mass = (1.0 / ((2.0 * low.astype(F32) + 1.0) * (2.0 * g.astype(F32) + 1.0))) * (
                    inside_y * inside_z[None])
                for n in range(CMODES):
                    inside = jnp.where((deg[0] >> 1) >= n, 8.0 / (2.0 * n + 1.0), 0.0)
                    residual = s[n, 0:CMODES, g] - (acc[n, 0:CMODES, g] + out[n])
                    kept[g, n * 32:(n + 1) * 32] = (residual * (mass * inside[None])).reshape(32, 128)
                fold(g)
            return 0
        if k == 0:
            lax.fori_loop(0, CMODES, functools.partial(pass_xy, following=True), 0)
            lax.fori_loop(CMODES, MODES, functools.partial(pass_xy, following=True, last=True), 0)
        elif k == 1:
            lax.fori_loop(0, CMODES, functools.partial(pass_xy, following=True), 0)
            lax.fori_loop(CMODES, MODES, functools.partial(pass_xy, coarse_only=True), 0)
        else:
            lax.fori_loop(0, CMODES, pass_xy, 0)

    def gather(g, _):
        for d in range(ny):
            @pl.when(gy != d)
            def _(d=d):
                fold_copy(d, g).wait_send()
                fold_arrival(d, g).wait_recv()
        lane = lanes((2 * CMODES**2, 128))
        owner = (lane % (4 * ny)) // 4
        spread_z = 128 // (4 * ny)
        blocks = [folded[d, g].reshape(2 * CMODES**2, 128) for d in range(ny)]
        total = []
        for j in range(4):
            at = (lane % 4 + gy) % ny * depth + j * spread_z + lane // (4 * ny)
            tile = jnp.take_along_axis(blocks[0], at, axis=1)
            for d in range(1, ny):
                tile = jnp.where(owner == d, jnp.take_along_axis(blocks[d], at, axis=1), tile)
            total.append(tile)
        for x in range(2):
            for a in range(CMODES):
                for j in range(4):
                    coarse[pl.ds((a * 16 + g) * 8 + j * 2 + x, CMODES, stride=32), :] = total[j][
                        x * 16 + a * 4:x * 16 + a * 4 + 4]
        return 0
    for d in range(4):
        @pl.when(exists[d])
        def _(d=d):
            param_copy(d).wait_send()
            make = (x_copy, y_copy)[d // 2]
            for k in range(3):
                def sent(i, _, make=make):
                    make(k, d % 2, i).wait_send()
                    return 0
                if d < 2 and k == 1:
                    lax.fori_loop(0, CMODES, sent, 0)
                    lax.fori_loop(CMODES, MODES, functools.partial(
                        sent, make=functools.partial(x_copy, width=CMODES)), 0)
                else:
                    lax.fori_loop(0, MODES if k < 2 else CMODES, sent, 0)
    lax.fori_loop(0, 2, gather, 0)
    for d in range(2):
        @pl.when(source[d])
        def _(d=d):
            late_copy(d).wait_recv()

    def pass_late(g, _):
        update(1, g, CMODES, MODES)
        return 0
    lax.fori_loop(CMODES, MODES, pass_late, 0)

    for d in range(2):
        @pl.when(exists[d])
        def _(d=d):
            late_copy(d).wait_send()
    lax.fori_loop(2, CMODES, gather, 0)


def smoother(nx, ny, rhs, coef, deg):
    field = pltpu.VMEM((MODES, MODES, MODES, 8, 128), F32)
    wide = pltpu.VMEM((2, 2, MODES, MODES, 8, 128), F32)
    narrow = pltpu.VMEM((2, CMODES, CMODES, 8, 128), F32)
    wide_half = pltpu.VMEM((2, 2, MODES, (MODES + 1) // 2, 8, 128), F32)
    narrow_half = pltpu.VMEM((2, CMODES, CMODES // 2, 8, 128), F32)
    return pl.pallas_call(
        functools.partial(kernel, nx, ny),
        out_shape=(jax.ShapeDtypeStruct((MODES, MODES, MODES, 8, 128), F32),
                   jax.ShapeDtypeStruct((CMODES**3 * 8, 128), F32)),
        in_specs=[pl.BlockSpec(memory_space=pltpu.HBM)] * 3,
        out_specs=[pl.BlockSpec(memory_space=pltpu.VMEM)] * 2,
        scratch_shapes=[
            field,
            pltpu.VMEM((8, 128), F32),
            pltpu.VMEM((3, 8, 128), jnp.int32),
            field, field, field,
            pltpu.VMEM((3, 6, 8, 128), F32),
            pltpu.VMEM((3, MODES, 8, 128), F32),
            pltpu.VMEM((MODES, 8, 128), F32),
            pltpu.VMEM((4, 8, 128), F32),
            pltpu.VMEM((4, 8, 128), F32),
            wide, wide, wide_half, wide_half, narrow, narrow, narrow_half, narrow_half,
            pltpu.VMEM((CMODES, 128, 128), F32),
            pltpu.VMEM((ny, CMODES, 2, CMODES**2, 128), F32),
            pltpu.VMEM((ny, CMODES, 2, CMODES**2, 128), F32),
            pltpu.SemaphoreType.DMA((3,)),
            pltpu.SemaphoreType.DMA((4,)),
            pltpu.SemaphoreType.DMA((4,)),
            pltpu.SemaphoreType.DMA((3, 2, MODES)),
            pltpu.SemaphoreType.DMA((3, 2, MODES)),
            pltpu.SemaphoreType.DMA((3, 2, MODES)),
            pltpu.SemaphoreType.DMA((3, 2, MODES)),
            pltpu.SemaphoreType.DMA((2,)),
            pltpu.SemaphoreType.DMA((2,)),
            pltpu.SemaphoreType.DMA((ny, CMODES)),
            pltpu.SemaphoreType.DMA((ny, CMODES)),
        ],
        compiler_params=pltpu.CompilerParams(
            collective_id=0, has_side_effects=True, vmem_limit_bytes=48 * 1024 * 1024
        ),
    )(*(pltpu.with_memory_space_constraint(v, pltpu.HBM) for v in (rhs, coef, deg)))


def finish_kernel(u, blocks, stored, coarse, sem):
    copies = [pltpu.make_async_copy(a, b, sem.at[i]) for i, (a, b) in enumerate(((u, stored), (blocks, coarse)))]
    for copy in copies:
        copy.start()
    for copy in copies:
        copy.wait()


def finish(u, blocks):
    return pl.pallas_call(
        finish_kernel,
        out_shape=(jax.ShapeDtypeStruct(u.shape, F32), jax.ShapeDtypeStruct(blocks.shape, F32)),
        in_specs=[pl.BlockSpec(memory_space=pl.ANY)] * 2,
        out_specs=[pl.BlockSpec(memory_space=pltpu.HBM)] * 2,
        scratch_shapes=[pltpu.SemaphoreType.DMA((2,))],
        compiler_params=pltpu.CompilerParams(vmem_limit_bytes=16 * 1024 * 1024),
    )(u, blocks)


def solution(mesh):
    nx, ny = mesh.shape["gx"], mesh.shape["gy"]

    def body(right_side, coefficient, degrees):
        local = right_side.shape[3:]
        flat = (local[0] * local[1], local[2])
        smoothed, blocks = smoother(
            nx, ny,
            right_side.reshape(right_side.shape[:3] + flat),
            coefficient.reshape(flat),
            degrees.reshape((3,) + flat),
        )
        smoothed, coarse = finish(smoothed, blocks)
        coarse = jnp.transpose(coarse.reshape(CMODES**3, 4, 2, 128), (0, 2, 1, 3))
        return smoothed.reshape(right_side.shape), coarse.reshape(CMODES**3, 2, 512)

    in_specs = (
        P(None, None, None, "gx", "gy", None),
        P("gx", "gy", None),
        P(None, "gx", "gy", None),
    )
    out_specs = (P(None, None, None, "gx", "gy", None), P(None, "gx", "gy"))
    return jax.shard_map(body, mesh=mesh, in_specs=in_specs, out_specs=out_specs, check_vma=False)
```
